32 devices in a mesh: groups: 1, seq: 32 (over z, y, x, core).
Axes of the slice: x: 2, y: 2, z: 4, core: 2. Of those that a mesh axis runs over, the one named last changes fastest.
Arguments:
- projected: bfloat16 [4096, 8192], P(('groups', 'seq')), may hold values from -6 to 6
- conv_weight: bfloat16 [4, 8192], replicated, may hold values from -3 to 3
- decay_log: float32 [32, 4096], P(None, ('groups', 'seq')), may hold values from -1 to 0, as said below
- write_strength: float32 [32, 4096], P(None, ('groups', 'seq')), may hold values from 0 to 1
- starts: int32 [4096], P(('groups', 'seq')), may hold values from 0 to 1, as said below
Outputs:
- mixer_out: bfloat16 [4096, 4096], P(('groups', 'seq'))
The draws below stay inside these ranges and needn't reach their ends.
Inputs may be any that keep to these rules, and one draw needn't show every extreme that they name: `starts`: 1 marks the first token of an episode; the first token of the stream is always 1. `decay_log`: never positive.
All inputs are finite; a program needn't handle non-finite values.
Results may differ from the reference program's by a relative error of at most 0.009.
Values may be sent and summed in bfloat16 or wider, within the bound.
No kernel may reach another device: no remote copies, remote signals or barrier semaphores. Data moves between devices by JAX's collectives and lax.ppermute only.
A program may use at most 1 GiB of HBM per device.

```python
import math
import jax
import jax.numpy as jnp
from jax import lax

HK = 16
DK = 128
HV = 32
DV = 128
KW = 4
SPAN = 64
TOK_DEV = 128
SEQUENCE_LENGTH = 4096
CH = 8192


def draw_decay_log(key, part):
    key_list = jax.random.split(key, 7)
    blocks = SEQUENCE_LENGTH // TOK_DEV
    slow_heads = jax.random.randint(key_list[0], (HV, 1, 1), 0, 10) < 5
    token_scale = jax.random.uniform(key_list[4], (HV, blocks, TOK_DEV), minval=0.5, maxval=1.5)
    slow_rate = jnp.exp(jax.random.uniform(key_list[1], (HV, 1, 1), minval=math.log(0.05 / SEQUENCE_LENGTH), maxval=math.log(0.5 / SEQUENCE_LENGTH)))
    fast_rate = jnp.exp(jax.random.uniform(key_list[2], (HV, 1, 1), minval=math.log(1.0 / (4 * TOK_DEV)), maxval=math.log(0.033)))
    head_rate = jnp.where(slow_heads, slow_rate, fast_rate)
    device_scale = jnp.exp(jax.random.uniform(key_list[3], (HV, blocks, 1), minval=math.log(0.5), maxval=math.log(2.0)))
    forgetting_speeds = (head_rate * device_scale * token_scale).reshape(HV, SEQUENCE_LENGTH)
    sampled_locations = jax.random.randint(key_list[5], (8,), 0, SEQUENCE_LENGTH)
    discard_markers = jnp.log(jax.random.uniform(key_list[6], (8,), minval=0.5, maxval=0.8))
    cluster_sets = jnp.zeros((SEQUENCE_LENGTH,), jnp.float32).at[sampled_locations].set(discard_markers)
    return (cluster_sets[None, :] - forgetting_speeds).astype(jnp.float32)


def draw_write_strength(key, part):
    head_key, token_key = jax.random.split(key)
    head_scale = jnp.exp(jax.random.uniform(head_key, (HV, 1), minval=math.log(0.01), maxval=0.0))
    token_scale = jax.random.uniform(token_key, (HV, SEQUENCE_LENGTH), minval=0.5, maxval=1.0)
    return (head_scale * token_scale).astype(jnp.float32)


def draw_starts(key, part):
    random_picker = jax.random.randint(key, (SEQUENCE_LENGTH,), 0, 6 * TOK_DEV)
    start_flags = (random_picker == 0).astype(jnp.int32)
    return start_flags.at[0].set(1)


def steps_of(own_key, shape, shards, smallest, largest):
    factor_of = 1.0
    for dim, shards_of in shards:
        heights = jax.random.uniform(jax.random.fold_in(jax.random.fold_in(own_key, 6), dim), (shards_of,), jnp.float32, smallest / len(shards), largest / len(shards))
        factor_of = factor_of * jnp.repeat(jnp.exp(heights), shape[dim] // shards_of).reshape((-1,) + (1,) * (len(shape) - 1 - dim))
    return factor_of


def bell_draw(own_key, dims, deviation, bound, cuts=(), kind=jnp.bfloat16):
    entries = deviation * jax.random.normal(own_key, dims, jnp.float32)
    if cuts:
        entries = entries * steps_of(own_key, dims, cuts, -0.22, 0.18)
    return jnp.clip(entries, -bound, bound).astype(kind)


def setup_inputs(seed: int = 0, part: int = 0) -> dict:
    key_of = jax.random.split(jax.random.key(seed), 6)
    part_keys = jax.random.split(jax.random.fold_in(key_of[5], part), 6)
    return {
        "projected": bell_draw(part_keys[0], (SEQUENCE_LENGTH, CH), 1.0, 6.0, ((0, 32),)),
        "conv_weight": bell_draw(key_of[1], (KW, CH), KW ** -0.5, 3.0),
        "decay_log": draw_decay_log(jax.random.fold_in(jax.random.fold_in(key_of[5], part), 71), part),
        "write_strength": draw_write_strength(jax.random.fold_in(jax.random.fold_in(key_of[5], part), 71), part),
        "starts": draw_starts(jax.random.fold_in(jax.random.fold_in(key_of[5], part), 71), part),
    }


norm_eps = 1e-06
highest_level = lax.Precision.HIGHEST

def convolve(window_rows, window_counts, conv_weight):
    length = window_rows.shape[0] - KW + 1
    summed = jnp.zeros((length, window_rows.shape[1]), jnp.float32)
    for shift_by in range(KW):
        first_row = KW - 1 - shift_by
        source = window_rows[first_row:first_row + length].astype(jnp.float32)
        usable = (window_counts[KW - 1:] == window_counts[first_row:first_row + length]).astype(jnp.float32)
        summed = summed + source * usable[:, None] * conv_weight[KW - 1 - shift_by].astype(jnp.float32)[None, :]
    return jax.nn.silu(summed).astype(jnp.bfloat16)

def split_heads(convolved):
    length = convolved.shape[0]
    blocks = length // SPAN
    as_float = convolved.astype(jnp.float32)
    queries = as_float[:, :HK * DK].reshape(length, HK, DK)
    keys_raw = as_float[:, HK * DK:2 * HK * DK].reshape(length, HK, DK)
    values = as_float[:, 2 * HK * DK:].reshape(length, HV, DV)
    queries = queries * lax.rsqrt(lax.optimization_barrier(jnp.sum(queries * queries, axis=-1, keepdims=True)) + norm_eps) * DK ** (-0.5)
    keys_raw = keys_raw * lax.rsqrt(lax.optimization_barrier(jnp.sum(keys_raw * keys_raw, axis=-1, keepdims=True)) + norm_eps)
    queries = jnp.repeat(queries, HV // HK, axis=1)
    keys_raw = jnp.repeat(keys_raw, HV // HK, axis=1)

    def arrange(tensor):
        return tensor.reshape(blocks, SPAN, HV, tensor.shape[-1]).transpose(2, 0, 1, 3)
    return (arrange(queries), arrange(keys_raw), arrange(values))

def block_terms(norm_queries, norm_keys, values, forget_factors, strengths, start_flags):
    cumulative = jnp.cumsum(forget_factors, axis=2)
    episode = jnp.cumsum(start_flags, axis=1)
    living = (episode == 0).astype(jnp.float32)
    position = lax.iota(jnp.int32, SPAN)
    lower_mask = position[:, None] >= position[None, :]
    strict = position[:, None] > position[None, :]
    same_episode = (episode[:, :, None] == episode[:, None, :]) & lower_mask[None]
    log_gap = cumulative[..., :, None] - cumulative[..., None, :]
    within = jnp.where(same_episode[None], jnp.exp(jnp.where(same_episode[None], log_gap, 0.0)), 0.0)
    carried = jnp.exp(cumulative) * living[None]
    ending = within[..., SPAN - 1, :]
    key_inner = jnp.einsum('hbik,hbjk->hbij', norm_keys, norm_keys, precision=highest_level)
    mixing = jnp.where(strict, strengths[..., :, None] * within * key_inner, 0.0)
    system = mixing + jnp.eye(SPAN, dtype=jnp.float32)
    right_side = jnp.concatenate([(strengths * carried)[..., None] * norm_keys, strengths[..., None] * values], axis=-1)
    solved = jax.scipy.linalg.solve_triangular(system, right_side, lower=True, unit_diagonal=True)
    erased = solved[..., :DK]
    fresh_values = solved[..., DK:]
    scores = jnp.einsum('hbik,hbjk->hbij', norm_queries, norm_keys, precision=highest_level) * within
    readout_values = carried[..., None] * norm_queries - jnp.einsum('hbij,hbjk->hbik', scores, erased, precision=highest_level)
    direct_path = jnp.einsum('hbij,hbjv->hbiv', scores, fresh_values, precision=highest_level)
    weighted = ending[..., None] * norm_keys
    transfer_state = carried[..., SPAN - 1][..., None, None] * jnp.eye(DK, dtype=jnp.float32) - jnp.einsum('hbjk,hbjl->hbkl', weighted, erased, precision=highest_level)
    offset_rows = jnp.einsum('hbjk,hbjv->hbkv', weighted, fresh_values, precision=highest_level)
    return (readout_values, direct_path, transfer_state, offset_rows)

def reference(projected, conv_weight, decay_log, write_strength, starts):
    total_tokens = projected.shape[0]
    blocks = total_tokens // SPAN
    counts = jnp.cumsum(starts).astype(jnp.int32)
    filled_entries = jnp.concatenate([jnp.zeros((KW - 1, projected.shape[1]), projected.dtype), projected], axis=0)
    padded_counts = jnp.concatenate([jnp.zeros((KW - 1,), jnp.int32), counts], axis=0)

    def advance(memory_state, block_index):
        start_row = (block_index * SPAN).astype(jnp.int32)
        window_rows = lax.dynamic_slice_in_dim(filled_entries, start_row, SPAN + KW - 1, 0)
        window_counts = lax.dynamic_slice_in_dim(padded_counts, start_row, SPAN + KW - 1, 0)
        convolved = convolve(window_rows, window_counts, conv_weight)
        norm_queries, norm_keys, values = split_heads(convolved)
        forget_factors = lax.dynamic_slice_in_dim(decay_log, start_row, SPAN, 1)[:, None, :]
        strengths = lax.dynamic_slice_in_dim(write_strength, start_row, SPAN, 1)[:, None, :]
        start_flags = lax.dynamic_slice_in_dim(starts, start_row, SPAN, 0)[None, :]
        readout_values, direct_path, transfer_state, offset_rows = block_terms(norm_queries, norm_keys, values, forget_factors, strengths, start_flags)
        output_rows = jnp.einsum('bje,bec->bjc', readout_values[:, 0], memory_state, precision=highest_level) + direct_path[:, 0]
        memory_state = jnp.einsum('trs,tsm->trm', transfer_state[:, 0], memory_state, precision=highest_level) + offset_rows[:, 0]
        return (memory_state, output_rows.transpose(1, 0, 2).reshape(SPAN, HV * DV).astype(jnp.bfloat16))
    _, outputs = lax.scan(advance, jnp.zeros((HV, DK, DV), jnp.float32), jnp.arange(blocks, dtype=jnp.int32))
    return outputs.reshape(total_tokens, HV * DV)
```

```python
import jax
import jax.numpy as jnp
from jax import lax
from jax.experimental import pallas as pl
from jax.experimental.pallas import tpu as pltpu
from jax.sharding import PartitionSpec as P

HK = 16
DK = 128
HV = 32
DV = 128
KW = 4
TOK = 128
NORM_EPS = 1e-06
GROUP = 4
ROWS = GROUP * DK + 16
F32 = jnp.float32
BF16 = jnp.bfloat16


def dot(a, b):
    return jnp.dot(a, b, preferred_element_type=F32)


def halves(a):
    high = a.astype(BF16)
    return high, (a - high.astype(F32)).astype(BF16)


def dot_split(a, b):
    ah, al = halves(a)
    bh, bl = halves(b)
    return dot(ah, bh) + (dot(ah, bl) + dot(al, bh))


def params(**kw):
    return pltpu.CompilerParams(vmem_limit_bytes=48 << 20, **kw)


def tables_kernel(decay_ref, beta_ref, starts_ref, out_ref):
    src = lax.broadcasted_iota(jnp.int32, (TOK, TOK), 0)
    dst = lax.broadcasted_iota(jnp.int32, (TOK, TOK), 1)
    upto = (src <= dst).astype(F32)
    cum = jnp.dot(
        decay_ref[...], upto, precision=lax.Precision.HIGHEST, preferred_element_type=F32
    )
    flags = jnp.broadcast_to(starts_ref[...].astype(F32), (8, TOK)).astype(BF16)
    episode = [dot(flags, (src + j <= dst).astype(BF16))[0:1] for j in range(KW)]
    usable = [(episode[0] == episode[j]).astype(F32) for j in range(1, KW)]
    living = (episode[0] == 0.0).astype(F32)
    zero = jnp.zeros((1, TOK), F32)
    shared = jnp.concatenate(usable + [episode[0], living, zero, zero, zero], axis=0)
    for pair in range(HV // GROUP):
        out_ref[pair, 0:4, :] = cum[GROUP * pair : GROUP * (pair + 1)]
        out_ref[pair, 4:8, :] = beta_ref[GROUP * pair : GROUP * (pair + 1), :]
        out_ref[pair, 8:16, :] = shared


def make_tables(decay_log, write_strength, starts):
    return pl.pallas_call(
        tables_kernel,
        out_shape=jax.ShapeDtypeStruct((HV // GROUP, 16, TOK), F32),
        compiler_params=params(),
        cost_estimate=pl.CostEstimate(flops=10**7, bytes_accessed=10**5, transcendentals=0),
        name="tables",
    )(decay_log, write_strength, starts.reshape(1, TOK))


def convolve(x_ref, halo_ref, w_ref, xs, first, usable):
    width = x_ref.shape[1]
    cols = slice(first, first + width)
    xs[8 : 8 + TOK, cols] = x_ref[...].astype(F32)
    xs[8 - KW + 1 : 8, cols] = halo_ref[...].astype(F32)
    taps = w_ref[...].astype(F32)
    pieces = []
    for c in range(0, width, 128):
        here = slice(first + c, first + c + 128)
        total = xs[8 : 8 + TOK, here] * taps[3:4, c : c + 128]
        for j in range(1, KW):
            total = total + (xs[8 - j : 8 - j + TOK, here] * usable[j - 1]) * taps[
                3 - j : 4 - j, c : c + 128
            ]
        pieces.append((total / (1.0 + jnp.exp(-total))).astype(BF16))
    return pieces


def column(cols, lane):
    return jnp.broadcast_to(cols[:, lane : lane + 1], (TOK, 128))


def decay_within(rows, cols, head, same):
    gap = column(cols, head) - rows[head : head + 1, :]
    return jnp.where(same, jnp.exp(jnp.where(same, gap, 0.0)), 0.0)


def positions():
    i = lax.broadcasted_iota(jnp.int32, (TOK, TOK), 0)
    j = lax.broadcasted_iota(jnp.int32, (TOK, TOK), 1)
    return i, j


def map_kernel(
    meta, xk_ref, xv_ref, hk_ref, hv_ref, wk_ref, wv_ref, rows_ref, pay_ref, kt_ref, ef_ref, xs
):
    rows = rows_ref[0]
    cols = jnp.transpose(rows)
    usable = [column(cols, 8 + j) for j in range(KW - 1)]
    living = column(cols, 12)
    i, j = positions()
    lower = i >= j
    same = (column(cols, 11) == rows[11:12, :]) & lower
    strict = i > j
    apart = i ^ j
    eye = (i == j).astype(F32)
    ks = convolve(xk_ref, hk_ref, wk_ref, xs, 0, usable)
    vs = convolve(xv_ref, hv_ref, wv_ref, xs, 256, usable)
    systems, endings, rights, keys_t = [], [], [], []
    carried_last = []
    for a in range(2):
        k = ks[a].astype(F32)
        k = k * lax.rsqrt(jnp.sum(k * k, axis=-1, keepdims=True) + NORM_EPS)
        kb = k.astype(BF16)
        kt = jnp.transpose(kb.astype(F32))
        ktb = kt.astype(BF16)
        keys_t.append(kt)
        kt_ref[0, a * DK : (a + 1) * DK, :] = ktb
        inner = dot(kb, ktb)
        for b in range(2):
            h = 2 * a + b
            within = decay_within(rows, cols, h, same)
            carried = jnp.exp(column(cols, h)) * living
            systems.append(jnp.where(strict, column(cols, 4 + h) * within * inner, 0.0))
            endings.append(within[TOK - 1 : TOK, :])
            rights.append(jnp.concatenate([(carried * k).astype(BF16), vs[h]], axis=1))
            carried_last.append(carried[TOK - 1 : TOK, :])
    inverse = [eye - jnp.where(apart == 1, s, 0.0) for s in systems]
    for level in range(1, 7):
        chosen = (apart >> level) == 1
        parts = [dot_split(jnp.where(chosen, systems[h], 0.0), inverse[h]) for h in range(GROUP)]
        inverse = [inverse[h] - dot_split(inverse[h], parts[h]) for h in range(GROUP)]
    pieces = []
    for h in range(GROUP):
        scaled = (inverse[h] * rows[4 + h : 5 + h, :]).astype(BF16)
        ef = dot(scaled, rights[h]).astype(BF16)
        ef_ref[0, h * TOK : (h + 1) * TOK, :] = ef
        weighted = (keys_t[h // 2] * endings[h]).astype(BF16)
        pay_ref[0, h * DK : (h + 1) * DK, :] = dot(weighted, ef).astype(BF16)
    rest = [jnp.concatenate([c, c], axis=1) for c in carried_last]
    for _ in range(3):
        highs = [c.astype(BF16).astype(F32) for c in rest]
        pieces += highs
        rest = [c - high for c, high in zip(rest, highs)]
    pieces.append(jnp.zeros((4, 256), F32))
    pay_ref[0, GROUP * DK : ROWS, :] = jnp.concatenate(pieces, axis=0).astype(BF16)


def make_maps(meta, slot, projected, halo, conv_weight, tables):
    def at(first):
        return lambda i, m: (0, first + m[slot] + i)

    return pl.pallas_call(
        map_kernel,
        grid_spec=pltpu.PrefetchScalarGridSpec(
            num_scalar_prefetch=1,
            grid=(4,),
            in_specs=[
                pl.BlockSpec((TOK, 256), at(8)),
                pl.BlockSpec((TOK, 512), at(8)),
                pl.BlockSpec((KW - 1, 256), at(8)),
                pl.BlockSpec((KW - 1, 512), at(8)),
                pl.BlockSpec((KW, 256), at(8)),
                pl.BlockSpec((KW, 512), at(8)),
                pl.BlockSpec((1, 16, TOK), lambda i, m: (m[slot] + i, 0, 0)),
            ],
            out_specs=[
                pl.BlockSpec((1, ROWS, 256), lambda i, m: (i, 0, 0)),
                pl.BlockSpec((1, 2 * DK, TOK), lambda i, m: (i, 0, 0)),
                pl.BlockSpec((1, GROUP * TOK, 256), lambda i, m: (i, 0, 0)),
            ],
            scratch_shapes=[pltpu.VMEM((8 + TOK, 768), F32)],
        ),
        out_shape=[
            jax.ShapeDtypeStruct((4, ROWS, 256), BF16),
            jax.ShapeDtypeStruct((4, 2 * DK, TOK), BF16),
            jax.ShapeDtypeStruct((4, GROUP * TOK, 256), BF16),
        ],
        compiler_params=params(),
        cost_estimate=pl.CostEstimate(
            flops=16 * 45 * 2 * 128**3, bytes_accessed=5 * 2**20, transcendentals=10**6
        ),
        name="maps",
    )(meta, projected, projected, halo, halo, conv_weight, conv_weight, tables)


def read_kernel(meta, xq_ref, hq_ref, wq_ref, rows_ref, kt_ref, ef_ref, r_ref, d_ref, xs):
    rows = rows_ref[0]
    cols = jnp.transpose(rows)
    usable = [column(cols, 8 + j) for j in range(KW - 1)]
    living = column(cols, 12)
    i, j = positions()
    same = (column(cols, 11) == rows[11:12, :]) & (i >= j)
    qs = convolve(xq_ref, hq_ref, wq_ref, xs, 0, usable)
    for a in range(2):
        q = qs[a].astype(F32)
        scale = lax.rsqrt(jnp.sum(q * q, axis=-1, keepdims=True) + NORM_EPS) * DK ** (-0.5)
        inner = dot(qs[a], kt_ref[0, a * DK : (a + 1) * DK, :])
        for b in range(2):
            h = 2 * a + b
            scores = (inner * decay_within(rows, cols, h, same)).astype(BF16)
            both = dot(scores, ef_ref[0, h * TOK : (h + 1) * TOK, :])
            carried = jnp.exp(column(cols, h)) * living
            mine = slice(h * TOK, (h + 1) * TOK)
            r_ref[0, mine, :] = ((carried * q - both[:, :DK]) * scale).astype(BF16)
            d_ref[0, mine, :] = both[:, DK:] * scale


def make_reads(meta, slot, projected, halo, conv_weight, tables, keys_t, ef):
    def at(i, m):
        return (0, m[slot] + i)

    return pl.pallas_call(
        read_kernel,
        grid_spec=pltpu.PrefetchScalarGridSpec(
            num_scalar_prefetch=1,
            grid=(4,),
            in_specs=[
                pl.BlockSpec((TOK, 256), at),
                pl.BlockSpec((KW - 1, 256), at),
                pl.BlockSpec((KW, 256), at),
                pl.BlockSpec((1, 16, TOK), lambda i, m: (m[slot] + i, 0, 0)),
                pl.BlockSpec((1, 2 * DK, TOK), lambda i, m: (i, 0, 0)),
                pl.BlockSpec((1, GROUP * TOK, 256), lambda i, m: (i, 0, 0)),
            ],
            out_specs=[
                pl.BlockSpec((1, GROUP * TOK, DK), lambda i, m: (i, 0, 0)),
                pl.BlockSpec((1, GROUP * TOK, DV), lambda i, m: (i, 0, 0)),
            ],
            scratch_shapes=[pltpu.VMEM((8 + TOK, 256), F32)],
        ),
        out_shape=[
            jax.ShapeDtypeStruct((4, GROUP * TOK, DK), BF16),
            jax.ShapeDtypeStruct((4, GROUP * TOK, DV), F32),
        ],
        compiler_params=params(),
        cost_estimate=pl.CostEstimate(
            flops=16 * 6 * 2 * 128**3, bytes_accessed=5 * 2**20, transcendentals=10**6
        ),
        name="reads",
    )(meta, projected, halo, conv_weight, tables, keys_t, ef)


def factor(tail, head):
    tail = tail.astype(F32)
    return (tail[head : head + 1] + tail[4 + head : 5 + head]) + tail[8 + head : 9 + head]


def pack_factors(factors):
    pieces, rest = [], list(factors)
    for _ in range(3):
        highs = [c.astype(BF16).astype(F32) for c in rest]
        pieces += highs
        rest = [c - high for c, high in zip(rest, highs)]
    pieces.append(jnp.zeros((4, 256), F32))
    return jnp.concatenate(pieces, axis=0).astype(BF16)


def compose(left, left_c, right, right_c):
    right_d = right[:, :DK]
    product = dot(right_d.astype(BF16), left.astype(BF16))
    return (
        right_c * left.astype(F32)
        + jnp.concatenate(
            [left_c[:, :DK] * right_d.astype(F32), right[:, DK:].astype(F32)], axis=1
        )
        - product
    )


def apply_map(each, c, state):
    product = dot(each[:, :DK], state)
    return c[:, :DK] * state.astype(F32) + each[:, DK:].astype(F32) - product


def pair_kernel(meta, mine_ref, other_ref, *out_refs):
    first = meta[2] == 0
    for m, out_ref in enumerate(out_refs):
        g = meta[3] ^ m
        tail_m, tail_o = mine_ref[g, GROUP * DK : ROWS, :], other_ref[g, GROUP * DK : ROWS, :]
        tail_l, tail_r = jnp.where(first, tail_m, tail_o), jnp.where(first, tail_o, tail_m)
        factors = []
        for h in range(GROUP):
            here = slice(h * DK, (h + 1) * DK)
            own, other = mine_ref[g, here, :], other_ref[g, here, :]
            left, right = jnp.where(first, own, other), jnp.where(first, other, own)
            left_c, right_c = factor(tail_l, h), factor(tail_r, h)
            out_ref[here, :] = compose(left, left_c, right, right_c).astype(BF16)
            factors.append(left_c * right_c)
        out_ref[GROUP * DK : ROWS, :] = pack_factors(factors)


def whole_spec():
    return pl.BlockSpec(memory_space=pltpu.VMEM)


def smem_spec():
    return pl.BlockSpec(memory_space=pltpu.SMEM)


def pair_maps(meta, mine, other):
    return pl.pallas_call(
        pair_kernel,
        in_specs=[smem_spec(), whole_spec(), whole_spec()],
        out_specs=[whole_spec()] * 4,
        out_shape=[jax.ShapeDtypeStruct((ROWS, 256), BF16)] * 4,
        compiler_params=params(),
        cost_estimate=pl.CostEstimate(
            flops=16 * 2 * 2 * 128**3, bytes_accessed=3 * 2**20, transcendentals=0
        ),
        name="pair",
    )(meta, mine, other)


def plane_kernel(meta, x0, x1, x2, x3, prefix_ref, plane_ref, exit_ref, maps, sems):
    copies = []
    for m, x in enumerate((x0, x1, x2, x3)):
        copy = pltpu.make_async_copy(x, maps.at[meta[3] ^ m], sems.at[m])
        copy.start()
        copies.append(copy)
    prefix_ref[0, 0 : GROUP * DK, :] = jnp.zeros((GROUP * DK, 256), BF16)
    ones = jnp.ones((1, 256), F32)
    prefix_ref[0, GROUP * DK : ROWS, :] = pack_factors([ones] * GROUP)
    for copy in copies:
        copy.wait()
    prefix_ref[1] = maps[0]
    run = [maps[0, h * DK : (h + 1) * DK, :].astype(F32) for h in range(GROUP)]
    run_c = [factor(maps[0, GROUP * DK : ROWS, :], h) for h in range(GROUP)]
    for a in range(1, 4):
        tail = maps[a, GROUP * DK : ROWS, :]
        for h in range(GROUP):
            here = slice(h * DK, (h + 1) * DK)
            c = factor(tail, h)
            run[h] = compose(run[h], run_c[h], maps[a, here, :], c)
            run_c[h] = run_c[h] * c
            if a < 3:
                prefix_ref[a + 1, here, :] = run[h].astype(BF16)
            else:
                plane_ref[here, :] = run[h].astype(BF16)
                exit_ref[here, :] = run[h][:, DK:].astype(BF16)
        if a < 3:
            prefix_ref[a + 1, GROUP * DK : ROWS, :] = pack_factors(run_c)
    plane_ref[GROUP * DK : ROWS, :] = pack_factors(run_c)


def plane_maps(meta, pieces):
    return pl.pallas_call(
        plane_kernel,
        in_specs=[smem_spec()] + [pl.BlockSpec(memory_space=pl.ANY)] * 4,
        out_specs=[whole_spec()] * 3,
        out_shape=[
            jax.ShapeDtypeStruct((4, ROWS, 256), BF16),
            jax.ShapeDtypeStruct((ROWS, 256), BF16),
            jax.ShapeDtypeStruct((GROUP * DK, DV), BF16),
        ],
        scratch_shapes=[pltpu.VMEM((4, ROWS, 256), BF16), pltpu.SemaphoreType.DMA((4,))],
        compiler_params=params(),
        cost_estimate=pl.CostEstimate(
            flops=12 * 2 * 2 * 128**3, bytes_accessed=2 * 2**20, transcendentals=0
        ),
        name="plane",
    )(meta, *pieces)


def hop_kernel(plane_ref, state_ref, out_ref):
    tail = plane_ref[GROUP * DK : ROWS, :]
    for h in range(GROUP):
        here = slice(h * DK, (h + 1) * DK)
        out_ref[here, :] = apply_map(plane_ref[here, :], factor(tail, h), state_ref[here, :]).astype(
            BF16
        )


def hop(plane_map, state):
    return pl.pallas_call(
        hop_kernel,
        in_specs=[whole_spec()] * 2,
        out_specs=whole_spec(),
        out_shape=jax.ShapeDtypeStruct((GROUP * DK, DV), BF16),
        compiler_params=params(),
        cost_estimate=pl.CostEstimate(
            flops=4 * 2 * 128**3, bytes_accessed=2**19, transcendentals=0
        ),
        name="hop",
    )(plane_map, state)


def spread_kernel(meta, prefix_ref, *refs):
    out_refs = refs[-4:]
    state_refs = refs[:-4]
    for h in range(GROUP):
        here = slice(h * DK, (h + 1) * DK)
        state = state_refs[0][here, :].astype(F32)
        for ref in state_refs[1:]:
            state = state + ref[here, :].astype(F32)
        state = state.astype(BF16)
        for m, out_ref in enumerate(out_refs):
            a = meta[3] ^ m
            c = factor(prefix_ref[a, GROUP * DK : ROWS, :], h)
            out_ref[here, :] = apply_map(prefix_ref[a, here, :], c, state).astype(BF16)


def spread(meta, prefix, states):
    return pl.pallas_call(
        spread_kernel,
        in_specs=[smem_spec()] + [whole_spec()] * (1 + len(states)),
        out_specs=[whole_spec()] * 4,
        out_shape=[jax.ShapeDtypeStruct((GROUP * DK, DV), BF16)] * 4,
        compiler_params=params(),
        cost_estimate=pl.CostEstimate(
            flops=16 * 2 * 128**3, bytes_accessed=2**21, transcendentals=0
        ),
        name="spread",
    )(meta, prefix, *states)


def core_kernel(meta, mine_ref, other_ref, e0, e1, e2, e3, keep_ref, send_ref, states, sems):
    copies = []
    for m, e in enumerate((e0, e1, e2, e3)):
        copy = pltpu.make_async_copy(e, states.at[meta[3] ^ m], sems.at[m])
        copy.start()
        copies.append(copy)
    for copy in copies:
        copy.wait()
    first = meta[2] == 0
    for g in range(4):
        tail = jnp.where(
            first, mine_ref[g, GROUP * DK : ROWS, :], other_ref[g, GROUP * DK : ROWS, :]
        )
        for h in range(GROUP):
            here = slice(h * DK, (h + 1) * DK)
            left = jnp.where(first, mine_ref[g, here, :], other_ref[g, here, :])
            state = states[g, here, :]
            after = apply_map(left, factor(tail, h), state).astype(BF16)
            keep_ref[g, here, :] = jnp.where(first, state, after)
            send_ref[g, here, :] = jnp.where(first, after, state)


def core_states(meta, mine, other, states):
    return pl.pallas_call(
        core_kernel,
        in_specs=[smem_spec(), whole_spec(), whole_spec()]
        + [pl.BlockSpec(memory_space=pl.ANY)] * 4,
        out_specs=[whole_spec()] * 2,
        out_shape=[jax.ShapeDtypeStruct((4, GROUP * DK, DV), BF16)] * 2,
        scratch_shapes=[pltpu.VMEM((4, GROUP * DK, DV), BF16), pltpu.SemaphoreType.DMA((4,))],
        compiler_params=params(),
        cost_estimate=pl.CostEstimate(
            flops=16 * 2 * 128**3, bytes_accessed=3 * 2**20, transcendentals=0
        ),
        name="core",
    )(meta, mine, other, *states)


def emit_kernel(meta, r_ref, d_ref, e_ref, *refs):
    out_ref = refs[-1]
    for h in range(GROUP):
        here = slice(h * TOK, (h + 1) * TOK)
        total = dot(r_ref[0, here, :], e_ref[0, here, :]) + d_ref[0, here, :]
        out_ref[:, h * DV : (h + 1) * DV] = total.astype(BF16)


def emit(meta, slot, reads, direct, states, into=None):
    in_specs = [
        pl.BlockSpec((1, GROUP * TOK, DK), lambda i, m: (i, 0, 0)),
        pl.BlockSpec((1, GROUP * TOK, DV), lambda i, m: (i, 0, 0)),
        pl.BlockSpec((1, GROUP * DK, DV), lambda i, m: (i, 0, 0)),
    ]
    args = [reads, direct, states]
    aliases = {}
    if into is not None:
        in_specs.append(pl.BlockSpec(memory_space=pl.ANY))
        args.append(into)
        aliases = {4: 0}
    return pl.pallas_call(
        emit_kernel,
        grid_spec=pltpu.PrefetchScalarGridSpec(
            num_scalar_prefetch=1,
            grid=(4,),
            in_specs=in_specs,
            out_specs=pl.BlockSpec((TOK, GROUP * DV), lambda i, m: (0, m[slot] + i)),
        ),
        out_shape=jax.ShapeDtypeStruct((TOK, HV * DV), BF16),
        input_output_aliases=aliases,
        compiler_params=params(),
        cost_estimate=pl.CostEstimate(
            flops=16 * 2 * 128**3, bytes_accessed=3 * 2**20, transcendentals=0
        ),
        name="emit",
    )(meta, *args)


def shards(projected, conv_weight, decay_log, write_strength, starts):
    length = projected.shape[0]
    count = lax.axis_size("seq")
    me = lax.axis_index("seq")
    core, place = me & 1, (me >> 1) & 3
    slots = lax.iota(jnp.int32, 4)
    meta = jnp.where(
        slots == 0,
        4 * (1 - core),
        jnp.where(slots == 1, 4 * core, jnp.where(slots == 2, core, place)),
    ).astype(jnp.int32)

    def exchange(block, bits):
        return lax.ppermute(block, "seq", [(i, i ^ bits) for i in range(count)])

    tail = starts[length - KW + 2 :]
    later = jnp.concatenate([lax.rev(jnp.cumsum(lax.rev(tail, (0,))), (0,)), jnp.zeros((1,), tail.dtype)])
    tail_rows = projected[length - KW + 1 :] * (later == 0).astype(BF16)[:, None]
    halo = lax.ppermute(tail_rows, "seq", [(i, i + 1) for i in range(count - 1)])
    tables = make_tables(decay_log, write_strength, starts)

    pay_s, kt_s, ef_s = make_maps(meta, 0, projected, halo, conv_weight, tables)
    other = exchange(pay_s, 1)
    mine, kt_k, ef_k = make_maps(meta, 1, projected, halo, conv_weight, tables)
    x0, x1, x2, x3 = pair_maps(meta, mine, other)
    x3, x1, x2 = exchange(x3, 6), exchange(x1, 2), exchange(x2, 4)
    r_s, d_s = make_reads(meta, 0, projected, halo, conv_weight, tables, kt_s, ef_s)
    r_k, d_k = make_reads(meta, 1, projected, halo, conv_weight, tables, kt_k, ef_k)
    prefix, plane_map, leaving = plane_maps(meta, (x0, x1, x2, x3))
    planes = count // 8
    received = []
    for step in range(planes - 1):
        route = [(i, i + 8) for i in range(8 * step, 8 * step + 8)]
        state = lax.ppermute(leaving, "seq", route)
        received.append(state)
        if step < planes - 2:
            leaving = hop(plane_map, state)
    if not received:
        received.append(jnp.zeros_like(leaving))
    e0, e1, e2, e3 = spread(meta, prefix, received)
    e3, e1, e2 = exchange(e3, 6), exchange(e1, 2), exchange(e2, 4)
    keep, send = core_states(meta, mine, other, (e0, e1, e2, e3))
    got = exchange(send, 1)
    out = emit(meta, 1, r_k, d_k, keep)
    return emit(meta, 0, r_s, d_s, got, into=out)


def solution(mesh):
    in_specs = (
        P(("groups", "seq"), None),
        P(),
        P(None, ("groups", "seq")),
        P(None, ("groups", "seq")),
        P(("groups", "seq")),
    )
    out_specs = P(("groups", "seq"), None)
    return jax.shard_map(shards, mesh=mesh, in_specs=in_specs, out_specs=out_specs, check_vma=False)
```

```python
import functools

import jax
import jax.numpy as jnp
from jax import lax
from jax.experimental import pallas as pl
from jax.experimental.pallas import tpu as pltpu
from jax.sharding import PartitionSpec as P

HK = 16
DK = 128
HV = 32
DV = 128
KW = 4
TOK = 128
NORM_EPS = 1e-06
GROUP = 4
ROWS = GROUP * DK + 16
F32 = jnp.float32
BF16 = jnp.bfloat16


def dot(a, b):
    return jnp.dot(a, b, preferred_element_type=F32)


def halves(a):
    high = a.astype(BF16)
    return high, (a - high.astype(F32)).astype(BF16)


def params(**kw):
    return pltpu.CompilerParams(vmem_limit_bytes=20 << 20, **kw)


def in_hbm(x):
    return pltpu.with_memory_space_constraint(x, pltpu.HBM)


def prologue_kernel(decay_ref, beta_ref, starts_ref, x_ref, out_ref, tail_ref):
    rows = x_ref.shape[0]
    flags = starts_ref[...].astype(F32)
    last = 1.0 - flags[:, TOK - 1 : TOK]
    keep = [last * (1.0 - flags[:, TOK - 2 : TOK - 1]), last, jnp.ones((1, 1), F32)]
    for r in range(KW - 1):
        row = x_ref[rows - KW + 1 + r : rows - KW + 2 + r, :].astype(F32)
        tail_ref[r : r + 1, :] = (row * keep[r]).astype(BF16)
    src = lax.broadcasted_iota(jnp.int32, (TOK, TOK), 0)
    dst = lax.broadcasted_iota(jnp.int32, (TOK, TOK), 1)
    upto = (src <= dst).astype(F32)
    cum = jnp.dot(
        decay_ref[...], upto, precision=lax.Precision.HIGHEST, preferred_element_type=F32
    )
    flags = jnp.broadcast_to(flags, (8, TOK)).astype(BF16)
    episode = [dot(flags, (src + j <= dst).astype(BF16))[0:1] for j in range(KW)]
    usable = [(episode[0] == episode[j]).astype(F32) for j in range(1, KW)]
    living = (episode[0] == 0.0).astype(F32)
    zero = jnp.zeros((1, TOK), F32)
    shared = jnp.concatenate(usable + [episode[0], living, zero, zero, zero], axis=0)
    for pair in range(HV // GROUP):
        out_ref[pair, 0:4, :] = cum[GROUP * pair : GROUP * (pair + 1)]
        out_ref[pair, 4:8, :] = beta_ref[GROUP * pair : GROUP * (pair + 1), :]
        out_ref[pair, 8:16, :] = shared


def prologue(decay_log, write_strength, starts, projected):
    channels = projected.shape[1]
    last = projected.shape[0] // 16 - 1
    return pl.pallas_call(
        prologue_kernel,
        grid=(1,),
        in_specs=[
            pl.BlockSpec((HV, TOK), lambda i: (0, 0)),
            pl.BlockSpec((HV, TOK), lambda i: (0, 0)),
            pl.BlockSpec((1, TOK), lambda i: (0, 0)),
            pl.BlockSpec((16, channels), lambda i: (last, 0)),
        ],
        out_specs=[
            pl.BlockSpec((HV // GROUP, 16, TOK), lambda i: (0, 0, 0)),
            pl.BlockSpec((KW - 1, channels), lambda i: (0, 0)),
        ],
        out_shape=[
            jax.ShapeDtypeStruct((HV // GROUP, 16, TOK), F32),
            jax.ShapeDtypeStruct((KW - 1, channels), BF16),
        ],
        compiler_params=params(),
        cost_estimate=pl.CostEstimate(flops=10**7, bytes_accessed=10**6, transcendentals=0),
        name="prologue",
    )(in_hbm(decay_log), in_hbm(write_strength), in_hbm(starts.reshape(1, TOK)), in_hbm(projected))


def convolve(x_ref, halo_ref, w_ref, xs, first, usable):
    width = x_ref.shape[1]
    cols = slice(first, first + width)
    xs[8 : 8 + TOK, cols] = x_ref[...].astype(F32)
    xs[8 - KW + 1 : 8, cols] = halo_ref[...].astype(F32)
    taps = w_ref[...].astype(F32)
    pieces = []
    for c in range(0, width, 128):
        here = slice(first + c, first + c + 128)
        total = xs[8 : 8 + TOK, here] * taps[3:4, c : c + 128]
        for j in range(1, KW):
            total = total + (xs[8 - j : 8 - j + TOK, here] * usable[j - 1]) * taps[
                3 - j : 4 - j, c : c + 128
            ]
        pieces.append((total / (1.0 + jnp.exp(-total))).astype(BF16))
    return pieces


def column(cols, lane):
    return jnp.broadcast_to(cols[:, lane : lane + 1], (TOK, 128))


def decay_within(rows, cols, head, same):
    gap = column(cols, head) - rows[head : head + 1, :]
    return jnp.where(same, jnp.exp(jnp.where(same, gap, 0.0)), 0.0)


def positions():
    i = lax.broadcasted_iota(jnp.int32, (TOK, TOK), 0)
    j = lax.broadcasted_iota(jnp.int32, (TOK, TOK), 1)
    return i, j


def map_kernel(
    meta, xk_ref, xv_ref, hk_ref, hv_ref, wk_ref, wv_ref, rows_ref, pay_ref, kt_ref, ef_ref, xs
):
    rows = rows_ref[0]
    cols = jnp.transpose(rows)
    usable = [column(cols, 8 + j) for j in range(KW - 1)]
    living = column(cols, 12)
    i, j = positions()
    lower = i >= j
    same = (column(cols, 11) == rows[11:12, :]) & lower
    strict = i > j
    apart = i ^ j
    eye = (i == j).astype(F32)
    ks = convolve(xk_ref, hk_ref, wk_ref, xs, 0, usable)
    vs = convolve(xv_ref, hv_ref, wv_ref, xs, 256, usable)
    systems, endings, rights, keys_t = [], [], [], []
    carried_last = []
    for a in range(2):
        k = ks[a].astype(F32)
        k = k * lax.rsqrt(jnp.sum(k * k, axis=-1, keepdims=True) + NORM_EPS)
        kb = k.astype(BF16)
        kt = jnp.transpose(kb.astype(F32))
        ktb = kt.astype(BF16)
        keys_t.append(kt)
        kt_ref[0, a * DK : (a + 1) * DK, :] = ktb
        inner = dot(kb, ktb)
        for b in range(2):
            h = 2 * a + b
            within = decay_within(rows, cols, h, same)
            carried = jnp.exp(column(cols, h)) * living
            systems.append(jnp.where(strict, column(cols, 4 + h) * within * inner, 0.0))
            endings.append(within[TOK - 1 : TOK, :])
            rights.append(jnp.concatenate([(carried * k).astype(BF16), vs[h]], axis=1))
            carried_last.append(carried[TOK - 1 : TOK, :])
    parts = [halves(system) for system in systems]
    inverse = [(eye - jnp.where(apart == 1, s, 0.0)).astype(BF16) for s in systems]
    for level in range(1, 7):
        chosen = (apart >> level) == 1
        steps = [dot(parts[h][0], inverse[h]).astype(BF16) for h in range(GROUP)]
        steps = [dot(inverse[h], steps[h]) for h in range(GROUP)]
        inverse = [
            inverse[h] - jnp.where(chosen, steps[h], 0.0).astype(BF16) for h in range(GROUP)
        ]
    exact = []
    for h in range(GROUP):
        both = jnp.concatenate(parts[h], axis=1)
        product = dot(both, jnp.concatenate([inverse[h], inverse[h]], axis=0))
        gap = (eye - inverse[h].astype(F32)) - product
        exact.append(inverse[h].astype(F32) + dot(inverse[h], gap.astype(BF16)))
    pieces = []
    for h in range(GROUP):
        scaled = (exact[h] * rows[4 + h : 5 + h, :]).astype(BF16)
        ef = dot(scaled, rights[h]).astype(BF16)
        ef_ref[0, h * TOK : (h + 1) * TOK, :] = ef
        weighted = (keys_t[h // 2] * endings[h]).astype(BF16)
        pay_ref[0, h * DK : (h + 1) * DK, :] = dot(weighted, ef).astype(BF16)
    rest = [jnp.concatenate([c, c], axis=1) for c in carried_last]
    for _ in range(3):
        highs = [c.astype(BF16).astype(F32) for c in rest]
        pieces += highs
        rest = [c - high for c, high in zip(rest, highs)]
    pieces.append(jnp.zeros((4, 256), F32))
    pay_ref[0, GROUP * DK : ROWS, :] = jnp.concatenate(pieces, axis=0).astype(BF16)


def make_maps(meta, slot, projected, halo, conv_weight, tables):
    def at(first):
        return lambda i, m: (0, first + m[slot] + i)

    return pl.pallas_call(
        map_kernel,
        grid_spec=pltpu.PrefetchScalarGridSpec(
            num_scalar_prefetch=1,
            grid=(4,),
            in_specs=[
                pl.BlockSpec((TOK, 256), at(8)),
                pl.BlockSpec((TOK, 512), at(8)),
                pl.BlockSpec((KW - 1, 256), at(8)),
                pl.BlockSpec((KW - 1, 512), at(8)),
                pl.BlockSpec((KW, 256), at(8)),
                pl.BlockSpec((KW, 512), at(8)),
                pl.BlockSpec((1, 16, TOK), lambda i, m: (m[slot] + i, 0, 0)),
            ],
            out_specs=[
                pl.BlockSpec((1, ROWS, 256), lambda i, m: (i, 0, 0)),
                pl.BlockSpec((1, 2 * DK, TOK), lambda i, m: (i, 0, 0)),
                pl.BlockSpec((1, GROUP * TOK, 256), lambda i, m: (i, 0, 0)),
            ],
            scratch_shapes=[pltpu.VMEM((8 + TOK, 768), F32)],
        ),
        out_shape=[
            jax.ShapeDtypeStruct((4, ROWS, 256), BF16),
            jax.ShapeDtypeStruct((4, 2 * DK, TOK), BF16),
            jax.ShapeDtypeStruct((4, GROUP * TOK, 256), BF16),
        ],
        compiler_params=params(),
        cost_estimate=pl.CostEstimate(
            flops=16 * 45 * 2 * 128**3, bytes_accessed=5 * 2**20, transcendentals=10**6
        ),
        name="maps",
    )(meta, in_hbm(projected), in_hbm(projected), halo, halo, in_hbm(conv_weight), in_hbm(conv_weight), tables)


def read_kernel(meta, xq_ref, hq_ref, wq_ref, rows_ref, kt_ref, ef_ref, left_ref, r_ref, d_ref, xs):
    first = meta[2] == 0
    tail = left_ref[0, GROUP * DK : ROWS, :]
    rows = rows_ref[0]
    cols = jnp.transpose(rows)
    usable = [column(cols, 8 + j) for j in range(KW - 1)]
    living = column(cols, 12)
    i, j = positions()
    same = (column(cols, 11) == rows[11:12, :]) & (i >= j)
    qs = convolve(xq_ref, hq_ref, wq_ref, xs, 0, usable)
    for a in range(2):
        q = qs[a].astype(F32)
        scale = lax.rsqrt(jnp.sum(q * q, axis=-1, keepdims=True) + NORM_EPS) * DK ** (-0.5)
        inner = dot(qs[a], kt_ref[0, a * DK : (a + 1) * DK, :])
        for b in range(2):
            h = 2 * a + b
            scores = (inner * decay_within(rows, cols, h, same)).astype(BF16)
            both = dot(scores, ef_ref[0, h * TOK : (h + 1) * TOK, :])
            carried = jnp.exp(column(cols, h)) * living
            mine = slice(h * TOK, (h + 1) * TOK)
            reader = (carried * q - both[:, :DK]) * scale
            direct = both[:, DK:] * scale
            moved = dot(reader.astype(BF16), left_ref[0, h * DK : (h + 1) * DK, :])
            c = factor(tail, h)[:, :DK]
            r_ref[0, mine, :] = jnp.where(first, reader, c * reader - moved[:, :DK]).astype(BF16)
            d_ref[0, mine, :] = jnp.where(first, direct, direct + moved[:, DK:])


def make_reads(meta, slot, projected, halo, conv_weight, tables, keys_t, ef, left):
    def at(i, m):
        return (0, m[slot] + i)

    return pl.pallas_call(
        read_kernel,
        grid_spec=pltpu.PrefetchScalarGridSpec(
            num_scalar_prefetch=1,
            grid=(4,),
            in_specs=[
                pl.BlockSpec((TOK, 256), at),
                pl.BlockSpec((KW - 1, 256), at),
                pl.BlockSpec((KW, 256), at),
                pl.BlockSpec((1, 16, TOK), lambda i, m: (m[slot] + i, 0, 0)),
                pl.BlockSpec((1, 2 * DK, TOK), lambda i, m: (i, 0, 0)),
                pl.BlockSpec((1, GROUP * TOK, 256), lambda i, m: (i, 0, 0)),
                pl.BlockSpec((1, ROWS, 256), lambda i, m: (i, 0, 0)),
            ],
            out_specs=[
                pl.BlockSpec((1, GROUP * TOK, DK), lambda i, m: (i, 0, 0)),
                pl.BlockSpec((1, GROUP * TOK, DV), lambda i, m: (i, 0, 0)),
            ],
            scratch_shapes=[pltpu.VMEM((8 + TOK, 256), F32)],
        ),
        out_shape=[
            jax.ShapeDtypeStruct((4, GROUP * TOK, DK), BF16),
            jax.ShapeDtypeStruct((4, GROUP * TOK, DV), F32),
        ],
        compiler_params=params(),
        cost_estimate=pl.CostEstimate(
            flops=16 * 6 * 2 * 128**3, bytes_accessed=5 * 2**20, transcendentals=10**6
        ),
        name="reads",
    )(meta, in_hbm(projected), halo, in_hbm(conv_weight), tables, keys_t, ef, left)


def factor(tail, head):
    tail = tail.astype(F32)
    return (tail[head : head + 1] + tail[4 + head : 5 + head]) + tail[8 + head : 9 + head]


def pack_factors(factors):
    pieces, rest = [], list(factors)
    for _ in range(3):
        highs = [c.astype(BF16).astype(F32) for c in rest]
        pieces += highs
        rest = [c - high for c, high in zip(rest, highs)]
    pieces.append(jnp.zeros((4, 256), F32))
    return jnp.concatenate(pieces, axis=0).astype(BF16)


def compose(left, left_c, right, right_c):
    right_d = right[:, :DK]
    product = dot(right_d.astype(BF16), left.astype(BF16))
    return (
        right_c * left.astype(F32)
        + jnp.concatenate(
            [left_c[:, :DK] * right_d.astype(F32), right[:, DK:].astype(F32)], axis=1
        )
        - product
    )


def apply_map(each, c, state):
    product = dot(each[:, :DK], state)
    return c[:, :DK] * state.astype(F32) + each[:, DK:].astype(F32) - product


def pair_kernel(meta, mine_ref, other_ref, *out_refs):
    first = meta[2] == 0
    for m, out_ref in enumerate(out_refs):
        g = meta[3] ^ m
        tail_m, tail_o = mine_ref[g, GROUP * DK : ROWS, :], other_ref[g, GROUP * DK : ROWS, :]
        tail_l, tail_r = jnp.where(first, tail_m, tail_o), jnp.where(first, tail_o, tail_m)
        factors = []
        for h in range(GROUP):
            here = slice(h * DK, (h + 1) * DK)
            own, other = mine_ref[g, here, :], other_ref[g, here, :]
            left, right = jnp.where(first, own, other), jnp.where(first, other, own)
            left_c, right_c = factor(tail_l, h), factor(tail_r, h)
            out_ref[here, :] = compose(left, left_c, right, right_c).astype(BF16)
            factors.append(left_c * right_c)
        out_ref[GROUP * DK : ROWS, :] = pack_factors(factors)


def whole_spec():
    return pl.BlockSpec(memory_space=pltpu.VMEM)


def smem_spec():
    return pl.BlockSpec(memory_space=pltpu.SMEM)


def pair_maps(meta, mine, other):
    return pl.pallas_call(
        pair_kernel,
        in_specs=[smem_spec(), whole_spec(), whole_spec()],
        out_specs=[whole_spec()] * 4,
        out_shape=[jax.ShapeDtypeStruct((ROWS, 256), BF16)] * 4,
        compiler_params=params(),
        cost_estimate=pl.CostEstimate(
            flops=16 * 2 * 2 * 128**3, bytes_accessed=3 * 2**20, transcendentals=0
        ),
        name="pair",
    )(meta, mine, other)


def plane_kernel(meta, x0, x1, x2, x3, prefix_ref, plane_ref, exit_ref, maps, sems):
    copies = []
    for m, x in enumerate((x0, x1, x2, x3)):
        copy = pltpu.make_async_copy(x, maps.at[meta[3] ^ m], sems.at[m])
        copy.start()
        copies.append(copy)
    prefix_ref[0, 0 : GROUP * DK, :] = jnp.zeros((GROUP * DK, 256), BF16)
    ones = jnp.ones((1, 256), F32)
    prefix_ref[0, GROUP * DK : ROWS, :] = pack_factors([ones] * GROUP)
    for copy in copies:
        copy.wait()
    prefix_ref[1] = maps[0]
    run = [maps[0, h * DK : (h + 1) * DK, :].astype(F32) for h in range(GROUP)]
    run_c = [factor(maps[0, GROUP * DK : ROWS, :], h) for h in range(GROUP)]
    for a in range(1, 4):
        tail = maps[a, GROUP * DK : ROWS, :]
        for h in range(GROUP):
            here = slice(h * DK, (h + 1) * DK)
            c = factor(tail, h)
            run[h] = compose(run[h], run_c[h], maps[a, here, :], c)
            run_c[h] = run_c[h] * c
            if a < 3:
                prefix_ref[a + 1, here, :] = run[h].astype(BF16)
            else:
                plane_ref[here, :] = run[h].astype(BF16)
                exit_ref[here, :] = run[h][:, DK:].astype(BF16)
        if a < 3:
            prefix_ref[a + 1, GROUP * DK : ROWS, :] = pack_factors(run_c)
    plane_ref[GROUP * DK : ROWS, :] = pack_factors(run_c)


def plane_maps(meta, pieces):
    return pl.pallas_call(
        plane_kernel,
        in_specs=[smem_spec()] + [pl.BlockSpec(memory_space=pl.ANY)] * 4,
        out_specs=[whole_spec()] * 3,
        out_shape=[
            jax.ShapeDtypeStruct((4, ROWS, 256), BF16),
            jax.ShapeDtypeStruct((ROWS, 256), BF16),
            jax.ShapeDtypeStruct((GROUP * DK, DV), BF16),
        ],
        scratch_shapes=[pltpu.VMEM((4, ROWS, 256), BF16), pltpu.SemaphoreType.DMA((4,))],
        compiler_params=params(),
        cost_estimate=pl.CostEstimate(
            flops=12 * 2 * 2 * 128**3, bytes_accessed=2 * 2**20, transcendentals=0
        ),
        name="plane",
    )(meta, *pieces)


def hop_kernel(plane_ref, state_ref, out_ref):
    tail = plane_ref[GROUP * DK : ROWS, :]
    for h in range(GROUP):
        here = slice(h * DK, (h + 1) * DK)
        out_ref[here, :] = apply_map(plane_ref[here, :], factor(tail, h), state_ref[here, :]).astype(
            BF16
        )


def hop(plane_map, state):
    return pl.pallas_call(
        hop_kernel,
        in_specs=[whole_spec()] * 2,
        out_specs=whole_spec(),
        out_shape=jax.ShapeDtypeStruct((GROUP * DK, DV), BF16),
        compiler_params=params(),
        cost_estimate=pl.CostEstimate(
            flops=4 * 2 * 128**3, bytes_accessed=2**19, transcendentals=0
        ),
        name="hop",
    )(plane_map, state)


def spread_kernel(meta, prefix_ref, *refs):
    out_refs = refs[-4:]
    state_refs = refs[:-4]
    for h in range(GROUP):
        here = slice(h * DK, (h + 1) * DK)
        state = state_refs[0][here, :].astype(F32)
        for ref in state_refs[1:]:
            state = state + ref[here, :].astype(F32)
        state = state.astype(BF16)
        for m, out_ref in enumerate(out_refs):
            a = meta[3] ^ m
            c = factor(prefix_ref[a, GROUP * DK : ROWS, :], h)
            out_ref[here, :] = apply_map(prefix_ref[a, here, :], c, state).astype(BF16)


def spread(meta, prefix, states):
    return pl.pallas_call(
        spread_kernel,
        in_specs=[smem_spec()] + [whole_spec()] * (1 + len(states)),
        out_specs=[whole_spec()] * 4,
        out_shape=[jax.ShapeDtypeStruct((GROUP * DK, DV), BF16)] * 4,
        compiler_params=params(),
        cost_estimate=pl.CostEstimate(
            flops=16 * 2 * 128**3, bytes_accessed=2**21, transcendentals=0
        ),
        name="spread",
    )(meta, prefix, *states)


def emit_kernel(slot, meta, r_ref, d_ref, e0, e1, e2, e3, *refs):
    out_ref, rows, sems = refs[-3:]
    copies = []
    for m, e_ref in enumerate((e0, e1, e2, e3)):
        g = meta[3] ^ m
        for h in range(GROUP):
            here = slice(h * TOK, (h + 1) * TOK)
            total = dot(r_ref[g, here, :], e_ref[here, :]) + d_ref[g, here, :]
            rows[m, :, h * DV : (h + 1) * DV] = total.astype(BF16)
        start = pl.multiple_of((meta[slot] + g) * (GROUP * DV), GROUP * DV)
        copy = pltpu.make_async_copy(
            rows.at[m], out_ref.at[:, pl.ds(start, GROUP * DV)], sems.at[m]
        )
        copy.start()
        copies.append(copy)
    for copy in copies:
        copy.wait()


def emit(meta, slot, reads, direct, states, into=None):
    in_specs = [smem_spec()] + [whole_spec()] * 6
    args = [meta, reads, direct, *states]
    aliases = {}
    if into is not None:
        in_specs.append(pl.BlockSpec(memory_space=pl.ANY))
        args.append(into)
        aliases = {7: 0}
    return pl.pallas_call(
        functools.partial(emit_kernel, slot),
        in_specs=in_specs,
        out_specs=pl.BlockSpec(memory_space=pl.ANY),
        out_shape=jax.ShapeDtypeStruct((TOK, HV * DV), BF16),
        scratch_shapes=[pltpu.VMEM((4, TOK, GROUP * DV), BF16), pltpu.SemaphoreType.DMA((4,))],
        input_output_aliases=aliases,
        compiler_params=params(),
        cost_estimate=pl.CostEstimate(
            flops=16 * 2 * 128**3, bytes_accessed=3 * 2**20, transcendentals=0
        ),
        name="emit",
    )(*args)


def shards(projected, conv_weight, decay_log, write_strength, starts):
    count = lax.axis_size("seq")
    me = lax.axis_index("seq")
    core, place = me & 1, (me >> 1) & 3
    slots = lax.iota(jnp.int32, 4)
    meta = jnp.where(
        slots == 0,
        4 * (1 - core),
        jnp.where(slots == 1, 4 * core, jnp.where(slots == 2, core, place)),
    ).astype(jnp.int32)

    def exchange(block, bits):
        return lax.ppermute(block, "seq", [(i, i ^ bits) for i in range(count)])

    tables, tail_rows = prologue(decay_log, write_strength, starts, projected)
    halo = lax.ppermute(tail_rows, "seq", [(i, i + 1) for i in range(count - 1)])

    pay_s, kt_s, ef_s = make_maps(meta, 0, projected, halo, conv_weight, tables)
    other = exchange(pay_s, 1)
    mine, kt_k, ef_k = make_maps(meta, 1, projected, halo, conv_weight, tables)
    x0, x1, x2, x3 = pair_maps(meta, mine, other)
    x3, x1, x2 = exchange(x3, 6), exchange(x1, 2), exchange(x2, 4)
    left = lax.ppermute(mine, "seq", [(i, i + 1) for i in range(0, count, 2)])
    r_k, d_k = make_reads(meta, 1, projected, halo, conv_weight, tables, kt_k, ef_k, other)
    r_s, d_s = make_reads(meta, 0, projected, halo, conv_weight, tables, kt_s, ef_s, left)
    x0, r_k, d_k, r_s, d_s = lax.optimization_barrier((x0, r_k, d_k, r_s, d_s))
    prefix, plane_map, leaving = plane_maps(meta, (x0, x1, x2, x3))
    planes = count // 8
    received = []
    for step in range(planes - 1):
        route = [(i, i + 8) for i in range(8 * step, 8 * step + 8)]
        state = lax.ppermute(leaving, "seq", route)
        received.append(state)
        if step < planes - 2:
            leaving = hop(plane_map, state)
    if not received:
        received.append(jnp.zeros_like(leaving))
    e0, e1, e2, e3 = spread(meta, prefix, received)
    e3, e1, e2 = exchange(e3, 6), exchange(e1, 2), exchange(e2, 4)
    states = (e0, e1, e2, e3)
    partner = [exchange(e, 1) for e in states]
    out = emit(meta, 1, r_k, d_k, states)
    return emit(meta, 0, r_s, d_s, partner, into=out)


def solution(mesh):
    in_specs = (
        P(("groups", "seq"), None),
        P(),
        P(None, ("groups", "seq")),
        P(None, ("groups", "seq")),
        P(("groups", "seq")),
    )
    out_specs = P(("groups", "seq"), None)
    return jax.shard_map(shards, mesh=mesh, in_specs=in_specs, out_specs=out_specs, check_vma=False)
```

```python
import functools

import jax
import jax.numpy as jnp
from jax import lax
from jax.experimental import pallas as pl
from jax.experimental.pallas import tpu as pltpu
from jax.sharding import PartitionSpec as P

HK = 16
DK = 128
HV = 32
DV = 128
KW = 4
TOK = 128
NORM_EPS = 1e-06
GROUP = 4
LOG2E = 1.4426950408889634
HIDDEN = -1e30
ROWS = GROUP * DK + 16
F32 = jnp.float32
BF16 = jnp.bfloat16


def dot(a, b):
    return jnp.dot(a, b, preferred_element_type=F32)


def halves(a):
    high = a.astype(BF16)
    return high, (a - high.astype(F32)).astype(BF16)


def params(**kw):
    return pltpu.CompilerParams(vmem_limit_bytes=20 << 20, **kw)


def whole_spec():
    return pl.BlockSpec(memory_space=pltpu.VMEM)


def smem_spec():
    return pl.BlockSpec(memory_space=pltpu.SMEM)


def in_hbm(x):
    return pltpu.with_memory_space_constraint(x, pltpu.HBM)


def prologue_kernel(
    decay_ref, beta_ref, starts_ref, x_ref, x_hbm, w_hbm, out_ref, tail_ref, x_out, w_out, sems
):
    rows = x_ref.shape[0]
    stage = [
        pltpu.make_async_copy(x_hbm, x_out, sems.at[0]),
        pltpu.make_async_copy(w_hbm, w_out, sems.at[1]),
    ]
    for copy in stage:
        copy.start()
    flags = starts_ref[...].astype(F32)
    last = 1.0 - flags[:, TOK - 1 : TOK]
    keep = [last * (1.0 - flags[:, TOK - 2 : TOK - 1]), last, jnp.ones((1, 1), F32)]
    for r in range(KW - 1):
        row = x_ref[rows - KW + 1 + r : rows - KW + 2 + r, :].astype(F32)
        tail_ref[r : r + 1, :] = (row * keep[r]).astype(BF16)
    src = lax.broadcasted_iota(jnp.int32, (TOK, TOK), 0)
    dst = lax.broadcasted_iota(jnp.int32, (TOK, TOK), 1)
    upto = (src <= dst).astype(F32)
    cum = LOG2E * jnp.dot(
        decay_ref[...], upto, precision=lax.Precision.HIGHEST, preferred_element_type=F32
    )
    flags = jnp.broadcast_to(flags, (8, TOK)).astype(BF16)
    episode = [dot(flags, (src + j <= dst).astype(BF16))[0:1] for j in range(KW)]
    usable = [(episode[0] == episode[j]).astype(F32) for j in range(1, KW)]
    living = (episode[0] == 0.0).astype(F32)
    zero = jnp.zeros((1, TOK), F32)
    shared = jnp.concatenate(usable + [episode[0], living, zero, zero, zero], axis=0)
    for pair in range(HV // GROUP):
        out_ref[pair, 0:4, :] = cum[GROUP * pair : GROUP * (pair + 1)]
        out_ref[pair, 4:8, :] = beta_ref[GROUP * pair : GROUP * (pair + 1), :]
        out_ref[pair, 8:16, :] = shared
    for copy in stage:
        copy.wait()


def prologue(decay_log, write_strength, starts, projected, conv_weight):
    channels = projected.shape[1]
    last = projected.shape[0] // 16 - 1
    return pl.pallas_call(
        prologue_kernel,
        grid=(1,),
        in_specs=[
            pl.BlockSpec((HV, TOK), lambda i: (0, 0)),
            pl.BlockSpec((HV, TOK), lambda i: (0, 0)),
            pl.BlockSpec((1, TOK), lambda i: (0, 0)),
            pl.BlockSpec((16, channels), lambda i: (last, 0)),
            pl.BlockSpec(memory_space=pl.ANY),
            pl.BlockSpec(memory_space=pl.ANY),
        ],
        out_specs=[
            pl.BlockSpec((HV // GROUP, 16, TOK), lambda i: (0, 0, 0)),
            pl.BlockSpec((KW - 1, channels), lambda i: (0, 0)),
            whole_spec(),
            whole_spec(),
        ],
        out_shape=[
            jax.ShapeDtypeStruct((HV // GROUP, 16, TOK), F32),
            jax.ShapeDtypeStruct((KW - 1, channels), BF16),
            jax.ShapeDtypeStruct(projected.shape, BF16),
            jax.ShapeDtypeStruct(conv_weight.shape, BF16),
        ],
        scratch_shapes=[pltpu.SemaphoreType.DMA((2,))],
        compiler_params=params(),
        cost_estimate=pl.CostEstimate(flops=10**7, bytes_accessed=10**6, transcendentals=0),
        name="prologue",
    )(
        in_hbm(decay_log),
        in_hbm(write_strength),
        in_hbm(starts.reshape(1, TOK)),
        in_hbm(projected),
        in_hbm(projected),
        in_hbm(conv_weight),
    )


def place_window(x, halo, xs, first):
    cols = slice(first, first + x.shape[1])
    xs[8 : 8 + TOK, cols] = x.astype(F32)
    xs[8 - KW + 1 : 8, cols] = halo.astype(F32)


def convolve_piece(xs, first, taps, usable):
    here = slice(first, first + 128)
    total = xs[8 : 8 + TOK, here] * taps[3:4]
    for j in range(1, KW):
        total = total + (xs[8 - j : 8 - j + TOK, here] * usable[j - 1]) * taps[3 - j : 4 - j]
    return (total / (1.0 + jnp.exp2(total * -LOG2E))).astype(BF16)


def column(cols, lane):
    return jnp.broadcast_to(cols[:, lane : lane + 1], (TOK, 128))


def positions():
    i = lax.broadcasted_iota(jnp.int32, (TOK, TOK), 0)
    j = lax.broadcasted_iota(jnp.int32, (TOK, TOK), 1)
    return i, j


def hidden_where(rows, cols):
    i, j = positions()
    seen = (column(cols, 11) == rows[11:12, :]) & (i >= j)
    return jnp.where(seen, 0.0, HIDDEN)


def decay_within(rows, clock, head, hidden):
    return jnp.exp2((clock - rows[head : head + 1, :]) + hidden)


def unit(x, scale=1.0):
    return lax.rsqrt(jnp.sum(x * x, axis=-1, keepdims=True) + NORM_EPS) * scale


def split_rows(x):
    pieces, rest = [], list(x)
    for _ in range(3):
        highs = [c.astype(BF16).astype(F32) for c in rest]
        pieces += highs
        rest = [c - high for c, high in zip(rest, highs)]
    pieces.append(jnp.zeros((4, 256), F32))
    return jnp.concatenate(pieces, axis=0).astype(BF16)


LEVELS = 7
HEADS = 8


def odd_rows(get, size):
    return jnp.concatenate([get(r, r + size) for r in range(size, TOK, 2 * size)], axis=0)


def map_kernel(
    slot, meta, x_ref, halo_ref, w_ref, tab_ref, pay_ref, kt_ref, ef_ref, xs, masks, shared, sys,
    inv, right,
):
    rows0 = tab_ref[0]
    cols0 = jnp.transpose(rows0)
    for j in range(KW - 1):
        shared[j] = column(cols0, 8 + j)
    shared[3] = column(cols0, 12)
    shared[4] = hidden_where(rows0, cols0)
    i, j = positions()
    apart = i ^ j
    for level in range(LEVELS):
        masks[level] = (((apart >> level) == 1) & (i > j)).astype(F32).astype(BF16)
    shared[5] = (i > j).astype(F32)
    masks[LEVELS] = (i == j).astype(F32).astype(BF16)

    def half(it, _):
        usable = [shared[j] for j in range(KW - 1)]
        pair = meta[slot] + 2 * it
        k_at = pl.multiple_of(HK * DK + pair * 256, 512)
        v_at = pl.multiple_of(2 * HK * DK + pair * 512, 1024)
        place_window(x_ref[:, pl.ds(k_at, 512)], halo_ref[:, pl.ds(k_at, 512)], xs, 0)
        place_window(x_ref[:, pl.ds(v_at, 1024)], halo_ref[:, pl.ds(v_at, 1024)], xs, 512)
        k_taps = w_ref[:, pl.ds(k_at, 512)].astype(F32)
        v_taps = w_ref[:, pl.ds(v_at, 1024)].astype(F32)
        endings, last, betas = [], [], []
        for p in range(2):
            rows = tab_ref[pair + p]
            cols = jnp.transpose(rows)
            for a in range(2):
                at = (2 * p + a) * DK
                k = convolve_piece(xs, at, k_taps[:, at : at + DK], usable).astype(F32)
                k = k * unit(k)
                kb = k.astype(BF16)
                ktb = jnp.transpose(kb.astype(F32)).astype(BF16)
                kt_ref[2 * it + p, a * DK : (a + 1) * DK, :] = ktb
                inner = dot(kb, ktb) * shared[5]
                for b in range(2):
                    lane = 2 * a + b
                    h = GROUP * p + lane
                    clock = column(cols, lane)
                    within = decay_within(rows, clock, lane, shared[4])
                    carried = jnp.exp2(clock) * shared[3]
                    system = (column(cols, 4 + lane) * within) * inner
                    high, low = halves(system)
                    sys[h, :, 0:128] = high
                    sys[h, :, 128:256] = low
                    inv[h] = masks[LEVELS] - high * masks[0]
                    right[h, :, 0:DK] = (carried * k).astype(BF16)
                    endings.append(within[TOK - 1 : TOK, :])
                    last.append(jnp.concatenate([carried[TOK - 1 : TOK, :]] * 2, axis=1))
                    betas.append(rows[4 + lane : 5 + lane, :])

        def value(h):
            at = h * DV
            right[h, :, DK : DK + DV] = convolve_piece(
                xs, 512 + at, v_taps[:, at : at + DV], usable
            )

        waiting = list(range(HEADS))
        for level in range(1, LEVELS):
            size = 1 << level
            steps = []
            for h in range(HEADS):
                if size < 16:
                    left = sys[h, :, 0:128]
                else:
                    left = odd_rows(lambda r, e: sys[h, r:e, 0:128], size)
                steps.append(dot(left, inv[h]).astype(BF16))
            if waiting:
                value(waiting.pop(0))
            if size < 16:
                steps = [dot(inv[h], steps[h]).astype(BF16) for h in range(HEADS)]
                for h in range(HEADS):
                    inv[h] = inv[h] - steps[h] * masks[level]
            else:
                blank = jnp.zeros((size, 128), BF16)
                found = []
                for h in range(HEADS):
                    spread_out = []
                    for r in range(0, TOK // 2, size):
                        spread_out += [blank, steps[h][r : r + size]]
                    left = odd_rows(lambda r, e: inv[h, r:e, :], size)
                    found.append(dot(left, jnp.concatenate(spread_out, axis=0)).astype(BF16))
                for h in range(HEADS):
                    for n, r in enumerate(range(size, TOK, 2 * size)):
                        inv[h, r : r + size, :] = inv[h, r : r + size, :] - (
                            found[h][n * size : (n + 1) * size] * masks[level, r : r + size, :]
                        )
            if waiting:
                value(waiting.pop(0))
        gaps = []
        for h in range(HEADS):
            rough = inv[h]
            product = dot(sys[h], jnp.concatenate([rough, rough], axis=0))
            gaps.append(((masks[LEVELS].astype(F32) - rough.astype(F32)) - product).astype(BF16))
        for h in range(HEADS):
            fixed = inv[h].astype(F32) + dot(inv[h], gaps[h])
            inv[h] = (fixed * betas[h]).astype(BF16)
        efs = []
        for h in range(HEADS):
            ef = dot(inv[h], right[h]).astype(BF16)
            ef_ref[2 * it + h // GROUP, (h % GROUP) * TOK : (h % GROUP + 1) * TOK, :] = ef
            efs.append(ef)
        for h in range(HEADS):
            g, n = h // GROUP, h % GROUP
            kt = kt_ref[2 * it + g, (n // 2) * DK : (n // 2 + 1) * DK, :].astype(F32)
            weighted = (kt * endings[h]).astype(BF16)
            pay_ref[2 * it + g, n * DK : (n + 1) * DK, :] = dot(weighted, efs[h]).astype(BF16)
        for g in range(2):
            pay_ref[2 * it + g, GROUP * DK : ROWS, :] = split_rows(
                last[GROUP * g : GROUP * (g + 1)]
            )
        return 0

    lax.fori_loop(0, 2, half, 0)


def make_maps(meta, slot, projected, halo, conv_weight, tables):
    return pl.pallas_call(
        functools.partial(map_kernel, slot),
        in_specs=[smem_spec()] + [whole_spec()] * 4,
        out_specs=[whole_spec()] * 3,
        out_shape=[
            jax.ShapeDtypeStruct((4, ROWS, 256), BF16),
            jax.ShapeDtypeStruct((4, 2 * DK, TOK), BF16),
            jax.ShapeDtypeStruct((4, GROUP * TOK, 256), BF16),
        ],
        scratch_shapes=[
            pltpu.VMEM((8 + TOK, 1536), F32),
            pltpu.VMEM((LEVELS + 1, TOK, TOK), BF16),
            pltpu.VMEM((6, TOK, 128), F32),
            pltpu.VMEM((HEADS, TOK, 256), BF16),
            pltpu.VMEM((HEADS, TOK, TOK), BF16),
            pltpu.VMEM((HEADS, TOK, 256), BF16),
        ],
        compiler_params=params(),
        cost_estimate=pl.CostEstimate(
            flops=16 * 20 * 2 * 128**3, bytes_accessed=5 * 2**20, transcendentals=10**6
        ),
        name="maps",
    )(meta, projected, halo, conv_weight, tables)


def read_kernel(meta, xq_ref, hq_ref, wq_ref, rows_ref, kt_ref, ef_ref, left_ref, r_ref, d_ref, xs):
    first = meta[2] == 0
    tail = left_ref[0, GROUP * DK : ROWS, :]
    rows = rows_ref[0]
    cols = jnp.transpose(rows)
    usable = [column(cols, 8 + j) for j in range(KW - 1)]
    living = column(cols, 12)
    hidden = hidden_where(rows, cols)
    place_window(xq_ref[...], hq_ref[...], xs, 0)
    taps = wq_ref[...].astype(F32)
    for a in range(2):
        queries = convolve_piece(xs, a * DK, taps[:, a * DK : (a + 1) * DK], usable)
        q = queries.astype(F32)
        scale = unit(q, DK ** (-0.5))
        inner = dot(queries, kt_ref[0, a * DK : (a + 1) * DK, :])
        for b in range(2):
            h = 2 * a + b
            clock = column(cols, h)
            scores = (inner * decay_within(rows, clock, h, hidden)).astype(BF16)
            both = dot(scores, ef_ref[0, h * TOK : (h + 1) * TOK, :])
            carried = jnp.exp2(clock) * living
            mine = slice(h * TOK, (h + 1) * TOK)
            reader = (carried * q - both[:, :DK]) * scale
            direct = both[:, DK:] * scale
            moved = dot(reader.astype(BF16), left_ref[0, h * DK : (h + 1) * DK, :])
            c = factor(tail, h)[:, :DK]
            r_ref[0, mine, :] = jnp.where(first, reader, c * reader - moved[:, :DK]).astype(BF16)
            d_ref[0, mine, :] = jnp.where(first, direct, direct + moved[:, DK:])


def make_reads(meta, slot, projected, halo, conv_weight, tables, keys_t, ef, left):
    def at(i, m):
        return (0, m[slot] + i)

    return pl.pallas_call(
        read_kernel,
        grid_spec=pltpu.PrefetchScalarGridSpec(
            num_scalar_prefetch=1,
            grid=(4,),
            in_specs=[
                pl.BlockSpec((TOK, 256), at),
                pl.BlockSpec((KW - 1, 256), at),
                pl.BlockSpec((KW, 256), at),
                pl.BlockSpec((1, 16, TOK), lambda i, m: (m[slot] + i, 0, 0)),
                pl.BlockSpec((1, 2 * DK, TOK), lambda i, m: (i, 0, 0)),
                pl.BlockSpec((1, GROUP * TOK, 256), lambda i, m: (i, 0, 0)),
                pl.BlockSpec((1, ROWS, 256), lambda i, m: (i, 0, 0)),
            ],
            out_specs=[
                pl.BlockSpec((1, GROUP * TOK, DK), lambda i, m: (i, 0, 0)),
                pl.BlockSpec((1, GROUP * TOK, DV), lambda i, m: (i, 0, 0)),
            ],
            scratch_shapes=[pltpu.VMEM((8 + TOK, 256), F32)],
        ),
        out_shape=[
            jax.ShapeDtypeStruct((4, GROUP * TOK, DK), BF16),
            jax.ShapeDtypeStruct((4, GROUP * TOK, DV), F32),
        ],
        compiler_params=params(),
        cost_estimate=pl.CostEstimate(
            flops=16 * 6 * 2 * 128**3, bytes_accessed=5 * 2**20, transcendentals=10**6
        ),
        name="reads",
    )(meta, projected, halo, conv_weight, tables, keys_t, ef, left)


def factor(tail, head):
    tail = tail.astype(F32)
    return (tail[head : head + 1] + tail[4 + head : 5 + head]) + tail[8 + head : 9 + head]


def compose(left, left_c, right, right_c):
    right_d = right[:, :DK]
    product = dot(right_d.astype(BF16), left.astype(BF16))
    return (
        right_c * left.astype(F32)
        + jnp.concatenate(
            [left_c[:, :DK] * right_d.astype(F32), right[:, DK:].astype(F32)], axis=1
        )
        - product
    )


def apply_map(each, c, state):
    product = dot(each[:, :DK], state)
    return c[:, :DK] * state.astype(F32) + each[:, DK:].astype(F32) - product


def pair_kernel(meta, mine_ref, other_ref, *out_refs):
    first = meta[2] == 0
    for m, out_ref in enumerate(out_refs):
        g = meta[3] ^ m
        tail_m, tail_o = mine_ref[g, GROUP * DK : ROWS, :], other_ref[g, GROUP * DK : ROWS, :]
        tail_l, tail_r = jnp.where(first, tail_m, tail_o), jnp.where(first, tail_o, tail_m)
        factors = []
        for h in range(GROUP):
            here = slice(h * DK, (h + 1) * DK)
            own, other = mine_ref[g, here, :], other_ref[g, here, :]
            left, right = jnp.where(first, own, other), jnp.where(first, other, own)
            left_c, right_c = factor(tail_l, h), factor(tail_r, h)
            out_ref[here, :] = compose(left, left_c, right, right_c).astype(BF16)
            factors.append(left_c * right_c)
        out_ref[GROUP * DK : ROWS, :] = split_rows(factors)


def pair_maps(meta, mine, other):
    return pl.pallas_call(
        pair_kernel,
        in_specs=[smem_spec(), whole_spec(), whole_spec()],
        out_specs=[whole_spec()] * 4,
        out_shape=[jax.ShapeDtypeStruct((ROWS, 256), BF16)] * 4,
        compiler_params=params(),
        cost_estimate=pl.CostEstimate(
            flops=16 * 2 * 2 * 128**3, bytes_accessed=3 * 2**20, transcendentals=0
        ),
        name="pair",
    )(meta, mine, other)


def plane_kernel(meta, x0, x1, x2, x3, prefix_ref, plane_ref, exit_ref, maps, sems):
    copies = []
    for m, x in enumerate((x0, x1, x2, x3)):
        copy = pltpu.make_async_copy(x, maps.at[meta[3] ^ m], sems.at[m])
        copy.start()
        copies.append(copy)
    prefix_ref[0, 0 : GROUP * DK, :] = jnp.zeros((GROUP * DK, 256), BF16)
    ones = jnp.ones((1, 256), F32)
    prefix_ref[0, GROUP * DK : ROWS, :] = split_rows([ones] * GROUP)
    for copy in copies:
        copy.wait()
    prefix_ref[1] = maps[0]
    run = [maps[0, h * DK : (h + 1) * DK, :].astype(F32) for h in range(GROUP)]
    run_c = [factor(maps[0, GROUP * DK : ROWS, :], h) for h in range(GROUP)]
    for a in range(1, 4):
        tail = maps[a, GROUP * DK : ROWS, :]
        for h in range(GROUP):
            here = slice(h * DK, (h + 1) * DK)
            c = factor(tail, h)
            run[h] = compose(run[h], run_c[h], maps[a, here, :], c)
            run_c[h] = run_c[h] * c
            if a < 3:
                prefix_ref[a + 1, here, :] = run[h].astype(BF16)
            else:
                plane_ref[here, :] = run[h].astype(BF16)
                exit_ref[here, :] = run[h][:, DK:].astype(BF16)
        if a < 3:
            prefix_ref[a + 1, GROUP * DK : ROWS, :] = split_rows(run_c)
    plane_ref[GROUP * DK : ROWS, :] = split_rows(run_c)


def plane_maps(meta, pieces):
    return pl.pallas_call(
        plane_kernel,
        in_specs=[smem_spec()] + [pl.BlockSpec(memory_space=pl.ANY)] * 4,
        out_specs=[whole_spec()] * 3,
        out_shape=[
            jax.ShapeDtypeStruct((4, ROWS, 256), BF16),
            jax.ShapeDtypeStruct((ROWS, 256), BF16),
            jax.ShapeDtypeStruct((GROUP * DK, DV), BF16),
        ],
        scratch_shapes=[pltpu.VMEM((4, ROWS, 256), BF16), pltpu.SemaphoreType.DMA((4,))],
        compiler_params=params(),
        cost_estimate=pl.CostEstimate(
            flops=12 * 2 * 2 * 128**3, bytes_accessed=2 * 2**20, transcendentals=0
        ),
        name="plane",
    )(meta, *pieces)


def hop_kernel(plane_ref, state_ref, out_ref):
    tail = plane_ref[GROUP * DK : ROWS, :]
    for h in range(GROUP):
        here = slice(h * DK, (h + 1) * DK)
        out_ref[here, :] = apply_map(plane_ref[here, :], factor(tail, h), state_ref[here, :]).astype(
            BF16
        )


def hop(plane_map, state):
    return pl.pallas_call(
        hop_kernel,
        in_specs=[whole_spec()] * 2,
        out_specs=whole_spec(),
        out_shape=jax.ShapeDtypeStruct((GROUP * DK, DV), BF16),
        compiler_params=params(),
        cost_estimate=pl.CostEstimate(
            flops=4 * 2 * 128**3, bytes_accessed=2**19, transcendentals=0
        ),
        name="hop",
    )(plane_map, state)


def spread_kernel(meta, prefix_ref, *refs):
    out_refs = refs[-4:]
    state_refs = refs[:-4]
    for h in range(GROUP):
        here = slice(h * DK, (h + 1) * DK)
        state = state_refs[0][here, :].astype(F32)
        for ref in state_refs[1:]:
            state = state + ref[here, :].astype(F32)
        state = state.astype(BF16)
        for m, out_ref in enumerate(out_refs):
            a = meta[3] ^ m
            c = factor(prefix_ref[a, GROUP * DK : ROWS, :], h)
            out_ref[here, :] = apply_map(prefix_ref[a, here, :], c, state).astype(BF16)


def spread(meta, prefix, states):
    return pl.pallas_call(
        spread_kernel,
        in_specs=[smem_spec()] + [whole_spec()] * (1 + len(states)),
        out_specs=[whole_spec()] * 4,
        out_shape=[jax.ShapeDtypeStruct((GROUP * DK, DV), BF16)] * 4,
        compiler_params=params(),
        cost_estimate=pl.CostEstimate(
            flops=16 * 2 * 128**3, bytes_accessed=2**21, transcendentals=0
        ),
        name="spread",
    )(meta, prefix, *states)


def emit_kernel(slot, meta, r_ref, d_ref, e0, e1, e2, e3, *refs):
    out_ref, rows, sems = refs[-3:]
    copies = []
    for m, e_ref in enumerate((e0, e1, e2, e3)):
        g = meta[3] ^ m
        for h in range(GROUP):
            here = slice(h * TOK, (h + 1) * TOK)
            total = dot(r_ref[g, here, :], e_ref[here, :]) + d_ref[g, here, :]
            rows[m, :, h * DV : (h + 1) * DV] = total.astype(BF16)
        start = pl.multiple_of((meta[slot] + g) * (GROUP * DV), GROUP * DV)
        copy = pltpu.make_async_copy(
            rows.at[m], out_ref.at[:, pl.ds(start, GROUP * DV)], sems.at[m]
        )
        copy.start()
        copies.append(copy)
    for copy in copies:
        copy.wait()


def emit(meta, slot, reads, direct, states, into=None):
    in_specs = [smem_spec()] + [whole_spec()] * 6
    args = [meta, reads, direct, *states]
    aliases = {}
    if into is not None:
        in_specs.append(pl.BlockSpec(memory_space=pl.ANY))
        args.append(into)
        aliases = {7: 0}
    return pl.pallas_call(
        functools.partial(emit_kernel, slot),
        in_specs=in_specs,
        out_specs=pl.BlockSpec(memory_space=pl.ANY),
        out_shape=jax.ShapeDtypeStruct((TOK, HV * DV), BF16),
        scratch_shapes=[pltpu.VMEM((4, TOK, GROUP * DV), BF16), pltpu.SemaphoreType.DMA((4,))],
        input_output_aliases=aliases,
        compiler_params=params(),
        cost_estimate=pl.CostEstimate(
            flops=16 * 2 * 128**3, bytes_accessed=3 * 2**20, transcendentals=0
        ),
        name="emit",
    )(*args)


def shards(projected, conv_weight, decay_log, write_strength, starts):
    count = lax.axis_size("seq")
    me = lax.axis_index("seq")
    core, place = me & 1, (me >> 1) & 3
    slots = lax.iota(jnp.int32, 4)
    meta = jnp.where(
        slots == 0,
        4 * (1 - core),
        jnp.where(slots == 1, 4 * core, jnp.where(slots == 2, core, place)),
    ).astype(jnp.int32)

    def exchange(block, bits):
        return lax.ppermute(block, "seq", [(i, i ^ bits) for i in range(count)])

    tables, tail_rows, projected, conv_weight = prologue(
        decay_log, write_strength, starts, projected, conv_weight
    )
    halo = lax.ppermute(tail_rows, "seq", [(i, i + 1) for i in range(count - 1)])

    pay_s, kt_s, ef_s = make_maps(meta, 0, projected, halo, conv_weight, tables)
    other = exchange(pay_s, 1)
    mine, kt_k, ef_k = make_maps(meta, 1, projected, halo, conv_weight, tables)
    x0, x1, x2, x3 = pair_maps(meta, mine, other)
    x3, x1, x2 = exchange(x3, 6), exchange(x1, 2), exchange(x2, 4)
    left = lax.ppermute(mine, "seq", [(i, i + 1) for i in range(0, count, 2)])
    r_k, d_k = make_reads(meta, 1, projected, halo, conv_weight, tables, kt_k, ef_k, other)
    r_s, d_s = make_reads(meta, 0, projected, halo, conv_weight, tables, kt_s, ef_s, left)
    x0, r_k, d_k, r_s, d_s = lax.optimization_barrier((x0, r_k, d_k, r_s, d_s))
    prefix, plane_map, leaving = plane_maps(meta, (x0, x1, x2, x3))
    planes = count // 8
    received = []
    for step in range(planes - 1):
        route = [(i, i + 8) for i in range(8 * step, 8 * step + 8)]
        state = lax.ppermute(leaving, "seq", route)
        received.append(state)
        if step < planes - 2:
            leaving = hop(plane_map, state)
    if not received:
        received.append(jnp.zeros_like(leaving))
    e0, e1, e2, e3 = spread(meta, prefix, received)
    e3, e1, e2 = exchange(e3, 6), exchange(e1, 2), exchange(e2, 4)
    states = (e0, e1, e2, e3)
    partner = [exchange(e, 1) for e in states]
    out = emit(meta, 1, r_k, d_k, states)
    return emit(meta, 0, r_s, d_s, partner, into=out)


def solution(mesh):
    in_specs = (
        P(("groups", "seq"), None),
        P(),
        P(None, ("groups", "seq")),
        P(None, ("groups", "seq")),
        P(("groups", "seq")),
    )
    out_specs = P(("groups", "seq"), None)
    return jax.shard_map(shards, mesh=mesh, in_specs=in_specs, out_specs=out_specs, check_vma=False)
```

```python
import functools

import jax
import jax.numpy as jnp
from jax import lax
from jax.experimental import pallas as pl
from jax.experimental.pallas import tpu as pltpu
from jax.sharding import PartitionSpec as P

HK = 16
DK = 128
HV = 32
DV = 128
KW = 4
TOK = 128
NORM_EPS = 1e-06
GROUP = 4
LOG2E = 1.4426950408889634
HIDDEN = -1e30
ROWS = GROUP * DK + 16
F32 = jnp.float32
BF16 = jnp.bfloat16


def dot(a, b):
    return jnp.dot(a, b, preferred_element_type=F32)


def halves(a):
    high = a.astype(BF16)
    return high, (a - high.astype(F32)).astype(BF16)


def params(**kw):
    return pltpu.CompilerParams(vmem_limit_bytes=20 << 20, **kw)


def whole_spec():
    return pl.BlockSpec(memory_space=pltpu.VMEM)


def smem_spec():
    return pl.BlockSpec(memory_space=pltpu.SMEM)


def in_hbm(x):
    return pltpu.with_memory_space_constraint(x, pltpu.HBM)


def prologue_kernel(decay_ref, beta_ref, starts_ref, x_ref, out_ref, tail_ref):
    rows = x_ref.shape[0]
    flags = starts_ref[...].astype(F32)
    last = 1.0 - flags[:, TOK - 1 : TOK]
    keep = [last * (1.0 - flags[:, TOK - 2 : TOK - 1]), last, jnp.ones((1, 1), F32)]
    for r in range(KW - 1):
        row = x_ref[rows - KW + 1 + r : rows - KW + 2 + r, :].astype(F32)
        tail_ref[r : r + 1, :] = (row * keep[r]).astype(BF16)
    src = lax.broadcasted_iota(jnp.int32, (TOK, TOK), 0)
    dst = lax.broadcasted_iota(jnp.int32, (TOK, TOK), 1)
    upto = (src <= dst).astype(F32)
    cum = LOG2E * jnp.dot(
        decay_ref[...], upto, precision=lax.Precision.HIGHEST, preferred_element_type=F32
    )
    flags = jnp.broadcast_to(flags, (8, TOK)).astype(BF16)
    episode = [dot(flags, (src + j <= dst).astype(BF16))[0:1] for j in range(KW)]
    usable = [(episode[0] == episode[j]).astype(F32) for j in range(1, KW)]
    living = (episode[0] == 0.0).astype(F32)
    zero = jnp.zeros((1, TOK), F32)
    shared = jnp.concatenate(usable + [episode[0], living, zero, zero, zero], axis=0)
    for pair in range(HV // GROUP):
        out_ref[pair, 0:4, :] = cum[GROUP * pair : GROUP * (pair + 1)]
        out_ref[pair, 4:8, :] = beta_ref[GROUP * pair : GROUP * (pair + 1), :]
        out_ref[pair, 8:16, :] = shared


def prologue(decay_log, write_strength, starts, projected):
    channels = projected.shape[1]
    last = projected.shape[0] // 16 - 1
    return pl.pallas_call(
        prologue_kernel,
        grid=(1,),
        in_specs=[
            pl.BlockSpec((HV, TOK), lambda i: (0, 0)),
            pl.BlockSpec((HV, TOK), lambda i: (0, 0)),
            pl.BlockSpec((1, TOK), lambda i: (0, 0)),
            pl.BlockSpec((16, channels), lambda i: (last, 0)),
        ],
        out_specs=[
            pl.BlockSpec((HV // GROUP, 16, TOK), lambda i: (0, 0, 0)),
            pl.BlockSpec((KW - 1, channels), lambda i: (0, 0)),
        ],
        out_shape=[
            jax.ShapeDtypeStruct((HV // GROUP, 16, TOK), F32),
            jax.ShapeDtypeStruct((KW - 1, channels), BF16),
        ],
        compiler_params=params(),
        cost_estimate=pl.CostEstimate(flops=10**7, bytes_accessed=10**6, transcendentals=0),
        name="prologue",
    )(
        in_hbm(decay_log),
        in_hbm(write_strength),
        in_hbm(starts.reshape(1, TOK)),
        in_hbm(projected),
    )


def place_window(x, halo, xs, first):
    cols = slice(first, first + x.shape[1])
    xs[8 : 8 + TOK, cols] = x.astype(F32)
    xs[8 - KW + 1 : 8, cols] = halo.astype(F32)


def convolve_piece(xs, first, taps, usable):
    here = slice(first, first + 128)
    total = xs[8 : 8 + TOK, here] * taps[3:4]
    for j in range(1, KW):
        total = total + (xs[8 - j : 8 - j + TOK, here] * usable[j - 1]) * taps[3 - j : 4 - j]
    return (total / (1.0 + jnp.exp2(total * -LOG2E))).astype(BF16)


def column(cols, lane):
    return jnp.broadcast_to(cols[:, lane : lane + 1], (TOK, 128))


def positions():
    i = lax.broadcasted_iota(jnp.int32, (TOK, TOK), 0)
    j = lax.broadcasted_iota(jnp.int32, (TOK, TOK), 1)
    return i, j


def hidden_where(rows, cols):
    i, j = positions()
    seen = (column(cols, 11) == rows[11:12, :]) & (i >= j)
    return jnp.where(seen, 0.0, HIDDEN)


def decay_within(rows, clock, head, hidden):
    return jnp.exp2((clock - rows[head : head + 1, :]) + hidden)


def unit(x, scale=1.0):
    return lax.rsqrt(jnp.sum(x * x, axis=-1, keepdims=True) + NORM_EPS) * scale


def split_rows(x):
    pieces, rest = [], list(x)
    for _ in range(3):
        highs = [c.astype(BF16).astype(F32) for c in rest]
        pieces += highs
        rest = [c - high for c, high in zip(rest, highs)]
    pieces.append(jnp.zeros((4, 256), F32))
    return jnp.concatenate(pieces, axis=0).astype(BF16)


LEVELS = 7
HEADS = 8


def odd_rows(get, size):
    return jnp.concatenate([get(r, r + size) for r in range(size, TOK, 2 * size)], axis=0)


def stage_kernel(tab_ref, x_hbm, w_hbm, x_out, w_out, masks, shared, sems):
    copies = [
        pltpu.make_async_copy(x_hbm, x_out, sems.at[0]),
        pltpu.make_async_copy(w_hbm, w_out, sems.at[1]),
    ]
    for copy in copies:
        copy.start()
    rows = tab_ref[0]
    cols = jnp.transpose(rows)
    for j in range(KW - 1):
        shared[j] = column(cols, 8 + j)
    shared[3] = column(cols, 12)
    shared[4] = hidden_where(rows, cols)
    i, j = positions()
    apart = i ^ j
    for level in range(LEVELS):
        masks[level] = (((apart >> level) == 1) & (i > j)).astype(F32).astype(BF16)
    shared[5] = (i > j).astype(F32)
    masks[LEVELS] = (i == j).astype(F32).astype(BF16)
    for copy in copies:
        copy.wait()


def stage(tables, projected, conv_weight):
    return pl.pallas_call(
        stage_kernel,
        in_specs=[whole_spec()] + [pl.BlockSpec(memory_space=pl.ANY)] * 2,
        out_specs=[whole_spec()] * 4,
        out_shape=[
            jax.ShapeDtypeStruct(projected.shape, BF16),
            jax.ShapeDtypeStruct(conv_weight.shape, BF16),
            jax.ShapeDtypeStruct((LEVELS + 1, TOK, TOK), BF16),
            jax.ShapeDtypeStruct((6, TOK, 128), F32),
        ],
        scratch_shapes=[pltpu.SemaphoreType.DMA((2,))],
        compiler_params=params(),
        cost_estimate=pl.CostEstimate(flops=10**6, bytes_accessed=4 * 2**20, transcendentals=0),
        name="stage",
    )(tables, in_hbm(projected), in_hbm(conv_weight))


def preparing(pair, ins, xs, sys, right, keys):
    x_ref, halo_ref, w_ref, tab_ref, masks, shared = ins
    k_at = pl.multiple_of(HK * DK + pair * 256, 512)
    v_at = pl.multiple_of(2 * HK * DK + pair * 512, 1024)
    kt_ref, kt_at = keys

    def usable():
        return [shared[j] for j in range(KW - 1)]

    def place():
        place_window(x_ref[:, pl.ds(k_at, 512)], halo_ref[:, pl.ds(k_at, 512)], xs, 0)
        place_window(x_ref[:, pl.ds(v_at, 1024)], halo_ref[:, pl.ds(v_at, 1024)], xs, 512)

    def key(n):
        p, a = n // 2, n % 2
        rows = tab_ref[pair + p]
        cols = jnp.transpose(rows)
        at = n * DK
        taps = w_ref[:, pl.ds(k_at + at, DK)].astype(F32)
        k = convolve_piece(xs, at, taps, usable()).astype(F32)
        k = k * unit(k)
        kb = k.astype(BF16)
        ktb = jnp.transpose(kb.astype(F32)).astype(BF16)
        kt_ref[kt_at + p, a * DK : (a + 1) * DK, :] = ktb
        inner = dot(kb, ktb) * shared[5]
        for b in range(2):
            lane = 2 * a + b
            h = GROUP * p + lane
            clock = column(cols, lane)
            within = decay_within(rows, clock, lane, shared[4])
            carried = jnp.exp2(clock) * shared[3]
            high, low = halves((column(cols, 4 + lane) * within) * inner)
            sys[h, :, 0:128] = high
            sys[h, :, 128:256] = low
            right[h, :, 0:DK] = (carried * k).astype(BF16)

    def value(h):
        taps = w_ref[:, pl.ds(v_at + h * DV, DV)].astype(F32)
        right[h, :, DK : DK + DV] = convolve_piece(xs, 512 + h * DV, taps, usable())

    steps = [place]
    steps += [functools.partial(key, n) for n in range(4)]
    steps += [functools.partial(value, h) for h in range(HEADS)]
    return steps


def solving(pair, ins, sys, right, keys, inv, pay_ref, ef_ref, at, kt_copy=None):
    tab_ref, masks, shared = ins[3:]
    kt_ref, kt_at = keys
    kept = {}

    def begin():
        for h in range(HEADS):
            inv[h] = masks[LEVELS] - sys[h, :, 0:128] * masks[0]

    def first_product(level):
        size = 1 << level
        kept["steps"] = []
        for h in range(HEADS):
            if size < 16:
                left = sys[h, :, 0:128]
            else:
                left = odd_rows(lambda r, e: sys[h, r:e, 0:128], size)
            kept["steps"].append(dot(left, inv[h]).astype(BF16))

    def second_product(level):
        size = 1 << level
        steps = kept["steps"]
        if size < 16:
            steps = [dot(inv[h], steps[h]).astype(BF16) for h in range(HEADS)]
            for h in range(HEADS):
                inv[h] = inv[h] - steps[h] * masks[level]
            return
        blank = jnp.zeros((size, 128), BF16)
        found = []
        for h in range(HEADS):
            expanded = []
            for r in range(0, TOK // 2, size):
                expanded += [blank, steps[h][r : r + size]]
            left = odd_rows(lambda r, e: inv[h, r:e, :], size)
            found.append(dot(left, jnp.concatenate(expanded, axis=0)).astype(BF16))
        for h in range(HEADS):
            for n, r in enumerate(range(size, TOK, 2 * size)):
                inv[h, r : r + size, :] = inv[h, r : r + size, :] - (
                    found[h][n * size : (n + 1) * size] * masks[level, r : r + size, :]
                )

    def check():
        kept["gaps"] = []
        for h in range(HEADS):
            rough = inv[h]
            product = dot(sys[h], jnp.concatenate([rough, rough], axis=0))
            kept["gaps"].append(
                ((masks[LEVELS].astype(F32) - rough.astype(F32)) - product).astype(BF16)
            )

    def row(h, n):
        return tab_ref[pair + h // GROUP, n : n + 1, :]

    def correct():
        for h in range(HEADS):
            fixed = inv[h].astype(F32) + dot(inv[h], kept["gaps"][h])
            inv[h] = (fixed * row(h, 4 + h % GROUP)).astype(BF16)

    def apply():
        kept["ef"] = []
        for h in range(HEADS):
            ef = dot(inv[h], right[h]).astype(BF16)
            here = slice((h % GROUP) * TOK, (h % GROUP + 1) * TOK)
            ef_ref[at + h // GROUP, here, :] = ef
            kept["ef"].append(ef)

    def write():
        last = []
        for h in range(HEADS):
            g, n = h // GROUP, h % GROUP
            ktb = kt_ref[kt_at + g, (n // 2) * DK : (n // 2 + 1) * DK, :]
            if kt_copy is not None and n % 2 == 0:
                kt_copy[at + g, (n // 2) * DK : (n // 2 + 1) * DK, :] = ktb
            clock = row(h, n)
            final = jnp.broadcast_to(clock[:, TOK - 1 : TOK], (1, TOK))
            ending = jnp.exp2((final - clock) + shared[4, TOK - 1 : TOK, :])
            carried = jnp.exp2(final) * shared[3, TOK - 1 : TOK, :]
            last.append(jnp.concatenate([carried, carried], axis=1))
            weighted = (ktb.astype(F32) * ending).astype(BF16)
            pay_ref[at + g, n * DK : (n + 1) * DK, :] = dot(weighted, kept["ef"][h]).astype(BF16)
        for g in range(2):
            pay_ref[at + g, GROUP * DK : ROWS, :] = split_rows(last[GROUP * g : GROUP * (g + 1)])

    steps = [begin]
    for level in range(1, LEVELS):
        steps.append(functools.partial(first_product, level))
        steps.append(functools.partial(second_product, level))
    return steps + [check, correct, apply, write]


def interleave(main, side):
    done = 0
    for n, step in enumerate(main):
        step()
        due = ((n + 1) * len(side) + len(main) - 1) // len(main)
        while done < min(due, len(side)):
            side[done]()
            done += 1


def send_kernel(
    meta, x_ref, halo_ref, w_ref, tab_ref, masks, shared, pay_ref, kt_ref, ef_ref, sys_out,
    right_out, kt_out, xs, sys, right, inv,
):
    ins = (x_ref, halo_ref, w_ref, tab_ref, masks, shared)
    pair, after = meta[0], meta[1]
    sets = [(sys.at[n], right.at[n], (kt_ref, 2 * n)) for n in range(2)]
    third = (sys_out, right_out, (kt_out, 0))
    for step in preparing(pair, ins, xs, *sets[0]):
        step()
    for n in range(2):
        main = solving(pair + 2 * n, ins, *sets[n], inv, pay_ref, ef_ref, 2 * n)
        if n == 0:
            side = preparing(pair + 2, ins, xs, *sets[1])
        else:
            side = preparing(after, ins, xs, *third)
        interleave(main, side)


def keep_kernel(
    meta, x_ref, halo_ref, w_ref, tab_ref, masks, shared, sys_in, right_in, kt_in, pay_ref,
    kt_ref, ef_ref, xs, sys, right, inv,
):
    ins = (x_ref, halo_ref, w_ref, tab_ref, masks, shared)
    pair = meta[1]
    own = (sys, right, (kt_ref, 2))
    interleave(
        solving(pair, ins, sys_in, right_in, (kt_in, 0), inv, pay_ref, ef_ref, 0, kt_ref),
        preparing(pair + 2, ins, xs, *own),
    )
    for step in solving(pair + 2, ins, *own, inv, pay_ref, ef_ref, 2):
        step()


def map_shapes():
    return [
        jax.ShapeDtypeStruct((4, ROWS, 256), BF16),
        jax.ShapeDtypeStruct((4, 2 * DK, TOK), BF16),
        jax.ShapeDtypeStruct((4, GROUP * TOK, 256), BF16),
    ]


def ready_shapes():
    return [
        jax.ShapeDtypeStruct((HEADS, TOK, 256), BF16),
        jax.ShapeDtypeStruct((HEADS, TOK, 256), BF16),
        jax.ShapeDtypeStruct((2, 2 * DK, TOK), BF16),
    ]


def map_cost():
    return pl.CostEstimate(
        flops=16 * 20 * 2 * 128**3, bytes_accessed=5 * 2**20, transcendentals=10**6
    )


def send_maps(meta, *ins):
    return pl.pallas_call(
        send_kernel,
        in_specs=[smem_spec()] + [whole_spec()] * len(ins),
        out_specs=[whole_spec()] * 6,
        out_shape=map_shapes() + ready_shapes(),
        scratch_shapes=[
            pltpu.VMEM((8 + TOK, 1536), F32),
            pltpu.VMEM((2, HEADS, TOK, 256), BF16),
            pltpu.VMEM((2, HEADS, TOK, 256), BF16),
            pltpu.VMEM((HEADS, TOK, TOK), BF16),
        ],
        compiler_params=params(),
        cost_estimate=map_cost(),
        name="send_maps",
    )(meta, *ins)


def keep_maps(meta, *ins):
    return pl.pallas_call(
        keep_kernel,
        in_specs=[smem_spec()] + [whole_spec()] * len(ins),
        out_specs=[whole_spec()] * 3,
        out_shape=map_shapes(),
        scratch_shapes=[
            pltpu.VMEM((8 + TOK, 1536), F32),
            pltpu.VMEM((HEADS, TOK, 256), BF16),
            pltpu.VMEM((HEADS, TOK, 256), BF16),
            pltpu.VMEM((HEADS, TOK, TOK), BF16),
        ],
        compiler_params=params(),
        cost_estimate=map_cost(),
        name="keep_maps",
    )(meta, *ins)


def read_kernel(meta, xq_ref, hq_ref, wq_ref, rows_ref, kt_ref, ef_ref, left_ref, r_ref, d_ref, xs):
    first = meta[2] == 0
    tail = left_ref[0, GROUP * DK : ROWS, :]
    rows = rows_ref[0]
    cols = jnp.transpose(rows)
    usable = [column(cols, 8 + j) for j in range(KW - 1)]
    living = column(cols, 12)
    hidden = hidden_where(rows, cols)
    place_window(xq_ref[...], hq_ref[...], xs, 0)
    taps = wq_ref[...].astype(F32)
    for a in range(2):
        queries = convolve_piece(xs, a * DK, taps[:, a * DK : (a + 1) * DK], usable)
        q = queries.astype(F32)
        scale = unit(q, DK ** (-0.5))
        inner = dot(queries, kt_ref[0, a * DK : (a + 1) * DK, :])
        for b in range(2):
            h = 2 * a + b
            clock = column(cols, h)
            scores = (inner * decay_within(rows, clock, h, hidden)).astype(BF16)
            both = dot(scores, ef_ref[0, h * TOK : (h + 1) * TOK, :])
            carried = jnp.exp2(clock) * living
            mine = slice(h * TOK, (h + 1) * TOK)
            reader = (carried * q - both[:, :DK]) * scale
            direct = both[:, DK:] * scale
            moved = dot(reader.astype(BF16), left_ref[0, h * DK : (h + 1) * DK, :])
            c = factor(tail, h)[:, :DK]
            r_ref[0, mine, :] = jnp.where(first, reader, c * reader - moved[:, :DK]).astype(BF16)
            d_ref[0, mine, :] = jnp.where(first, direct, direct + moved[:, DK:])


def make_reads(meta, slot, projected, halo, conv_weight, tables, keys_t, ef, left):
    def at(i, m):
        return (0, m[slot] + i)

    return pl.pallas_call(
        read_kernel,
        grid_spec=pltpu.PrefetchScalarGridSpec(
            num_scalar_prefetch=1,
            grid=(4,),
            in_specs=[
                pl.BlockSpec((TOK, 256), at),
                pl.BlockSpec((KW - 1, 256), at),
                pl.BlockSpec((KW, 256), at),
                pl.BlockSpec((1, 16, TOK), lambda i, m: (m[slot] + i, 0, 0)),
                pl.BlockSpec((1, 2 * DK, TOK), lambda i, m: (i, 0, 0)),
                pl.BlockSpec((1, GROUP * TOK, 256), lambda i, m: (i, 0, 0)),
                pl.BlockSpec((1, ROWS, 256), lambda i, m: (i, 0, 0)),
            ],
            out_specs=[
                pl.BlockSpec((1, GROUP * TOK, DK), lambda i, m: (i, 0, 0)),
                pl.BlockSpec((1, GROUP * TOK, DV), lambda i, m: (i, 0, 0)),
            ],
            scratch_shapes=[pltpu.VMEM((8 + TOK, 256), F32)],
        ),
        out_shape=[
            jax.ShapeDtypeStruct((4, GROUP * TOK, DK), BF16),
            jax.ShapeDtypeStruct((4, GROUP * TOK, DV), F32),
        ],
        compiler_params=params(),
        cost_estimate=pl.CostEstimate(
            flops=16 * 6 * 2 * 128**3, bytes_accessed=5 * 2**20, transcendentals=10**6
        ),
        name="reads",
    )(meta, projected, halo, conv_weight, tables, keys_t, ef, left)


def factor(tail, head):
    tail = tail.astype(F32)
    return (tail[head : head + 1] + tail[4 + head : 5 + head]) + tail[8 + head : 9 + head]


def compose(left, left_c, right, right_c):
    right_d = right[:, :DK]
    product = dot(right_d.astype(BF16), left.astype(BF16))
    return (
        right_c * left.astype(F32)
        + jnp.concatenate(
            [left_c[:, :DK] * right_d.astype(F32), right[:, DK:].astype(F32)], axis=1
        )
        - product
    )


def apply_map(each, c, state):
    product = dot(each[:, :DK], state)
    return c[:, :DK] * state.astype(F32) + each[:, DK:].astype(F32) - product


def pair_kernel(meta, mine_ref, other_ref, *out_refs):
    first = meta[2] == 0
    for m, out_ref in enumerate(out_refs):
        g = meta[3] ^ m
        tail_m, tail_o = mine_ref[g, GROUP * DK : ROWS, :], other_ref[g, GROUP * DK : ROWS, :]
        tail_l, tail_r = jnp.where(first, tail_m, tail_o), jnp.where(first, tail_o, tail_m)
        factors = []
        for h in range(GROUP):
            here = slice(h * DK, (h + 1) * DK)
            own, other = mine_ref[g, here, :], other_ref[g, here, :]
            left, right = jnp.where(first, own, other), jnp.where(first, other, own)
            left_c, right_c = factor(tail_l, h), factor(tail_r, h)
            out_ref[here, :] = compose(left, left_c, right, right_c).astype(BF16)
            factors.append(left_c * right_c)
        out_ref[GROUP * DK : ROWS, :] = split_rows(factors)


def pair_maps(meta, mine, other):
    return pl.pallas_call(
        pair_kernel,
        in_specs=[smem_spec(), whole_spec(), whole_spec()],
        out_specs=[whole_spec()] * 4,
        out_shape=[jax.ShapeDtypeStruct((ROWS, 256), BF16)] * 4,
        compiler_params=params(),
        cost_estimate=pl.CostEstimate(
            flops=16 * 2 * 2 * 128**3, bytes_accessed=3 * 2**20, transcendentals=0
        ),
        name="pair",
    )(meta, mine, other)


def plane_kernel(meta, x0, x1, x2, x3, prefix_ref, plane_ref, exit_ref, maps, sems):
    copies = []
    for m, x in enumerate((x0, x1, x2, x3)):
        copy = pltpu.make_async_copy(x, maps.at[meta[3] ^ m], sems.at[m])
        copy.start()
        copies.append(copy)
    prefix_ref[0, 0 : GROUP * DK, :] = jnp.zeros((GROUP * DK, 256), BF16)
    ones = jnp.ones((1, 256), F32)
    prefix_ref[0, GROUP * DK : ROWS, :] = split_rows([ones] * GROUP)
    for copy in copies:
        copy.wait()
    prefix_ref[1] = maps[0]
    run = [maps[0, h * DK : (h + 1) * DK, :].astype(F32) for h in range(GROUP)]
    run_c = [factor(maps[0, GROUP * DK : ROWS, :], h) for h in range(GROUP)]
    for a in range(1, 4):
        tail = maps[a, GROUP * DK : ROWS, :]
        for h in range(GROUP):
            here = slice(h * DK, (h + 1) * DK)
            c = factor(tail, h)
            run[h] = compose(run[h], run_c[h], maps[a, here, :], c)
            run_c[h] = run_c[h] * c
            if a < 3:
                prefix_ref[a + 1, here, :] = run[h].astype(BF16)
            else:
                plane_ref[here, :] = run[h].astype(BF16)
                exit_ref[here, :] = run[h][:, DK:].astype(BF16)
        if a < 3:
            prefix_ref[a + 1, GROUP * DK : ROWS, :] = split_rows(run_c)
    plane_ref[GROUP * DK : ROWS, :] = split_rows(run_c)


def plane_maps(meta, pieces):
    return pl.pallas_call(
        plane_kernel,
        in_specs=[smem_spec()] + [pl.BlockSpec(memory_space=pl.ANY)] * 4,
        out_specs=[whole_spec()] * 3,
        out_shape=[
            jax.ShapeDtypeStruct((4, ROWS, 256), BF16),
            jax.ShapeDtypeStruct((ROWS, 256), BF16),
            jax.ShapeDtypeStruct((GROUP * DK, DV), BF16),
        ],
        scratch_shapes=[pltpu.VMEM((4, ROWS, 256), BF16), pltpu.SemaphoreType.DMA((4,))],
        compiler_params=params(),
        cost_estimate=pl.CostEstimate(
            flops=12 * 2 * 2 * 128**3, bytes_accessed=2 * 2**20, transcendentals=0
        ),
        name="plane",
    )(meta, *pieces)


def hop_kernel(plane_ref, state_ref, out_ref):
    tail = plane_ref[GROUP * DK : ROWS, :]
    for h in range(GROUP):
        here = slice(h * DK, (h + 1) * DK)
        out_ref[here, :] = apply_map(plane_ref[here, :], factor(tail, h), state_ref[here, :]).astype(
            BF16
        )


def hop(plane_map, state):
    return pl.pallas_call(
        hop_kernel,
        in_specs=[whole_spec()] * 2,
        out_specs=whole_spec(),
        out_shape=jax.ShapeDtypeStruct((GROUP * DK, DV), BF16),
        compiler_params=params(),
        cost_estimate=pl.CostEstimate(
            flops=4 * 2 * 128**3, bytes_accessed=2**19, transcendentals=0
        ),
        name="hop",
    )(plane_map, state)


def spread_kernel(meta, prefix_ref, *refs):
    out_refs = refs[-4:]
    state_refs = refs[:-4]
    for h in range(GROUP):
        here = slice(h * DK, (h + 1) * DK)
        state = state_refs[0][here, :].astype(F32)
        for ref in state_refs[1:]:
            state = state + ref[here, :].astype(F32)
        state = state.astype(BF16)
        for m, out_ref in enumerate(out_refs):
            a = meta[3] ^ m
            c = factor(prefix_ref[a, GROUP * DK : ROWS, :], h)
            out_ref[here, :] = apply_map(prefix_ref[a, here, :], c, state).astype(BF16)


def spread(meta, prefix, states):
    return pl.pallas_call(
        spread_kernel,
        in_specs=[smem_spec()] + [whole_spec()] * (1 + len(states)),
        out_specs=[whole_spec()] * 4,
        out_shape=[jax.ShapeDtypeStruct((GROUP * DK, DV), BF16)] * 4,
        compiler_params=params(),
        cost_estimate=pl.CostEstimate(
            flops=16 * 2 * 128**3, bytes_accessed=2**21, transcendentals=0
        ),
        name="spread",
    )(meta, prefix, *states)


def emit_kernel(slot, meta, r_ref, d_ref, e0, e1, e2, e3, *refs):
    out_ref, rows, sems = refs[-3:]
    copies = []
    for m, e_ref in enumerate((e0, e1, e2, e3)):
        g = meta[3] ^ m
        for h in range(GROUP):
            here = slice(h * TOK, (h + 1) * TOK)
            total = dot(r_ref[g, here, :], e_ref[here, :]) + d_ref[g, here, :]
            rows[m, :, h * DV : (h + 1) * DV] = total.astype(BF16)
        start = pl.multiple_of((meta[slot] + g) * (GROUP * DV), GROUP * DV)
        copy = pltpu.make_async_copy(
            rows.at[m], out_ref.at[:, pl.ds(start, GROUP * DV)], sems.at[m]
        )
        copy.start()
        copies.append(copy)
    for copy in copies:
        copy.wait()


def emit(meta, slot, reads, direct, states, into=None):
    in_specs = [smem_spec()] + [whole_spec()] * 6
    args = [meta, reads, direct, *states]
    aliases = {}
    if into is not None:
        in_specs.append(pl.BlockSpec(memory_space=pl.ANY))
        args.append(into)
        aliases = {7: 0}
    return pl.pallas_call(
        functools.partial(emit_kernel, slot),
        in_specs=in_specs,
        out_specs=pl.BlockSpec(memory_space=pl.ANY),
        out_shape=jax.ShapeDtypeStruct((TOK, HV * DV), BF16),
        scratch_shapes=[pltpu.VMEM((4, TOK, GROUP * DV), BF16), pltpu.SemaphoreType.DMA((4,))],
        input_output_aliases=aliases,
        compiler_params=params(),
        cost_estimate=pl.CostEstimate(
            flops=16 * 2 * 128**3, bytes_accessed=3 * 2**20, transcendentals=0
        ),
        name="emit",
    )(*args)


def shards(projected, conv_weight, decay_log, write_strength, starts):
    count = lax.axis_size("seq")
    me = lax.axis_index("seq")
    core, place = me & 1, (me >> 1) & 3
    slots = lax.iota(jnp.int32, 4)
    meta = jnp.where(
        slots == 0,
        4 * (1 - core),
        jnp.where(slots == 1, 4 * core, jnp.where(slots == 2, core, place)),
    ).astype(jnp.int32)

    def exchange(block, bits):
        return lax.ppermute(block, "seq", [(i, i ^ bits) for i in range(count)])

    tables, tail_rows = prologue(decay_log, write_strength, starts, projected)
    halo = lax.ppermute(tail_rows, "seq", [(i, i + 1) for i in range(count - 1)])
    projected, conv_weight, masks, shared = stage(tables, projected, conv_weight)
    ins = (projected, halo, conv_weight, tables, masks, shared)

    pay_s, kt_s, ef_s, *ready = send_maps(meta, *ins)
    other = exchange(pay_s, 1)
    mine, kt_k, ef_k = keep_maps(meta, *ins, *ready)
    x0, x1, x2, x3 = pair_maps(meta, mine, other)
    x3, x1, x2 = exchange(x3, 6), exchange(x1, 2), exchange(x2, 4)
    x0, own = lax.optimization_barrier((x0, mine))
    left = lax.ppermute(own, "seq", [(i, i + 1) for i in range(0, count, 2)])
    r_k, d_k = make_reads(meta, 1, projected, halo, conv_weight, tables, kt_k, ef_k, other)
    r_s, d_s = make_reads(meta, 0, projected, halo, conv_weight, tables, kt_s, ef_s, left)
    x0, r_k, d_k, r_s, d_s = lax.optimization_barrier((x0, r_k, d_k, r_s, d_s))
    prefix, plane_map, leaving = plane_maps(meta, (x0, x1, x2, x3))
    planes = count // 8
    received = []
    for step in range(planes - 1):
        route = [(i, i + 8) for i in range(8 * step, 8 * step + 8)]
        state = lax.ppermute(leaving, "seq", route)
        received.append(state)
        if step < planes - 2:
            leaving = hop(plane_map, state)
    if not received:
        received.append(jnp.zeros_like(leaving))
    e0, e1, e2, e3 = spread(meta, prefix, received)
    e3, e1, e2 = exchange(e3, 6), exchange(e1, 2), exchange(e2, 4)
    states = (e0, e1, e2, e3)
    partner = [exchange(e, 1) for e in states]
    out = emit(meta, 1, r_k, d_k, states)
    return emit(meta, 0, r_s, d_s, partner, into=out)


def solution(mesh):
    in_specs = (
        P(("groups", "seq"), None),
        P(),
        P(None, ("groups", "seq")),
        P(None, ("groups", "seq")),
        P(("groups", "seq")),
    )
    out_specs = P(("groups", "seq"), None)
    return jax.shard_map(shards, mesh=mesh, in_specs=in_specs, out_specs=out_specs, check_vma=False)
```

```python
import functools

import jax
import jax.numpy as jnp
from jax import lax
from jax.experimental import pallas as pl
from jax.experimental.pallas import tpu as pltpu
from jax.sharding import PartitionSpec as P


HK = 16
DK = 128
HV = 32
DV = 128
KW = 4
TOK = 128
NORM_EPS = 1e-06
GROUP = 4
LOG2E = 1.4426950408889634
HIDDEN = -1e30
ROWS = GROUP * DK + 16
F32 = jnp.float32
BF16 = jnp.bfloat16


def dot(a, b):
    return jnp.dot(a, b, preferred_element_type=F32)


def halves(a):
    high = a.astype(BF16)
    return high, (a - high.astype(F32)).astype(BF16)


def params(**kw):
    return pltpu.CompilerParams(vmem_limit_bytes=20 << 20, **kw)


def whole_spec():
    return pl.BlockSpec(memory_space=pltpu.VMEM)


def smem_spec():
    return pl.BlockSpec(memory_space=pltpu.SMEM)


def in_hbm(x):
    return pltpu.with_memory_space_constraint(x, pltpu.HBM)


def prologue_kernel(decay_ref, beta_ref, starts_ref, x_ref, out_ref, tail_ref):
    rows = x_ref.shape[0]
    flags = starts_ref[...].astype(F32)
    last = 1.0 - flags[:, TOK - 1 : TOK]
    keep = [last * (1.0 - flags[:, TOK - 2 : TOK - 1]), last, jnp.ones((1, 1), F32)]
    for r in range(KW - 1):
        row = x_ref[rows - KW + 1 + r : rows - KW + 2 + r, :].astype(F32)
        tail_ref[r : r + 1, :] = (row * keep[r]).astype(BF16)
    src = lax.broadcasted_iota(jnp.int32, (TOK, TOK), 0)
    dst = lax.broadcasted_iota(jnp.int32, (TOK, TOK), 1)
    upto = (src <= dst).astype(F32)
    cum = LOG2E * jnp.dot(
        decay_ref[...], upto, precision=lax.Precision.HIGHEST, preferred_element_type=F32
    )
    flags = jnp.broadcast_to(flags, (8, TOK)).astype(BF16)
    episode = [dot(flags, (src + j <= dst).astype(BF16))[0:1] for j in range(KW)]
    usable = [(episode[0] == episode[j]).astype(F32) for j in range(1, KW)]
    living = (episode[0] == 0.0).astype(F32)
    zero = jnp.zeros((1, TOK), F32)
    shared = jnp.concatenate(usable + [episode[0], living, zero, zero, zero], axis=0)
    for pair in range(HV // GROUP):
        out_ref[pair, 0:4, :] = cum[GROUP * pair : GROUP * (pair + 1)]
        out_ref[pair, 4:8, :] = beta_ref[GROUP * pair : GROUP * (pair + 1), :]
        out_ref[pair, 8:16, :] = shared


def prologue(decay_log, write_strength, starts, projected):
    channels = projected.shape[1]
    last = projected.shape[0] // 16 - 1
    return pl.pallas_call(
        prologue_kernel,
        grid=(1,),
        in_specs=[
            pl.BlockSpec((HV, TOK), lambda i: (0, 0)),
            pl.BlockSpec((HV, TOK), lambda i: (0, 0)),
            pl.BlockSpec((1, TOK), lambda i: (0, 0)),
            pl.BlockSpec((16, channels), lambda i: (last, 0)),
        ],
        out_specs=[
            pl.BlockSpec((HV // GROUP, 16, TOK), lambda i: (0, 0, 0)),
            pl.BlockSpec((KW - 1, channels), lambda i: (0, 0)),
        ],
        out_shape=[
            jax.ShapeDtypeStruct((HV // GROUP, 16, TOK), F32),
            jax.ShapeDtypeStruct((KW - 1, channels), BF16),
        ],
        compiler_params=params(),
        cost_estimate=pl.CostEstimate(flops=10**7, bytes_accessed=10**6, transcendentals=0),
        name="prologue",
    )(
        in_hbm(decay_log),
        in_hbm(write_strength),
        in_hbm(starts.reshape(1, TOK)),
        in_hbm(projected),
    )


def place_window(x, halo, xs, first):
    cols = slice(first, first + x.shape[1])
    xs[8 : 8 + TOK, cols] = x.astype(F32)
    xs[8 - KW + 1 : 8, cols] = halo.astype(F32)


def convolve_piece(xs, first, taps, usable):
    here = slice(first, first + 128)
    total = xs[8 : 8 + TOK, here] * taps[3:4]
    for j in range(1, KW):
        total = total + (xs[8 - j : 8 - j + TOK, here] * usable[j - 1]) * taps[3 - j : 4 - j]
    return (total / (1.0 + jnp.exp2(total * -LOG2E))).astype(BF16)


def column(cols, lane):
    return jnp.broadcast_to(cols[:, lane : lane + 1], (TOK, 128))


def positions():
    i = lax.broadcasted_iota(jnp.int32, (TOK, TOK), 0)
    j = lax.broadcasted_iota(jnp.int32, (TOK, TOK), 1)
    return i, j


def hidden_where(rows, cols):
    i, j = positions()
    seen = (column(cols, 11) == rows[11:12, :]) & (i >= j)
    return jnp.where(seen, 0.0, HIDDEN)


def decay_within(rows, clock, head, hidden):
    return jnp.exp2((clock - rows[head : head + 1, :]) + hidden)


def unit(x, scale=1.0):
    return lax.rsqrt(jnp.sum(x * x, axis=-1, keepdims=True) + NORM_EPS) * scale


def split_rows(x):
    pieces, rest = [], list(x)
    for _ in range(3):
        highs = [c.astype(BF16).astype(F32) for c in rest]
        pieces += highs
        rest = [c - high for c, high in zip(rest, highs)]
    pieces.append(jnp.zeros((4, 256), F32))
    return jnp.concatenate(pieces, axis=0).astype(BF16)


LEVELS = 7
HEADS = 8


def odd_rows(get, size):
    return jnp.concatenate([get(r, r + size) for r in range(size, TOK, 2 * size)], axis=0)


def stage_kernel(tab_ref, x_hbm, w_hbm, x_out, w_out, masks, shared, sems):
    copies = [
        pltpu.make_async_copy(x_hbm, x_out, sems.at[0]),
        pltpu.make_async_copy(w_hbm, w_out, sems.at[1]),
    ]
    for copy in copies:
        copy.start()
    rows = tab_ref[0]
    cols = jnp.transpose(rows)
    for j in range(KW - 1):
        shared[j] = column(cols, 8 + j)
    shared[3] = column(cols, 12)
    shared[4] = hidden_where(rows, cols)
    i, j = positions()
    apart = i ^ j
    for level in range(LEVELS):
        masks[level] = (((apart >> level) == 1) & (i > j)).astype(F32).astype(BF16)
    shared[5] = (i > j).astype(F32)
    masks[LEVELS] = (i == j).astype(F32).astype(BF16)
    for copy in copies:
        copy.wait()


def stage(tables, projected, conv_weight):
    return pl.pallas_call(
        stage_kernel,
        in_specs=[whole_spec()] + [pl.BlockSpec(memory_space=pl.ANY)] * 2,
        out_specs=[whole_spec()] * 4,
        out_shape=[
            jax.ShapeDtypeStruct(projected.shape, BF16),
            jax.ShapeDtypeStruct(conv_weight.shape, BF16),
            jax.ShapeDtypeStruct((LEVELS + 1, TOK, TOK), BF16),
            jax.ShapeDtypeStruct((6, TOK, 128), F32),
        ],
        scratch_shapes=[pltpu.SemaphoreType.DMA((2,))],
        compiler_params=params(),
        cost_estimate=pl.CostEstimate(flops=10**6, bytes_accessed=4 * 2**20, transcendentals=0),
        name="stage",
    )(tables, in_hbm(projected), in_hbm(conv_weight))


def preparing(pair, ins, xs, sys, right, keys):
    x_ref, halo_ref, w_ref, tab_ref, _, shared = ins
    k_at = pl.multiple_of(HK * DK + pair * 256, 512)
    v_at = pl.multiple_of(2 * HK * DK + pair * 512, 1024)
    kt_ref, kt_at = keys

    def usable():
        return [shared[j] for j in range(KW - 1)]

    def place():
        place_window(x_ref[:, pl.ds(k_at, 512)], halo_ref[:, pl.ds(k_at, 512)], xs, 0)
        place_window(x_ref[:, pl.ds(v_at, 1024)], halo_ref[:, pl.ds(v_at, 1024)], xs, 512)

    def key(n):
        p, a = n // 2, n % 2
        rows = tab_ref[pair + p]
        cols = jnp.transpose(rows)
        at = n * DK
        taps = w_ref[:, pl.ds(k_at + at, DK)].astype(F32)
        k = convolve_piece(xs, at, taps, usable()).astype(F32)
        k = k * unit(k)
        kb = k.astype(BF16)
        ktb = jnp.transpose(kb.astype(F32)).astype(BF16)
        kt_ref[kt_at + p, a * DK : (a + 1) * DK, :] = ktb
        inner = dot(kb, ktb) * shared[5]
        for b in range(2):
            lane = 2 * a + b
            h = GROUP * p + lane
            clock = column(cols, lane)
            within = decay_within(rows, clock, lane, shared[4])
            carried = jnp.exp2(clock) * shared[3]
            high, low = halves((column(cols, 4 + lane) * within) * inner)
            sys[h, :, 0:128] = high
            sys[h, :, 128:256] = low
            right[h, :, 0:DK] = (carried * k).astype(BF16)

    def value(h):
        taps = w_ref[:, pl.ds(v_at + h * DV, DV)].astype(F32)
        right[h, :, DK : DK + DV] = convolve_piece(xs, 512 + h * DV, taps, usable())

    steps = [place]
    steps += [functools.partial(key, n) for n in range(4)]
    steps += [functools.partial(value, h) for h in range(HEADS)]
    return steps


def solving(pair, ins, sys, right, keys, inv, pay_ref, ef_ref, at, kt_copy=None):
    tab_ref, masks, shared = ins[3:]
    kt_ref, kt_at = keys
    kept = {}

    def begin():
        for h in range(HEADS):
            inv[h] = masks[LEVELS] - sys[h, :, 0:128] * masks[0]

    def first_product(level):
        size = 1 << level
        kept["steps"] = []
        for h in range(HEADS):
            if size < 16:
                left = sys[h, :, 0:128]
            else:
                left = odd_rows(lambda r, e: sys[h, r:e, 0:128], size)
            kept["steps"].append(dot(left, inv[h]).astype(BF16))

    def second_product(level):
        size = 1 << level
        steps = kept["steps"]
        if size < 16:
            steps = [dot(inv[h], steps[h]).astype(BF16) for h in range(HEADS)]
            for h in range(HEADS):
                inv[h] = inv[h] - steps[h] * masks[level]
            return
        blank = jnp.zeros((size, 128), BF16)
        found = []
        for h in range(HEADS):
            expanded = []
            for r in range(0, TOK // 2, size):
                expanded += [blank, steps[h][r : r + size]]
            left = odd_rows(lambda r, e: inv[h, r:e, :], size)
            found.append(dot(left, jnp.concatenate(expanded, axis=0)).astype(BF16))
        for h in range(HEADS):
            for n, r in enumerate(range(size, TOK, 2 * size)):
                inv[h, r : r + size, :] = inv[h, r : r + size, :] - (
                    found[h][n * size : (n + 1) * size] * masks[level, r : r + size, :]
                )

    def check():
        kept["gaps"] = []
        for h in range(HEADS):
            rough = inv[h]
            product = dot(sys[h], jnp.concatenate([rough, rough], axis=0))
            kept["gaps"].append(
                ((masks[LEVELS].astype(F32) - rough.astype(F32)) - product).astype(BF16)
            )

    def row(h, n):
        return tab_ref[pair + h // GROUP, n : n + 1, :]

    def correct():
        for h in range(HEADS):
            fixed = inv[h].astype(F32) + dot(inv[h], kept["gaps"][h])
            inv[h] = (fixed * row(h, 4 + h % GROUP)).astype(BF16)

    def apply():
        kept["ef"] = []
        for h in range(HEADS):
            ef = dot(inv[h], right[h]).astype(BF16)
            here = slice((h % GROUP) * TOK, (h % GROUP + 1) * TOK)
            ef_ref[at + h // GROUP, here, :] = ef
            kept["ef"].append(ef)

    def write():
        last = []
        for h in range(HEADS):
            g, n = h // GROUP, h % GROUP
            ktb = kt_ref[kt_at + g, (n // 2) * DK : (n // 2 + 1) * DK, :]
            if kt_copy is not None and n % 2 == 0:
                kt_copy[at + g, (n // 2) * DK : (n // 2 + 1) * DK, :] = ktb
            clock = row(h, n)
            final = jnp.broadcast_to(clock[:, TOK - 1 : TOK], (1, TOK))
            ending = jnp.exp2((final - clock) + shared[4, TOK - 1 : TOK, :])
            carried = jnp.exp2(final) * shared[3, TOK - 1 : TOK, :]
            last.append(jnp.concatenate([carried, carried], axis=1))
            weighted = (ktb.astype(F32) * ending).astype(BF16)
            pay_ref[at + g, n * DK : (n + 1) * DK, :] = dot(weighted, kept["ef"][h]).astype(BF16)
        for g in range(2):
            pay_ref[at + g, GROUP * DK : ROWS, :] = split_rows(last[GROUP * g : GROUP * (g + 1)])

    steps = [begin]
    for level in range(1, LEVELS):
        steps.append(functools.partial(first_product, level))
        steps.append(functools.partial(second_product, level))
    return steps + [check, correct, apply, write]


def interleave(main, side):
    done = 0
    for n, step in enumerate(main):
        step()
        due = ((n + 1) * len(side) + len(main) - 1) // len(main)
        while done < min(due, len(side)):
            side[done]()
            done += 1


def send_kernel(
    meta, x_ref, halo_ref, w_ref, tab_ref, masks, shared, pay_ref, kt_ref, ef_ref, sys_out,
    right_out, kt_out, xs, sys, right, inv,
):
    ins = (x_ref, halo_ref, w_ref, tab_ref, masks, shared)
    pair, after = meta[0], meta[1]
    sets = [(sys.at[n], right.at[n], (kt_ref, 2 * n)) for n in range(2)]
    third = (sys_out, right_out, (kt_out, 0))
    for step in preparing(pair, ins, xs, *sets[0]):
        step()
    for n in range(2):
        main = solving(pair + 2 * n, ins, *sets[n], inv, pay_ref, ef_ref, 2 * n)
        if n == 0:
            side = preparing(pair + 2, ins, xs, *sets[1])
        else:
            side = preparing(after, ins, xs, *third)
        interleave(main, side)


def keep_kernel(
    meta, x_ref, halo_ref, w_ref, tab_ref, masks, shared, sys_in, right_in, kt_in, pay_ref,
    kt_ref, ef_ref, xs, sys, right, inv,
):
    ins = (x_ref, halo_ref, w_ref, tab_ref, masks, shared)
    pair = meta[1]
    own = (sys, right, (kt_ref, 2))
    interleave(
        solving(pair, ins, sys_in, right_in, (kt_in, 0), inv, pay_ref, ef_ref, 0, kt_ref),
        preparing(pair + 2, ins, xs, *own),
    )
    for step in solving(pair + 2, ins, *own, inv, pay_ref, ef_ref, 2):
        step()


def map_shapes():
    return [
        jax.ShapeDtypeStruct((4, ROWS, 256), BF16),
        jax.ShapeDtypeStruct((4, 2 * DK, TOK), BF16),
        jax.ShapeDtypeStruct((4, GROUP * TOK, 256), BF16),
    ]


def ready_shapes():
    return [
        jax.ShapeDtypeStruct((HEADS, TOK, 256), BF16),
        jax.ShapeDtypeStruct((HEADS, TOK, 256), BF16),
        jax.ShapeDtypeStruct((2, 2 * DK, TOK), BF16),
    ]


def map_cost():
    return pl.CostEstimate(
        flops=16 * 20 * 2 * 128**3, bytes_accessed=5 * 2**20, transcendentals=10**6
    )


def send_maps(meta, *ins):
    return pl.pallas_call(
        send_kernel,
        in_specs=[smem_spec()] + [whole_spec()] * len(ins),
        out_specs=[whole_spec()] * 6,
        out_shape=map_shapes() + ready_shapes(),
        scratch_shapes=[
            pltpu.VMEM((8 + TOK, 1536), F32),
            pltpu.VMEM((2, HEADS, TOK, 256), BF16),
            pltpu.VMEM((2, HEADS, TOK, 256), BF16),
            pltpu.VMEM((HEADS, TOK, TOK), BF16),
        ],
        compiler_params=params(),
        cost_estimate=map_cost(),
        name="send_maps",
    )(meta, *ins)


def keep_maps(meta, *ins):
    return pl.pallas_call(
        keep_kernel,
        in_specs=[smem_spec()] + [whole_spec()] * len(ins),
        out_specs=[whole_spec()] * 3,
        out_shape=map_shapes(),
        scratch_shapes=[
            pltpu.VMEM((8 + TOK, 1536), F32),
            pltpu.VMEM((HEADS, TOK, 256), BF16),
            pltpu.VMEM((HEADS, TOK, 256), BF16),
            pltpu.VMEM((HEADS, TOK, TOK), BF16),
        ],
        compiler_params=params(),
        cost_estimate=map_cost(),
        name="keep_maps",
    )(meta, *ins)


def read_kernel(meta, xq_ref, hq_ref, wq_ref, rows_ref, kt_ref, ef_ref, left_ref, r_ref, d_ref, xs):
    first = meta[2] == 0
    tail = left_ref[0, GROUP * DK : ROWS, :]
    rows = rows_ref[0]
    cols = jnp.transpose(rows)
    usable = [column(cols, 8 + j) for j in range(KW - 1)]
    living = column(cols, 12)
    hidden = hidden_where(rows, cols)
    place_window(xq_ref[...], hq_ref[...], xs, 0)
    taps = wq_ref[...].astype(F32)
    for a in range(2):
        queries = convolve_piece(xs, a * DK, taps[:, a * DK : (a + 1) * DK], usable)
        q = queries.astype(F32)
        scale = unit(q, DK ** (-0.5))
        inner = dot(queries, kt_ref[0, a * DK : (a + 1) * DK, :])
        for b in range(2):
            h = 2 * a + b
            clock = column(cols, h)
            scores = (inner * decay_within(rows, clock, h, hidden)).astype(BF16)
            both = dot(scores, ef_ref[0, h * TOK : (h + 1) * TOK, :])
            carried = jnp.exp2(clock) * living
            mine = slice(h * TOK, (h + 1) * TOK)
            reader = (carried * q - both[:, :DK]) * scale
            direct = both[:, DK:] * scale
            moved = dot(reader.astype(BF16), left_ref[0, h * DK : (h + 1) * DK, :])
            c = factor(tail, h)[:, :DK]
            r_ref[0, mine, :] = jnp.where(first, reader, c * reader - moved[:, :DK]).astype(BF16)
            d_ref[0, mine, :] = jnp.where(first, direct, direct + moved[:, DK:])


def make_reads(meta, slot, projected, halo, conv_weight, tables, keys_t, ef, left):
    def at(i, m):
        return (0, m[slot] + i)

    return pl.pallas_call(
        read_kernel,
        grid_spec=pltpu.PrefetchScalarGridSpec(
            num_scalar_prefetch=1,
            grid=(4,),
            in_specs=[
                pl.BlockSpec((TOK, 256), at),
                pl.BlockSpec((KW - 1, 256), at),
                pl.BlockSpec((KW, 256), at),
                pl.BlockSpec((1, 16, TOK), lambda i, m: (m[slot] + i, 0, 0)),
                pl.BlockSpec((1, 2 * DK, TOK), lambda i, m: (i, 0, 0)),
                pl.BlockSpec((1, GROUP * TOK, 256), lambda i, m: (i, 0, 0)),
                pl.BlockSpec((1, ROWS, 256), lambda i, m: (i, 0, 0)),
            ],
            out_specs=[
                pl.BlockSpec((1, GROUP * TOK, DK), lambda i, m: (i, 0, 0)),
                pl.BlockSpec((1, GROUP * TOK, DV), lambda i, m: (i, 0, 0)),
            ],
            scratch_shapes=[pltpu.VMEM((8 + TOK, 256), F32)],
        ),
        out_shape=[
            jax.ShapeDtypeStruct((4, GROUP * TOK, DK), BF16),
            jax.ShapeDtypeStruct((4, GROUP * TOK, DV), F32),
        ],
        compiler_params=params(),
        cost_estimate=pl.CostEstimate(
            flops=16 * 6 * 2 * 128**3, bytes_accessed=5 * 2**20, transcendentals=10**6
        ),
        name="reads",
    )(meta, projected, halo, conv_weight, tables, keys_t, ef, left)


def factor(tail, head):
    tail = tail.astype(F32)
    return (tail[head : head + 1] + tail[4 + head : 5 + head]) + tail[8 + head : 9 + head]


def compose(left, left_c, right, right_c):
    right_d = right[:, :DK]
    product = dot(right_d.astype(BF16), left.astype(BF16))
    return (
        right_c * left.astype(F32)
        + jnp.concatenate(
            [left_c[:, :DK] * right_d.astype(F32), right[:, DK:].astype(F32)], axis=1
        )
        - product
    )


def apply_map(each, c, state):
    product = dot(each[:, :DK], state)
    return c[:, :DK] * state.astype(F32) + each[:, DK:].astype(F32) - product


def pair_kernel(meta, mine_ref, other_ref, *out_refs):
    first = meta[2] == 0
    for m, out_ref in enumerate(out_refs):
        g = meta[3] ^ m
        tail_m, tail_o = mine_ref[g, GROUP * DK : ROWS, :], other_ref[g, GROUP * DK : ROWS, :]
        tail_l, tail_r = jnp.where(first, tail_m, tail_o), jnp.where(first, tail_o, tail_m)
        factors = []
        for h in range(GROUP):
            here = slice(h * DK, (h + 1) * DK)
            own, other = mine_ref[g, here, :], other_ref[g, here, :]
            left, right = jnp.where(first, own, other), jnp.where(first, other, own)
            left_c, right_c = factor(tail_l, h), factor(tail_r, h)
            out_ref[here, :] = compose(left, left_c, right, right_c).astype(BF16)
            factors.append(left_c * right_c)
        out_ref[GROUP * DK : ROWS, :] = split_rows(factors)


def pair_maps(meta, mine, other):
    return pl.pallas_call(
        pair_kernel,
        in_specs=[smem_spec(), whole_spec(), whole_spec()],
        out_specs=[whole_spec()] * 4,
        out_shape=[jax.ShapeDtypeStruct((ROWS, 256), BF16)] * 4,
        compiler_params=params(),
        cost_estimate=pl.CostEstimate(
            flops=16 * 2 * 2 * 128**3, bytes_accessed=3 * 2**20, transcendentals=0
        ),
        name="pair",
    )(meta, mine, other)


CHUNK = GROUP // 2


def chunk_rows(h):
    return slice((h % CHUNK) * DK, (h % CHUNK + 1) * DK)


def plane_kernel(meta, x0, x1, x2, x3, prefix_ref, plane_ref, exit_a, exit_b, maps, sems):
    copies = []
    for m, x in enumerate((x0, x1, x2, x3)):
        copy = pltpu.make_async_copy(x, maps.at[meta[3] ^ m], sems.at[m])
        copy.start()
        copies.append(copy)
    prefix_ref[0, 0 : GROUP * DK, :] = jnp.zeros((GROUP * DK, 256), BF16)
    ones = jnp.ones((1, 256), F32)
    prefix_ref[0, GROUP * DK : ROWS, :] = split_rows([ones] * GROUP)
    for copy in copies:
        copy.wait()
    prefix_ref[1] = maps[0]
    run = [maps[0, h * DK : (h + 1) * DK, :].astype(F32) for h in range(GROUP)]
    run_c = [factor(maps[0, GROUP * DK : ROWS, :], h) for h in range(GROUP)]
    for a in range(1, 4):
        tail = maps[a, GROUP * DK : ROWS, :]
        for h in range(GROUP):
            here = slice(h * DK, (h + 1) * DK)
            c = factor(tail, h)
            run[h] = compose(run[h], run_c[h], maps[a, here, :], c)
            run_c[h] = run_c[h] * c
            if a < 3:
                prefix_ref[a + 1, here, :] = run[h].astype(BF16)
            else:
                plane_ref[here, :] = run[h].astype(BF16)
                exit_ref = exit_b if h // CHUNK else exit_a
                exit_ref[chunk_rows(h), :] = run[h][:, DK:].astype(BF16)
        if a < 3:
            prefix_ref[a + 1, GROUP * DK : ROWS, :] = split_rows(run_c)
    plane_ref[GROUP * DK : ROWS, :] = split_rows(run_c)


def plane_maps(meta, pieces):
    return pl.pallas_call(
        plane_kernel,
        in_specs=[smem_spec()] + [pl.BlockSpec(memory_space=pl.ANY)] * 4,
        out_specs=[whole_spec()] * 4,
        out_shape=[
            jax.ShapeDtypeStruct((4, ROWS, 256), BF16),
            jax.ShapeDtypeStruct((ROWS, 256), BF16),
            jax.ShapeDtypeStruct((CHUNK * DK, DV), BF16),
            jax.ShapeDtypeStruct((CHUNK * DK, DV), BF16),
        ],
        scratch_shapes=[pltpu.VMEM((4, ROWS, 256), BF16), pltpu.SemaphoreType.DMA((4,))],
        compiler_params=params(),
        cost_estimate=pl.CostEstimate(
            flops=12 * 2 * 2 * 128**3, bytes_accessed=2 * 2**20, transcendentals=0
        ),
        name="plane",
    )(meta, *pieces)


def hop_kernel(chunk, plane_ref, state_ref, out_ref):
    tail = plane_ref[GROUP * DK : ROWS, :]
    for h in range(chunk * CHUNK, (chunk + 1) * CHUNK):
        each = plane_ref[h * DK : (h + 1) * DK, :]
        out_ref[chunk_rows(h), :] = apply_map(
            each, factor(tail, h), state_ref[chunk_rows(h), :]
        ).astype(BF16)


def hop(chunk, plane_map, state):
    return pl.pallas_call(
        functools.partial(hop_kernel, chunk),
        in_specs=[whole_spec()] * 2,
        out_specs=whole_spec(),
        out_shape=jax.ShapeDtypeStruct((CHUNK * DK, DV), BF16),
        compiler_params=params(),
        cost_estimate=pl.CostEstimate(
            flops=2 * 2 * 128**3, bytes_accessed=2**18, transcendentals=0
        ),
        name="hop",
    )(plane_map, state)


def spread_kernel(meta, prefix_ref, *refs):
    out_refs = refs[-4:]
    state_refs = refs[:-4]
    each = len(state_refs) // 2
    for h in range(GROUP):
        here = slice(h * DK, (h + 1) * DK)
        mine = state_refs[(h // CHUNK) * each : (h // CHUNK + 1) * each]
        state = mine[0][chunk_rows(h), :]
        for ref in mine[1:]:
            state = state + ref[chunk_rows(h), :]
        for m, out_ref in enumerate(out_refs):
            a = meta[3] ^ m
            c = factor(prefix_ref[a, GROUP * DK : ROWS, :], h)
            out_ref[here, :] = apply_map(prefix_ref[a, here, :], c, state).astype(BF16)


def spread(meta, prefix, states):
    return pl.pallas_call(
        spread_kernel,
        in_specs=[smem_spec()] + [whole_spec()] * (1 + len(states)),
        out_specs=[whole_spec()] * 4,
        out_shape=[jax.ShapeDtypeStruct((GROUP * DK, DV), BF16)] * 4,
        compiler_params=params(),
        cost_estimate=pl.CostEstimate(
            flops=16 * 2 * 128**3, bytes_accessed=2**21, transcendentals=0
        ),
        name="spread",
    )(meta, prefix, *states)


def emit_kernel(parts, meta, *refs):
    out_ref, rows, sems = refs[-3:]
    copies = []
    for n, (slot, m) in enumerate(parts):
        r_ref, d_ref, e_ref = refs[3 * n : 3 * n + 3]
        g = meta[3] ^ m
        for h in range(GROUP):
            here = slice(h * TOK, (h + 1) * TOK)
            total = dot(r_ref[g, here, :], e_ref[here, :]) + d_ref[g, here, :]
            rows[n, :, h * DV : (h + 1) * DV] = total.astype(BF16)
        start = pl.multiple_of((meta[slot] + g) * (GROUP * DV), GROUP * DV)
        copy = pltpu.make_async_copy(
            rows.at[n], out_ref.at[:, pl.ds(start, GROUP * DV)], sems.at[n]
        )
        copy.start()
        copies.append(copy)
    for copy in copies:
        copy.wait()


def emit(meta, parts, into=None):
    args = [meta]
    for _, _, reads, direct, state in parts:
        args += [reads, direct, state]
    in_specs = [smem_spec()] + [whole_spec()] * (len(args) - 1)
    aliases = {}
    if into is not None:
        in_specs.append(pl.BlockSpec(memory_space=pl.ANY))
        aliases = {len(args): 0}
        args.append(into)
    return pl.pallas_call(
        functools.partial(emit_kernel, [part[:2] for part in parts]),
        in_specs=in_specs,
        out_specs=pl.BlockSpec(memory_space=pl.ANY),
        out_shape=jax.ShapeDtypeStruct((TOK, HV * DV), BF16),
        scratch_shapes=[
            pltpu.VMEM((len(parts), TOK, GROUP * DV), BF16),
            pltpu.SemaphoreType.DMA((len(parts),)),
        ],
        input_output_aliases=aliases,
        compiler_params=params(),
        cost_estimate=pl.CostEstimate(
            flops=len(parts) * 4 * 2 * 128**3,
            bytes_accessed=len(parts) * 5 * 2**17,
            transcendentals=0,
        ),
        name="emit",
    )(*args)


def shards(projected, conv_weight, decay_log, write_strength, starts):
    count = lax.axis_size("seq")
    me = lax.axis_index("seq")
    core, place = me & 1, (me >> 1) & 3
    slots = lax.iota(jnp.int32, 4)
    meta = jnp.where(
        slots == 0,
        4 * (1 - core),
        jnp.where(slots == 1, 4 * core, jnp.where(slots == 2, core, place)),
    ).astype(jnp.int32)

    def exchange(block, bits):
        return lax.ppermute(block, "seq", [(i, i ^ bits) for i in range(count)])

    tables, tail_rows = prologue(decay_log, write_strength, starts, projected)
    halo = lax.ppermute(tail_rows, "seq", [(i, i + 1) for i in range(count - 1)])
    projected, conv_weight, masks, shared = stage(tables, projected, conv_weight)
    ins = (projected, halo, conv_weight, tables, masks, shared)

    pay_s, kt_s, ef_s, *ready = send_maps(meta, *ins)
    other = exchange(pay_s, 1)
    mine, kt_k, ef_k = keep_maps(meta, *ins, *ready)
    x0, x1, x2, x3 = pair_maps(meta, mine, other)
    x3, x1, x2 = exchange(x3, 6), exchange(x1, 2), exchange(x2, 4)
    x0, own = lax.optimization_barrier((x0, mine))
    left = exchange(own, 1)
    r_k, d_k = make_reads(meta, 1, projected, halo, conv_weight, tables, kt_k, ef_k, other)
    r_s, d_s = make_reads(meta, 0, projected, halo, conv_weight, tables, kt_s, ef_s, left)
    x0, r_k, d_k, r_s, d_s = lax.optimization_barrier((x0, r_k, d_k, r_s, d_s))
    prefix, plane_map, *leaving = plane_maps(meta, (x0, x1, x2, x3))
    planes = count // 8
    received = [[], []]
    for step in range(planes - 1):
        route = [(i, i + 8) for i in range(8 * step, 8 * step + 8)]
        arrived = [lax.ppermute(state, "seq", route) for state in leaving]
        for chunk, state in enumerate(arrived):
            received[chunk].append(state)
            if step < planes - 2:
                leaving[chunk] = hop(chunk, plane_map, state)
    if planes == 1:
        received = [[jnp.zeros_like(state)] for state in leaving]
    e0, e1, e2, e3 = spread(meta, prefix, received[0] + received[1])
    e1 = exchange(e1, 2)
    e2 = exchange(e2, 4)
    e3 = exchange(e3, 6)
    states = (e0, e1, e2, e3)
    partner = [exchange(e, 1) for e in states]
    out = None
    for m in range(3):
        parts = [(1, m, r_k, d_k, states[m]), (0, m, r_s, d_s, partner[m])]
        out = emit(meta, parts, into=out)
    out = emit(meta, [(1, 3, r_k, d_k, states[3])], into=out)
    return emit(meta, [(0, 3, r_s, d_s, partner[3])], into=out)


def solution(mesh):
    in_specs = (
        P(("groups", "seq"), None),
        P(),
        P(None, ("groups", "seq")),
        P(None, ("groups", "seq")),
        P(("groups", "seq")),
    )
    out_specs = P(("groups", "seq"), None)

    return jax.shard_map(shards, mesh=mesh, in_specs=in_specs, out_specs=out_specs, check_vma=False)
```

```python
import functools

import jax
import jax.numpy as jnp
from jax import lax
from jax.experimental import pallas as pl
from jax.experimental.pallas import tpu as pltpu
from jax.sharding import PartitionSpec as P


HK = 16
DK = 128
HV = 32
DV = 128
KW = 4
TOK = 128
NORM_EPS = 1e-06
GROUP = 4
LOG2E = 1.4426950408889634
HIDDEN = -1e30
ROWS = GROUP * DK + 16
F32 = jnp.float32
BF16 = jnp.bfloat16


def dot(a, b):
    return jnp.dot(a, b, preferred_element_type=F32)


def halves(a):
    high = a.astype(BF16)
    return high, (a - high.astype(F32)).astype(BF16)


def params(**kw):
    return pltpu.CompilerParams(vmem_limit_bytes=20 << 20, **kw)


def whole_spec():
    return pl.BlockSpec(memory_space=pltpu.VMEM)


def smem_spec():
    return pl.BlockSpec(memory_space=pltpu.SMEM)


def in_hbm(x):
    return pltpu.with_memory_space_constraint(x, pltpu.HBM)


def prologue_kernel(decay_ref, beta_ref, starts_ref, x_ref, out_ref, tail_ref):
    rows = x_ref.shape[0]
    flags = starts_ref[...].astype(F32)
    last = 1.0 - flags[:, TOK - 1 : TOK]
    keep = [last * (1.0 - flags[:, TOK - 2 : TOK - 1]), last, jnp.ones((1, 1), F32)]
    for r in range(KW - 1):
        row = x_ref[rows - KW + 1 + r : rows - KW + 2 + r, :].astype(F32)
        tail_ref[r : r + 1, :] = (row * keep[r]).astype(BF16)
    src = lax.broadcasted_iota(jnp.int32, (TOK, TOK), 0)
    dst = lax.broadcasted_iota(jnp.int32, (TOK, TOK), 1)
    upto = (src <= dst).astype(F32)
    cum = LOG2E * jnp.dot(
        decay_ref[...], upto, precision=lax.Precision.HIGHEST, preferred_element_type=F32
    )
    flags = jnp.broadcast_to(flags, (8, TOK)).astype(BF16)
    episode = [dot(flags, (src + j <= dst).astype(BF16))[0:1] for j in range(KW)]
    usable = [(episode[0] == episode[j]).astype(F32) for j in range(1, KW)]
    living = (episode[0] == 0.0).astype(F32)
    zero = jnp.zeros((1, TOK), F32)
    shared = jnp.concatenate(usable + [episode[0], living, zero, zero, zero], axis=0)
    for pair in range(HV // GROUP):
        out_ref[pair, 0:4, :] = cum[GROUP * pair : GROUP * (pair + 1)]
        out_ref[pair, 4:8, :] = beta_ref[GROUP * pair : GROUP * (pair + 1), :]
        out_ref[pair, 8:16, :] = shared


def prologue(decay_log, write_strength, starts, projected):
    channels = projected.shape[1]
    last = projected.shape[0] // 16 - 1
    return pl.pallas_call(
        prologue_kernel,
        grid=(1,),
        in_specs=[
            pl.BlockSpec((HV, TOK), lambda i: (0, 0)),
            pl.BlockSpec((HV, TOK), lambda i: (0, 0)),
            pl.BlockSpec((1, TOK), lambda i: (0, 0)),
            pl.BlockSpec((16, channels), lambda i: (last, 0)),
        ],
        out_specs=[
            pl.BlockSpec((HV // GROUP, 16, TOK), lambda i: (0, 0, 0)),
            pl.BlockSpec((KW - 1, channels), lambda i: (0, 0)),
        ],
        out_shape=[
            jax.ShapeDtypeStruct((HV // GROUP, 16, TOK), F32),
            jax.ShapeDtypeStruct((KW - 1, channels), BF16),
        ],
        compiler_params=params(),
        cost_estimate=pl.CostEstimate(flops=10**7, bytes_accessed=10**6, transcendentals=0),
        name="prologue",
    )(
        in_hbm(decay_log),
        in_hbm(write_strength),
        in_hbm(starts.reshape(1, TOK)),
        in_hbm(projected),
    )


def place_window(x, halo, xs, first):
    cols = slice(first, first + x.shape[1])
    xs[8 : 8 + TOK, cols] = x.astype(F32)
    xs[8 - KW + 1 : 8, cols] = halo.astype(F32)


def convolve_piece(xs, first, taps, usable):
    here = slice(first, first + 128)
    total = xs[8 : 8 + TOK, here] * taps[3:4]
    for j in range(1, KW):
        total = total + (xs[8 - j : 8 - j + TOK, here] * usable[j - 1]) * taps[3 - j : 4 - j]
    return (total / (1.0 + jnp.exp2(total * -LOG2E))).astype(BF16)


def column(cols, lane):
    return jnp.broadcast_to(cols[:, lane : lane + 1], (TOK, 128))


def positions():
    i = lax.broadcasted_iota(jnp.int32, (TOK, TOK), 0)
    j = lax.broadcasted_iota(jnp.int32, (TOK, TOK), 1)
    return i, j


def hidden_where(rows, cols):
    i, j = positions()
    seen = (column(cols, 11) == rows[11:12, :]) & (i >= j)
    return jnp.where(seen, 0.0, HIDDEN)


def decay_within(rows, clock, head, hidden):
    return jnp.exp2((clock - rows[head : head + 1, :]) + hidden)


def unit(x, scale=1.0):
    return lax.rsqrt(jnp.sum(x * x, axis=-1, keepdims=True) + NORM_EPS) * scale


def split_rows(x):
    pieces, rest = [], list(x)
    for _ in range(3):
        highs = [c.astype(BF16).astype(F32) for c in rest]
        pieces += highs
        rest = [c - high for c, high in zip(rest, highs)]
    pieces.append(jnp.zeros((4, 256), F32))
    return jnp.concatenate(pieces, axis=0).astype(BF16)


LEVELS = 7
HEADS = 8


def odd_rows(get, size):
    return jnp.concatenate([get(r, r + size) for r in range(size, TOK, 2 * size)], axis=0)


def stage_kernel(tab_ref, x_hbm, w_hbm, x_out, w_out, masks, shared, sems):
    copies = [
        pltpu.make_async_copy(x_hbm, x_out, sems.at[0]),
        pltpu.make_async_copy(w_hbm, w_out, sems.at[1]),
    ]
    for copy in copies:
        copy.start()
    rows = tab_ref[0]
    cols = jnp.transpose(rows)
    for j in range(KW - 1):
        shared[j] = column(cols, 8 + j)
    shared[3] = column(cols, 12)
    shared[4] = hidden_where(rows, cols)
    i, j = positions()
    apart = i ^ j
    for level in range(LEVELS):
        masks[level] = (((apart >> level) == 1) & (i > j)).astype(F32).astype(BF16)
    shared[5] = (i > j).astype(F32)
    masks[LEVELS] = (i == j).astype(F32).astype(BF16)
    for copy in copies:
        copy.wait()


def stage(tables, projected, conv_weight):
    return pl.pallas_call(
        stage_kernel,
        in_specs=[whole_spec()] + [pl.BlockSpec(memory_space=pl.ANY)] * 2,
        out_specs=[whole_spec()] * 4,
        out_shape=[
            jax.ShapeDtypeStruct(projected.shape, BF16),
            jax.ShapeDtypeStruct(conv_weight.shape, BF16),
            jax.ShapeDtypeStruct((LEVELS + 1, TOK, TOK), BF16),
            jax.ShapeDtypeStruct((6, TOK, 128), F32),
        ],
        scratch_shapes=[pltpu.SemaphoreType.DMA((2,))],
        compiler_params=params(),
        cost_estimate=pl.CostEstimate(flops=10**6, bytes_accessed=4 * 2**20, transcendentals=0),
        name="stage",
    )(tables, in_hbm(projected), in_hbm(conv_weight))


def preparing(pair, ins, xs, sys, right, keys):
    x_ref, halo_ref, w_ref, tab_ref, _, shared = ins
    k_at = pl.multiple_of(HK * DK + pair * 256, 512)
    v_at = pl.multiple_of(2 * HK * DK + pair * 512, 1024)
    kt_ref, kt_at = keys

    def usable():
        return [shared[j] for j in range(KW - 1)]

    def place():
        place_window(x_ref[:, pl.ds(k_at, 512)], halo_ref[:, pl.ds(k_at, 512)], xs, 0)
        place_window(x_ref[:, pl.ds(v_at, 1024)], halo_ref[:, pl.ds(v_at, 1024)], xs, 512)

    def key(n):
        p, a = n // 2, n % 2
        rows = tab_ref[pair + p]
        cols = jnp.transpose(rows)
        at = n * DK
        taps = w_ref[:, pl.ds(k_at + at, DK)].astype(F32)
        k = convolve_piece(xs, at, taps, usable()).astype(F32)
        k = k * unit(k)
        kb = k.astype(BF16)
        ktb = jnp.transpose(kb.astype(F32)).astype(BF16)
        kt_ref[kt_at + p, a * DK : (a + 1) * DK, :] = ktb
        inner = dot(kb, ktb) * shared[5]
        for b in range(2):
            lane = 2 * a + b
            h = GROUP * p + lane
            clock = column(cols, lane)
            within = decay_within(rows, clock, lane, shared[4])
            carried = jnp.exp2(clock) * shared[3]
            high, low = halves((column(cols, 4 + lane) * within) * inner)
            sys[h, :, 0:128] = high
            sys[h, :, 128:256] = low
            right[h, :, 0:DK] = (carried * k).astype(BF16)

    def value(h):
        taps = w_ref[:, pl.ds(v_at + h * DV, DV)].astype(F32)
        right[h, :, DK : DK + DV] = convolve_piece(xs, 512 + h * DV, taps, usable())

    steps = [place]
    steps += [functools.partial(key, n) for n in range(4)]
    steps += [functools.partial(value, h) for h in range(HEADS)]
    return steps


def solving(pair, ins, sys, right, keys, inv, pay_ref, ef_ref, at, kt_copy=None):
    tab_ref, masks, shared = ins[3:]
    kt_ref, kt_at = keys
    kept = {}

    def begin():
        for h in range(HEADS):
            inv[h] = masks[LEVELS] - sys[h, :, 0:128] * masks[0]

    def first_product(level):
        size = 1 << level
        kept["steps"] = []
        for h in range(HEADS):
            if size < 16:
                left = sys[h, :, 0:128]
            else:
                left = odd_rows(lambda r, e: sys[h, r:e, 0:128], size)
            kept["steps"].append(dot(left, inv[h]).astype(BF16))

    def second_product(level):
        size = 1 << level
        steps = kept["steps"]
        if size < 16:
            steps = [dot(inv[h], steps[h]).astype(BF16) for h in range(HEADS)]
            for h in range(HEADS):
                inv[h] = inv[h] - steps[h] * masks[level]
            return
        blank = jnp.zeros((size, 128), BF16)
        found = []
        for h in range(HEADS):
            expanded = []
            for r in range(0, TOK // 2, size):
                expanded += [blank, steps[h][r : r + size]]
            left = odd_rows(lambda r, e: inv[h, r:e, :], size)
            found.append(dot(left, jnp.concatenate(expanded, axis=0)).astype(BF16))
        for h in range(HEADS):
            for n, r in enumerate(range(size, TOK, 2 * size)):
                inv[h, r : r + size, :] = inv[h, r : r + size, :] - (
                    found[h][n * size : (n + 1) * size] * masks[level, r : r + size, :]
                )

    def check():
        kept["gaps"] = []
        for h in range(HEADS):
            rough = inv[h]
            product = dot(sys[h], jnp.concatenate([rough, rough], axis=0))
            kept["gaps"].append(
                ((masks[LEVELS].astype(F32) - rough.astype(F32)) - product).astype(BF16)
            )

    def row(h, n):
        return tab_ref[pair + h // GROUP, n : n + 1, :]

    def correct():
        for h in range(HEADS):
            fixed = inv[h].astype(F32) + dot(inv[h], kept["gaps"][h])
            inv[h] = (fixed * row(h, 4 + h % GROUP)).astype(BF16)

    def apply():
        kept["ef"] = []
        for h in range(HEADS):
            ef = dot(inv[h], right[h]).astype(BF16)
            here = slice((h % GROUP) * TOK, (h % GROUP + 1) * TOK)
            ef_ref[at + h // GROUP, here, :] = ef
            kept["ef"].append(ef)

    def write():
        last = []
        for h in range(HEADS):
            g, n = h // GROUP, h % GROUP
            ktb = kt_ref[kt_at + g, (n // 2) * DK : (n // 2 + 1) * DK, :]
            if kt_copy is not None and n % 2 == 0:
                kt_copy[at + g, (n // 2) * DK : (n // 2 + 1) * DK, :] = ktb
            clock = row(h, n)
            final = jnp.broadcast_to(clock[:, TOK - 1 : TOK], (1, TOK))
            ending = jnp.exp2((final - clock) + shared[4, TOK - 1 : TOK, :])
            carried = jnp.exp2(final) * shared[3, TOK - 1 : TOK, :]
            last.append(jnp.concatenate([carried, carried], axis=1))
            weighted = (ktb.astype(F32) * ending).astype(BF16)
            pay_ref[at + g, n * DK : (n + 1) * DK, :] = dot(weighted, kept["ef"][h]).astype(BF16)
        for g in range(2):
            pay_ref[at + g, GROUP * DK : ROWS, :] = split_rows(last[GROUP * g : GROUP * (g + 1)])

    steps = [begin]
    for level in range(1, LEVELS):
        steps.append(functools.partial(first_product, level))
        steps.append(functools.partial(second_product, level))
    return steps + [check, correct, apply, write]


def interleave(main, side):
    done = 0
    for n, step in enumerate(main):
        step()
        due = ((n + 1) * len(side) + len(main) - 1) // len(main)
        while done < min(due, len(side)):
            side[done]()
            done += 1


def send_kernel(
    meta, x_ref, halo_ref, w_ref, tab_ref, masks, shared, pay_ref, kt_ref, ef_ref, sys_out,
    right_out, kt_out, xs, sys, right, inv,
):
    ins = (x_ref, halo_ref, w_ref, tab_ref, masks, shared)
    pair, after = meta[0], meta[1]
    sets = [(sys.at[n], right.at[n], (kt_ref, 2 * n)) for n in range(2)]
    third = (sys_out, right_out, (kt_out, 0))
    for step in preparing(pair, ins, xs, *sets[0]):
        step()
    for n in range(2):
        main = solving(pair + 2 * n, ins, *sets[n], inv, pay_ref, ef_ref, 2 * n)
        if n == 0:
            side = preparing(pair + 2, ins, xs, *sets[1])
        else:
            side = preparing(after, ins, xs, *third)
        interleave(main, side)


def keep_kernel(
    meta, x_ref, halo_ref, w_ref, tab_ref, masks, shared, sys_in, right_in, kt_in, pay_ref,
    kt_ref, ef_ref, xs, sys, right, inv,
):
    ins = (x_ref, halo_ref, w_ref, tab_ref, masks, shared)
    pair = meta[1]
    own = (sys, right, (kt_ref, 2))
    interleave(
        solving(pair, ins, sys_in, right_in, (kt_in, 0), inv, pay_ref, ef_ref, 0, kt_ref),
        preparing(pair + 2, ins, xs, *own),
    )
    for step in solving(pair + 2, ins, *own, inv, pay_ref, ef_ref, 2):
        step()


def map_shapes():
    return [
        jax.ShapeDtypeStruct((4, ROWS, 256), BF16),
        jax.ShapeDtypeStruct((4, 2 * DK, TOK), BF16),
        jax.ShapeDtypeStruct((4, GROUP * TOK, 256), BF16),
    ]


def ready_shapes():
    return [
        jax.ShapeDtypeStruct((HEADS, TOK, 256), BF16),
        jax.ShapeDtypeStruct((HEADS, TOK, 256), BF16),
        jax.ShapeDtypeStruct((2, 2 * DK, TOK), BF16),
    ]


def map_cost():
    return pl.CostEstimate(
        flops=16 * 20 * 2 * 128**3, bytes_accessed=5 * 2**20, transcendentals=10**6
    )


def send_maps(meta, *ins):
    return pl.pallas_call(
        send_kernel,
        in_specs=[smem_spec()] + [whole_spec()] * len(ins),
        out_specs=[whole_spec()] * 6,
        out_shape=map_shapes() + ready_shapes(),
        scratch_shapes=[
            pltpu.VMEM((8 + TOK, 1536), F32),
            pltpu.VMEM((2, HEADS, TOK, 256), BF16),
            pltpu.VMEM((2, HEADS, TOK, 256), BF16),
            pltpu.VMEM((HEADS, TOK, TOK), BF16),
        ],
        compiler_params=params(),
        cost_estimate=map_cost(),
        name="send_maps",
    )(meta, *ins)


def keep_maps(meta, *ins):
    return pl.pallas_call(
        keep_kernel,
        in_specs=[smem_spec()] + [whole_spec()] * len(ins),
        out_specs=[whole_spec()] * 3,
        out_shape=map_shapes(),
        scratch_shapes=[
            pltpu.VMEM((8 + TOK, 1536), F32),
            pltpu.VMEM((HEADS, TOK, 256), BF16),
            pltpu.VMEM((HEADS, TOK, 256), BF16),
            pltpu.VMEM((HEADS, TOK, TOK), BF16),
        ],
        compiler_params=params(),
        cost_estimate=map_cost(),
        name="keep_maps",
    )(meta, *ins)


def read_kernel(meta, xq_ref, hq_ref, wq_ref, rows_ref, kt_ref, ef_ref, left_ref, r_ref, d_ref, xs):
    first = meta[2] == 0
    tail = left_ref[0, GROUP * DK : ROWS, :]
    rows = rows_ref[0]
    cols = jnp.transpose(rows)
    usable = [column(cols, 8 + j) for j in range(KW - 1)]
    living = column(cols, 12)
    hidden = hidden_where(rows, cols)
    place_window(xq_ref[...], hq_ref[...], xs, 0)
    taps = wq_ref[...].astype(F32)
    for a in range(2):
        queries = convolve_piece(xs, a * DK, taps[:, a * DK : (a + 1) * DK], usable)
        q = queries.astype(F32)
        scale = unit(q, DK ** (-0.5))
        inner = dot(queries, kt_ref[0, a * DK : (a + 1) * DK, :])
        for b in range(2):
            h = 2 * a + b
            clock = column(cols, h)
            scores = (inner * decay_within(rows, clock, h, hidden)).astype(BF16)
            both = dot(scores, ef_ref[0, h * TOK : (h + 1) * TOK, :])
            carried = jnp.exp2(clock) * living
            mine = slice(h * TOK, (h + 1) * TOK)
            reader = (carried * q - both[:, :DK]) * scale
            direct = both[:, DK:] * scale
            moved = dot(reader.astype(BF16), left_ref[0, h * DK : (h + 1) * DK, :])
            c = factor(tail, h)[:, :DK]
            r_ref[0, mine, :] = jnp.where(first, reader, c * reader - moved[:, :DK]).astype(BF16)
            d_ref[0, mine, :] = jnp.where(first, direct, direct + moved[:, DK:])


def make_reads(meta, slot, projected, halo, conv_weight, tables, keys_t, ef, left):
    def at(i, m):
        return (0, m[slot] + i)

    return pl.pallas_call(
        read_kernel,
        grid_spec=pltpu.PrefetchScalarGridSpec(
            num_scalar_prefetch=1,
            grid=(4,),
            in_specs=[
                pl.BlockSpec((TOK, 256), at),
                pl.BlockSpec((KW - 1, 256), at),
                pl.BlockSpec((KW, 256), at),
                pl.BlockSpec((1, 16, TOK), lambda i, m: (m[slot] + i, 0, 0)),
                pl.BlockSpec((1, 2 * DK, TOK), lambda i, m: (i, 0, 0)),
                pl.BlockSpec((1, GROUP * TOK, 256), lambda i, m: (i, 0, 0)),
                pl.BlockSpec((1, ROWS, 256), lambda i, m: (i, 0, 0)),
            ],
            out_specs=[
                pl.BlockSpec((1, GROUP * TOK, DK), lambda i, m: (i, 0, 0)),
                pl.BlockSpec((1, GROUP * TOK, DV), lambda i, m: (i, 0, 0)),
            ],
            scratch_shapes=[pltpu.VMEM((8 + TOK, 256), F32)],
        ),
        out_shape=[
            jax.ShapeDtypeStruct((4, GROUP * TOK, DK), BF16),
            jax.ShapeDtypeStruct((4, GROUP * TOK, DV), F32),
        ],
        compiler_params=params(),
        cost_estimate=pl.CostEstimate(
            flops=16 * 6 * 2 * 128**3, bytes_accessed=5 * 2**20, transcendentals=10**6
        ),
        name="reads",
    )(meta, projected, halo, conv_weight, tables, keys_t, ef, left)


def factor(tail, head):
    tail = tail.astype(F32)
    return (tail[head : head + 1] + tail[4 + head : 5 + head]) + tail[8 + head : 9 + head]


def compose(left, left_c, right, right_c):
    right_d = right[:, :DK]
    product = dot(right_d.astype(BF16), left.astype(BF16))
    return (
        right_c * left.astype(F32)
        + jnp.concatenate(
            [left_c[:, :DK] * right_d.astype(F32), right[:, DK:].astype(F32)], axis=1
        )
        - product
    )


def apply_map(each, c, state):
    product = dot(each[:, :DK], state)
    return c[:, :DK] * state.astype(F32) + each[:, DK:].astype(F32) - product


def pair_kernel(meta, mine_ref, other_ref, *out_refs):
    first = meta[2] == 0
    for m, out_ref in enumerate(out_refs):
        g = meta[3] ^ m
        tail_m, tail_o = mine_ref[g, GROUP * DK : ROWS, :], other_ref[g, GROUP * DK : ROWS, :]
        tail_l, tail_r = jnp.where(first, tail_m, tail_o), jnp.where(first, tail_o, tail_m)
        factors = []
        for h in range(GROUP):
            here = slice(h * DK, (h + 1) * DK)
            own, other = mine_ref[g, here, :], other_ref[g, here, :]
            left, right = jnp.where(first, own, other), jnp.where(first, other, own)
            left_c, right_c = factor(tail_l, h), factor(tail_r, h)
            out_ref[here, :] = compose(left, left_c, right, right_c).astype(BF16)
            factors.append(left_c * right_c)
        out_ref[GROUP * DK : ROWS, :] = split_rows(factors)


def pair_maps(meta, mine, other):
    return pl.pallas_call(
        pair_kernel,
        in_specs=[smem_spec(), whole_spec(), whole_spec()],
        out_specs=[whole_spec()] * 4,
        out_shape=[jax.ShapeDtypeStruct((ROWS, 256), BF16)] * 4,
        compiler_params=params(),
        cost_estimate=pl.CostEstimate(
            flops=16 * 2 * 2 * 128**3, bytes_accessed=3 * 2**20, transcendentals=0
        ),
        name="pair",
    )(meta, mine, other)


def plane_kernel(meta, x0, x1, x2, x3, prefix_ref, plane_ref, exit_ref, maps, sems):
    copies = []
    for m, x in enumerate((x0, x1, x2, x3)):
        copy = pltpu.make_async_copy(x, maps.at[meta[3] ^ m], sems.at[m])
        copy.start()
        copies.append(copy)
    prefix_ref[0, 0 : GROUP * DK, :] = jnp.zeros((GROUP * DK, 256), BF16)
    ones = jnp.ones((1, 256), F32)
    prefix_ref[0, GROUP * DK : ROWS, :] = split_rows([ones] * GROUP)
    for copy in copies:
        copy.wait()
    prefix_ref[1] = maps[0]
    run = [maps[0, h * DK : (h + 1) * DK, :].astype(F32) for h in range(GROUP)]
    run_c = [factor(maps[0, GROUP * DK : ROWS, :], h) for h in range(GROUP)]
    for a in range(1, 4):
        tail = maps[a, GROUP * DK : ROWS, :]
        for h in range(GROUP):
            here = slice(h * DK, (h + 1) * DK)
            c = factor(tail, h)
            run[h] = compose(run[h], run_c[h], maps[a, here, :], c)
            run_c[h] = run_c[h] * c
            if a < 3:
                prefix_ref[a + 1, here, :] = run[h].astype(BF16)
            else:
                plane_ref[here, :] = run[h].astype(BF16)
                exit_ref[here, :] = run[h][:, DK:].astype(BF16)
        if a < 3:
            prefix_ref[a + 1, GROUP * DK : ROWS, :] = split_rows(run_c)
    plane_ref[GROUP * DK : ROWS, :] = split_rows(run_c)


def plane_maps(meta, pieces):
    return pl.pallas_call(
        plane_kernel,
        in_specs=[smem_spec()] + [pl.BlockSpec(memory_space=pl.ANY)] * 4,
        out_specs=[whole_spec()] * 3,
        out_shape=[
            jax.ShapeDtypeStruct((4, ROWS, 256), BF16),
            jax.ShapeDtypeStruct((ROWS, 256), BF16),
            jax.ShapeDtypeStruct((GROUP * DK, DV), BF16),
        ],
        scratch_shapes=[pltpu.VMEM((4, ROWS, 256), BF16), pltpu.SemaphoreType.DMA((4,))],
        compiler_params=params(),
        cost_estimate=pl.CostEstimate(
            flops=12 * 2 * 2 * 128**3, bytes_accessed=2 * 2**20, transcendentals=0
        ),
        name="plane",
    )(meta, *pieces)


def hop_kernel(plane_ref, state_ref, out_ref):
    tail = plane_ref[GROUP * DK : ROWS, :]
    for h in range(GROUP):
        here = slice(h * DK, (h + 1) * DK)
        state = apply_map(plane_ref[here, :], factor(tail, h), state_ref[here, :])
        out_ref[here, :] = state.astype(BF16)


def hop(plane_map, state):
    return pl.pallas_call(
        hop_kernel,
        in_specs=[whole_spec()] * 2,
        out_specs=whole_spec(),
        out_shape=jax.ShapeDtypeStruct((GROUP * DK, DV), BF16),
        compiler_params=params(),
        cost_estimate=pl.CostEstimate(
            flops=4 * 2 * 128**3, bytes_accessed=2**19, transcendentals=0
        ),
        name="hop",
    )(plane_map, state)


def spread_kernel(meta, prefix_ref, before_ref, far_ref, *refs):
    out_refs = refs[-4:]
    state_refs = refs[:-4]
    before_tail = before_ref[GROUP * DK : ROWS, :]
    for h in range(GROUP):
        here = slice(h * DK, (h + 1) * DK)
        state = apply_map(before_ref[here, :], factor(before_tail, h), far_ref[here, :])
        state = state.astype(BF16)
        for ref in state_refs:
            state = state + ref[here, :]
        for m, out_ref in enumerate(out_refs):
            a = meta[3] ^ m
            c = factor(prefix_ref[a, GROUP * DK : ROWS, :], h)
            out_ref[here, :] = apply_map(prefix_ref[a, here, :], c, state).astype(BF16)


def spread(meta, prefix, before, far, states):
    return pl.pallas_call(
        spread_kernel,
        in_specs=[smem_spec()] + [whole_spec()] * (3 + len(states)),
        out_specs=[whole_spec()] * 4,
        out_shape=[jax.ShapeDtypeStruct((GROUP * DK, DV), BF16)] * 4,
        compiler_params=params(),
        cost_estimate=pl.CostEstimate(
            flops=20 * 2 * 128**3, bytes_accessed=2**21, transcendentals=0
        ),
        name="spread",
    )(meta, prefix, before, far, *states)


def entering_states(plane_map, leaving, planes):
    def ahead(block, plane, distance=1):
        members = range(8 * plane, 8 * plane + 8)
        return lax.ppermute(block, "seq", [(i, i + 8 * distance) for i in members])

    if planes == 4:
        first = ahead(leaving, 0)
        before = ahead(plane_map, 2)
        second = hop(plane_map, first)
        far = ahead(second, 1, 2)
        near = ahead(second, 1)
        return before, far, [first, near]
    states = []
    for plane in range(planes - 1):
        state = ahead(leaving, plane)
        states.append(state)
        if plane < planes - 2:
            leaving = hop(plane_map, state)
    return jnp.zeros_like(plane_map), jnp.zeros_like(leaving), states


def read_out(meta, r_ref, d_ref, e_refs, rows):
    for m, e_ref in enumerate(e_refs):
        g = meta[3] ^ m
        for h in range(GROUP):
            here = slice(h * TOK, (h + 1) * TOK)
            total = dot(r_ref[g, here, :], e_ref[here, :]) + d_ref[g, here, :]
            rows[g, :, h * DV : (h + 1) * DV] = total.astype(BF16)
        yield m, g


def half_kernel(meta, r_ref, d_ref, e0, e1, e2, e3, rows):
    for _ in read_out(meta, r_ref, d_ref, (e0, e1, e2, e3), rows):
        pass


def read_half(meta, reads, direct, states):
    return pl.pallas_call(
        half_kernel,
        in_specs=[smem_spec()] + [whole_spec()] * 6,
        out_specs=whole_spec(),
        out_shape=jax.ShapeDtypeStruct((4, TOK, GROUP * DV), BF16),
        compiler_params=params(),
        cost_estimate=pl.CostEstimate(
            flops=16 * 2 * 128**3, bytes_accessed=3 * 2**20, transcendentals=0
        ),
        name="half",
    )(meta, reads, direct, *states)


def emit_kernel(meta, kept, r_ref, d_ref, e0, e1, e2, e3, out_ref, rows, sems):
    copies = []

    def put(source, n, slot, g):
        start = pl.multiple_of((meta[slot] + g) * (GROUP * DV), GROUP * DV)
        copy = pltpu.make_async_copy(
            source.at[g], out_ref.at[:, pl.ds(start, GROUP * DV)], sems.at[n]
        )
        copy.start()
        copies.append(copy)

    for g in range(4):
        put(kept, g, 1, g)
    for m, g in read_out(meta, r_ref, d_ref, (e0, e1, e2, e3), rows):
        put(rows, 4 + m, 0, g)
    for copy in copies:
        copy.wait()


def emit(meta, kept, reads, direct, states):
    return pl.pallas_call(
        emit_kernel,
        in_specs=[smem_spec()] + [whole_spec()] * 7,
        out_specs=pl.BlockSpec(memory_space=pl.ANY),
        out_shape=jax.ShapeDtypeStruct((TOK, HV * DV), BF16),
        scratch_shapes=[
            pltpu.VMEM((4, TOK, GROUP * DV), BF16),
            pltpu.SemaphoreType.DMA((8,)),
        ],
        compiler_params=params(),
        cost_estimate=pl.CostEstimate(
            flops=16 * 2 * 128**3, bytes_accessed=3 * 2**20, transcendentals=0
        ),
        name="emit",
    )(meta, kept, reads, direct, *states)


def shards(projected, conv_weight, decay_log, write_strength, starts):
    count = lax.axis_size("seq")
    me = lax.axis_index("seq")
    core, place = me & 1, (me >> 1) & 3
    slots = lax.iota(jnp.int32, 8)
    meta = jnp.zeros((8,), jnp.int32)
    for slot, value in enumerate((4 * (1 - core), 4 * core, core, place, me >> 3)):
        meta = jnp.where(slots == slot, value, meta)

    def exchange(block, bits):
        return lax.ppermute(block, "seq", [(i, i ^ bits) for i in range(count)])

    tables, tail_rows = prologue(decay_log, write_strength, starts, projected)
    halo = lax.ppermute(tail_rows, "seq", [(i, i + 1) for i in range(count - 1)])
    projected, conv_weight, masks, shared = stage(tables, projected, conv_weight)
    ins = (projected, halo, conv_weight, tables, masks, shared)

    pay_s, kt_s, ef_s, *ready = send_maps(meta, *ins)
    other = exchange(pay_s, 1)
    mine, kt_k, ef_k = keep_maps(meta, *ins, *ready)
    x0, x1, x2, x3 = pair_maps(meta, mine, other)
    x3, x1, x2 = exchange(x3, 6), exchange(x1, 2), exchange(x2, 4)
    x0, own = lax.optimization_barrier((x0, mine))
    left = exchange(own, 1)
    r_k, d_k = make_reads(meta, 1, projected, halo, conv_weight, tables, kt_k, ef_k, other)
    r_s, d_s = make_reads(meta, 0, projected, halo, conv_weight, tables, kt_s, ef_s, left)
    x0, r_k, d_k, r_s, d_s = lax.optimization_barrier((x0, r_k, d_k, r_s, d_s))
    prefix, plane_map, leaving = plane_maps(meta, (x0, x1, x2, x3))
    before, far, arrived = entering_states(plane_map, leaving, count // 8)
    e0, e1, e2, e3 = spread(meta, prefix, before, far, arrived)
    e3, e1, e2 = exchange(e3, 6), exchange(e1, 2), exchange(e2, 4)
    states = (e0, e1, e2, e3)
    partner = [exchange(e, 1) for e in states]
    kept = read_half(meta, r_k, d_k, states)
    return emit(meta, kept, r_s, d_s, partner)


def solution(mesh):
    in_specs = (
        P(("groups", "seq"), None),
        P(),
        P(None, ("groups", "seq")),
        P(None, ("groups", "seq")),
        P(("groups", "seq")),
    )
    out_specs = P(("groups", "seq"), None)

    return jax.shard_map(shards, mesh=mesh, in_specs=in_specs, out_specs=out_specs, check_vma=False)
```

```python
import functools

import jax
import jax.numpy as jnp
from jax import lax
from jax.experimental import pallas as pl
from jax.experimental.pallas import tpu as pltpu
from jax.sharding import PartitionSpec as P


HK = 16
DK = 128
HV = 32
DV = 128
KW = 4
TOK = 128
NORM_EPS = 1e-06
GROUP = 4
LOG2E = 1.4426950408889634
HIDDEN = -1e30
ROWS = GROUP * DK + 16
F32 = jnp.float32
BF16 = jnp.bfloat16


def dot(a, b):
    return jnp.dot(a, b, preferred_element_type=F32)


def params(**kw):
    return pltpu.CompilerParams(vmem_limit_bytes=20 << 20, **kw)


def whole_spec():
    return pl.BlockSpec(memory_space=pltpu.VMEM)


def smem_spec():
    return pl.BlockSpec(memory_space=pltpu.SMEM)


def in_hbm(x):
    return pltpu.with_memory_space_constraint(x, pltpu.HBM)


def tail_kernel(starts_ref, x_ref, tail_ref):
    rows = x_ref.shape[0]
    flags = starts_ref[...].astype(F32)
    last = 1.0 - flags[:, TOK - 1 : TOK]
    keep = [last * (1.0 - flags[:, TOK - 2 : TOK - 1]), last, jnp.ones((1, 1), F32)]
    for r in range(KW - 1):
        row = x_ref[rows - KW + 1 + r : rows - KW + 2 + r, :].astype(F32)
        tail_ref[r : r + 1, :] = (row * keep[r]).astype(BF16)


def tail_of(starts, projected):
    channels = projected.shape[1]
    last = projected.shape[0] // 16 - 1
    return pl.pallas_call(
        tail_kernel,
        grid=(1,),
        in_specs=[
            pl.BlockSpec((1, TOK), lambda i: (0, 0)),
            pl.BlockSpec((16, channels), lambda i: (last, 0)),
        ],
        out_specs=pl.BlockSpec((KW - 1, channels), lambda i: (0, 0)),
        out_shape=jax.ShapeDtypeStruct((KW - 1, channels), BF16),
        compiler_params=params(),
        cost_estimate=pl.CostEstimate(flops=10**5, bytes_accessed=10**6, transcendentals=0),
        name="tail",
    )(in_hbm(starts), in_hbm(projected))


def write_tables(decay_ref, beta_ref, starts_ref, out_ref):
    src, dst = positions()
    cum = LOG2E * jnp.dot(
        decay_ref[...],
        (src <= dst).astype(F32),
        precision=lax.Precision.HIGHEST,
        preferred_element_type=F32,
    )
    flags = jnp.broadcast_to(starts_ref[...].astype(F32), (8, TOK)).astype(BF16)
    episode = [dot(flags, (src + j <= dst).astype(BF16))[0:1] for j in range(KW)]
    usable = [(episode[0] == episode[j]).astype(F32) for j in range(1, KW)]
    living = (episode[0] == 0.0).astype(F32)
    zero = jnp.zeros((1, TOK), F32)
    shared = jnp.concatenate(usable + [episode[0], living, zero, zero, zero], axis=0)
    for pair in range(HV // GROUP):
        out_ref[pair, 0:4, :] = cum[GROUP * pair : GROUP * (pair + 1)]
        out_ref[pair, 4:8, :] = beta_ref[GROUP * pair : GROUP * (pair + 1), :]
        out_ref[pair, 8:16, :] = shared


def place_window(x, halo, xs, first):
    cols = slice(first, first + x.shape[1])
    xs[8 : 8 + TOK, cols] = x.astype(F32)
    xs[8 - KW + 1 : 8, cols] = halo.astype(F32)


def convolve_piece(xs, first, taps, usable):
    here = slice(first, first + 128)
    total = xs[8 : 8 + TOK, here] * taps[3:4]
    for j in range(1, KW):
        total = total + (xs[8 - j : 8 - j + TOK, here] * usable[j - 1]) * taps[3 - j : 4 - j]
    return (total / (1.0 + jnp.exp2(total * -LOG2E))).astype(BF16)


def column(cols, lane):
    return jnp.broadcast_to(cols[:, lane : lane + 1], (TOK, 128))


def positions():
    i = lax.broadcasted_iota(jnp.int32, (TOK, TOK), 0)
    j = lax.broadcasted_iota(jnp.int32, (TOK, TOK), 1)
    return i, j


def hidden_where(rows, cols):
    i, j = positions()
    seen = (column(cols, 11) == rows[11:12, :]) & (i >= j)
    return jnp.where(seen, 0.0, HIDDEN)


def decay_within(rows, clock, head, hidden):
    return jnp.exp2((clock - rows[head : head + 1, :]) + hidden)


def unit(x, scale=1.0):
    return lax.rsqrt(jnp.sum(x * x, axis=-1, keepdims=True) + NORM_EPS) * scale


def split_rows(x):
    pieces, rest = [], list(x)
    for _ in range(3):
        highs = [c.astype(BF16).astype(F32) for c in rest]
        pieces += highs
        rest = [c - high for c, high in zip(rest, highs)]
    pieces.append(jnp.zeros((4, 256), F32))
    return jnp.concatenate(pieces, axis=0).astype(BF16)


LEVELS = 7
HEADS = 8


def odd_rows(get, size):
    return jnp.concatenate([get(r, r + size) for r in range(size, TOK, 2 * size)], axis=0)


def stage_kernel(
    decay_ref, beta_ref, starts_ref, x_hbm, w_hbm, x_out, w_out, tab_ref, masks, shared, sems
):
    copies = [
        pltpu.make_async_copy(x_hbm, x_out, sems.at[0]),
        pltpu.make_async_copy(w_hbm, w_out, sems.at[1]),
    ]
    for copy in copies:
        copy.start()
    write_tables(decay_ref, beta_ref, starts_ref, tab_ref)
    rows = tab_ref[0]
    cols = jnp.transpose(rows)
    for j in range(KW - 1):
        shared[j] = column(cols, 8 + j)
    shared[3] = column(cols, 12)
    shared[4] = hidden_where(rows, cols)
    i, j = positions()
    apart = i ^ j
    for level in range(LEVELS):
        masks[level] = (((apart >> level) == 1) & (i > j)).astype(F32).astype(BF16)
    shared[5] = (i > j).astype(F32)
    masks[LEVELS] = (i == j).astype(F32).astype(BF16)
    for copy in copies:
        copy.wait()


def stage(decay_log, write_strength, starts, projected, conv_weight):
    def whole(*shape):
        return pl.BlockSpec(shape, lambda i: (0,) * len(shape))

    return pl.pallas_call(
        stage_kernel,
        grid=(1,),
        in_specs=[whole(HV, TOK), whole(HV, TOK), whole(1, TOK)]
        + [pl.BlockSpec(memory_space=pl.ANY)] * 2,
        out_specs=[whole_spec()] * 5,
        out_shape=[
            jax.ShapeDtypeStruct(projected.shape, BF16),
            jax.ShapeDtypeStruct(conv_weight.shape, BF16),
            jax.ShapeDtypeStruct((HV // GROUP, 16, TOK), F32),
            jax.ShapeDtypeStruct((LEVELS + 1, TOK, TOK), BF16),
            jax.ShapeDtypeStruct((6, TOK, 128), F32),
        ],
        scratch_shapes=[pltpu.SemaphoreType.DMA((2,))],
        compiler_params=params(),
        cost_estimate=pl.CostEstimate(flops=10**7, bytes_accessed=4 * 2**20, transcendentals=0),
        name="stage",
    )(
        in_hbm(decay_log),
        in_hbm(write_strength),
        in_hbm(starts),
        in_hbm(projected),
        in_hbm(conv_weight),
    )


def preparing(pair, ins, xs, sys, right, keys):
    x_ref, halo_ref, w_ref, tab_ref, _, shared = ins
    k_at = pl.multiple_of(HK * DK + pair * 256, 512)
    v_at = pl.multiple_of(2 * HK * DK + pair * 512, 1024)
    kt_ref, kt_at = keys

    def usable():
        return [shared[j] for j in range(KW - 1)]

    def place():
        place_window(x_ref[:, pl.ds(k_at, 512)], halo_ref[:, pl.ds(k_at, 512)], xs, 0)
        place_window(x_ref[:, pl.ds(v_at, 1024)], halo_ref[:, pl.ds(v_at, 1024)], xs, 512)

    def key(n):
        p, a = n // 2, n % 2
        rows = tab_ref[pair + p]
        cols = jnp.transpose(rows)
        at = n * DK
        taps = w_ref[:, pl.ds(k_at + at, DK)].astype(F32)
        k = convolve_piece(xs, at, taps, usable()).astype(F32)
        k = k * unit(k)
        kb = k.astype(BF16)
        ktb = jnp.transpose(kb.astype(F32)).astype(BF16)
        kt_ref[kt_at + p, a * DK : (a + 1) * DK, :] = ktb
        inner = dot(kb, ktb) * shared[5]
        for b in range(2):
            lane = 2 * a + b
            h = GROUP * p + lane
            clock = column(cols, lane)
            within = decay_within(rows, clock, lane, shared[4])
            carried = jnp.exp2(clock) * shared[3]
            sys[h] = ((column(cols, 4 + lane) * within) * inner).astype(BF16)
            right[h, :, 0:DK] = (carried * k).astype(BF16)

    def value(h):
        taps = w_ref[:, pl.ds(v_at + h * DV, DV)].astype(F32)
        right[h, :, DK : DK + DV] = convolve_piece(xs, 512 + h * DV, taps, usable())

    steps = [place]
    steps += [functools.partial(key, n) for n in range(4)]
    steps += [functools.partial(value, h) for h in range(HEADS)]
    return steps


def solving(pair, ins, sys, right, keys, inv, pay_ref, ef_ref, at, kt_copy=None):
    tab_ref, masks, shared = ins[3:]
    kt_ref, kt_at = keys
    kept = {}

    def begin():
        for h in range(HEADS):
            inv[h] = masks[LEVELS] - sys[h] * masks[0]

    def first_product(level):
        size = 1 << level
        kept["steps"] = []
        for h in range(HEADS):
            if size < 16:
                left = sys[h]
            else:
                left = odd_rows(lambda r, e: sys[h, r:e, :], size)
            kept["steps"].append(dot(left, inv[h]).astype(BF16))

    def second_product(level):
        size = 1 << level
        steps = kept["steps"]
        if size < 16:
            steps = [dot(inv[h], steps[h]).astype(BF16) for h in range(HEADS)]
            for h in range(HEADS):
                inv[h] = inv[h] - steps[h] * masks[level]
            return
        blank = jnp.zeros((size, 128), BF16)
        found = []
        for h in range(HEADS):
            expanded = []
            for r in range(0, TOK // 2, size):
                expanded += [blank, steps[h][r : r + size]]
            left = odd_rows(lambda r, e: inv[h, r:e, :], size)
            found.append(dot(left, jnp.concatenate(expanded, axis=0)).astype(BF16))
        for h in range(HEADS):
            for n, r in enumerate(range(size, TOK, 2 * size)):
                inv[h, r : r + size, :] = inv[h, r : r + size, :] - (
                    found[h][n * size : (n + 1) * size] * masks[level, r : r + size, :]
                )

    def check():
        kept["gaps"] = []
        for h in range(HEADS):
            rough = inv[h]
            product = dot(sys[h], rough)
            kept["gaps"].append(
                ((masks[LEVELS].astype(F32) - rough.astype(F32)) - product).astype(BF16)
            )

    def row(h, n):
        return tab_ref[pair + h // GROUP, n : n + 1, :]

    def correct():
        for h in range(HEADS):
            fixed = inv[h].astype(F32) + dot(inv[h], kept["gaps"][h])
            inv[h] = (fixed * row(h, 4 + h % GROUP)).astype(BF16)

    def apply():
        kept["ef"] = []
        for h in range(HEADS):
            ef = dot(inv[h], right[h]).astype(BF16)
            here = slice((h % GROUP) * TOK, (h % GROUP + 1) * TOK)
            ef_ref[at + h // GROUP, here, :] = ef
            kept["ef"].append(ef)

    def write():
        last = []
        for h in range(HEADS):
            g, n = h // GROUP, h % GROUP
            ktb = kt_ref[kt_at + g, (n // 2) * DK : (n // 2 + 1) * DK, :]
            if kt_copy is not None and n % 2 == 0:
                kt_copy[at + g, (n // 2) * DK : (n // 2 + 1) * DK, :] = ktb
            clock = row(h, n)
            final = jnp.broadcast_to(clock[:, TOK - 1 : TOK], (1, TOK))
            ending = jnp.exp2((final - clock) + shared[4, TOK - 1 : TOK, :])
            carried = jnp.exp2(final) * shared[3, TOK - 1 : TOK, :]
            last.append(jnp.concatenate([carried, carried], axis=1))
            weighted = (ktb.astype(F32) * ending).astype(BF16)
            pay_ref[at + g, n * DK : (n + 1) * DK, :] = dot(weighted, kept["ef"][h]).astype(BF16)
        for g in range(2):
            pay_ref[at + g, GROUP * DK : ROWS, :] = split_rows(last[GROUP * g : GROUP * (g + 1)])

    steps = [begin]
    for level in range(1, LEVELS):
        steps.append(functools.partial(first_product, level))
        steps.append(functools.partial(second_product, level))
    return steps + [check, correct, apply, write]


def interleave(main, side):
    done = 0
    for n, step in enumerate(main):
        step()
        due = ((n + 1) * len(side) + len(main) - 1) // len(main)
        while done < min(due, len(side)):
            side[done]()
            done += 1


def send_kernel(
    meta, x_ref, halo_ref, w_ref, tab_ref, masks, shared, pay_ref, kt_ref, ef_ref, sys_out,
    right_out, kt_out, xs, sys, right, inv,
):
    ins = (x_ref, halo_ref, w_ref, tab_ref, masks, shared)
    pair, after = meta[0], meta[1]
    sets = [(sys.at[n], right.at[n], (kt_ref, 2 * n)) for n in range(2)]
    third = (sys_out, right_out, (kt_out, 0))
    for step in preparing(pair, ins, xs, *sets[0]):
        step()
    for n in range(2):
        main = solving(pair + 2 * n, ins, *sets[n], inv, pay_ref, ef_ref, 2 * n)
        if n == 0:
            side = preparing(pair + 2, ins, xs, *sets[1])
        else:
            side = preparing(after, ins, xs, *third)
        interleave(main, side)


def keep_kernel(
    meta, x_ref, halo_ref, w_ref, tab_ref, masks, shared, sys_in, right_in, kt_in, pay_ref,
    kt_ref, ef_ref, xs, sys, right, inv,
):
    ins = (x_ref, halo_ref, w_ref, tab_ref, masks, shared)
    pair = meta[1]
    own = (sys, right, (kt_ref, 2))
    interleave(
        solving(pair, ins, sys_in, right_in, (kt_in, 0), inv, pay_ref, ef_ref, 0, kt_ref),
        preparing(pair + 2, ins, xs, *own),
    )
    for step in solving(pair + 2, ins, *own, inv, pay_ref, ef_ref, 2):
        step()


def map_shapes():
    return [
        jax.ShapeDtypeStruct((4, ROWS, 256), BF16),
        jax.ShapeDtypeStruct((4, 2 * DK, TOK), BF16),
        jax.ShapeDtypeStruct((4, GROUP * TOK, 256), BF16),
    ]


def ready_shapes():
    return [
        jax.ShapeDtypeStruct((HEADS, TOK, TOK), BF16),
        jax.ShapeDtypeStruct((HEADS, TOK, 256), BF16),
        jax.ShapeDtypeStruct((2, 2 * DK, TOK), BF16),
    ]


def map_cost():
    return pl.CostEstimate(
        flops=16 * 20 * 2 * 128**3, bytes_accessed=5 * 2**20, transcendentals=10**6
    )


def send_maps(meta, *ins):
    return pl.pallas_call(
        send_kernel,
        in_specs=[smem_spec()] + [whole_spec()] * len(ins),
        out_specs=[whole_spec()] * 6,
        out_shape=map_shapes() + ready_shapes(),
        scratch_shapes=[
            pltpu.VMEM((8 + TOK, 1536), F32),
            pltpu.VMEM((2, HEADS, TOK, TOK), BF16),
            pltpu.VMEM((2, HEADS, TOK, 256), BF16),
            pltpu.VMEM((HEADS, TOK, TOK), BF16),
        ],
        compiler_params=params(),
        cost_estimate=map_cost(),
        name="send_maps",
    )(meta, *ins)


def keep_maps(meta, *ins):
    return pl.pallas_call(
        keep_kernel,
        in_specs=[smem_spec()] + [whole_spec()] * len(ins),
        out_specs=[whole_spec()] * 3,
        out_shape=map_shapes(),
        scratch_shapes=[
            pltpu.VMEM((8 + TOK, 1536), F32),
            pltpu.VMEM((HEADS, TOK, TOK), BF16),
            pltpu.VMEM((HEADS, TOK, 256), BF16),
            pltpu.VMEM((HEADS, TOK, TOK), BF16),
        ],
        compiler_params=params(),
        cost_estimate=map_cost(),
        name="keep_maps",
    )(meta, *ins)


def read_kernel(meta, xq_ref, hq_ref, wq_ref, rows_ref, kt_ref, ef_ref, left_ref, r_ref, d_ref, xs):
    first = meta[2] == 0
    tail = left_ref[0, GROUP * DK : ROWS, :]
    rows = rows_ref[0]
    cols = jnp.transpose(rows)
    usable = [column(cols, 8 + j) for j in range(KW - 1)]
    living = column(cols, 12)
    hidden = hidden_where(rows, cols)
    place_window(xq_ref[...], hq_ref[...], xs, 0)
    taps = wq_ref[...].astype(F32)
    for a in range(2):
        queries = convolve_piece(xs, a * DK, taps[:, a * DK : (a + 1) * DK], usable)
        q = queries.astype(F32)
        scale = unit(q, DK ** (-0.5))
        inner = dot(queries, kt_ref[0, a * DK : (a + 1) * DK, :])
        for b in range(2):
            h = 2 * a + b
            clock = column(cols, h)
            scores = (inner * decay_within(rows, clock, h, hidden)).astype(BF16)
            both = dot(scores, ef_ref[0, h * TOK : (h + 1) * TOK, :])
            carried = jnp.exp2(clock) * living
            mine = slice(h * TOK, (h + 1) * TOK)
            reader = (carried * q - both[:, :DK]) * scale
            direct = both[:, DK:] * scale
            moved = dot(reader.astype(BF16), left_ref[0, h * DK : (h + 1) * DK, :])
            c = factor(tail, h)[:, :DK]
            r_ref[0, mine, :] = jnp.where(first, reader, c * reader - moved[:, :DK]).astype(BF16)
            d_ref[0, mine, :] = jnp.where(first, direct, direct + moved[:, DK:])


def make_reads(meta, slot, projected, halo, conv_weight, tables, keys_t, ef, left):
    def at(i, m):
        return (0, m[slot] + i)

    return pl.pallas_call(
        read_kernel,
        grid_spec=pltpu.PrefetchScalarGridSpec(
            num_scalar_prefetch=1,
            grid=(4,),
            in_specs=[
                pl.BlockSpec((TOK, 256), at),
                pl.BlockSpec((KW - 1, 256), at),
                pl.BlockSpec((KW, 256), at),
                pl.BlockSpec((1, 16, TOK), lambda i, m: (m[slot] + i, 0, 0)),
                pl.BlockSpec((1, 2 * DK, TOK), lambda i, m: (i, 0, 0)),
                pl.BlockSpec((1, GROUP * TOK, 256), lambda i, m: (i, 0, 0)),
                pl.BlockSpec((1, ROWS, 256), lambda i, m: (i, 0, 0)),
            ],
            out_specs=[
                pl.BlockSpec((1, GROUP * TOK, DK), lambda i, m: (i, 0, 0)),
                pl.BlockSpec((1, GROUP * TOK, DV), lambda i, m: (i, 0, 0)),
            ],
            scratch_shapes=[pltpu.VMEM((8 + TOK, 256), F32)],
        ),
        out_shape=[
            jax.ShapeDtypeStruct((4, GROUP * TOK, DK), BF16),
            jax.ShapeDtypeStruct((4, GROUP * TOK, DV), F32),
        ],
        compiler_params=params(),
        cost_estimate=pl.CostEstimate(
            flops=16 * 6 * 2 * 128**3, bytes_accessed=5 * 2**20, transcendentals=10**6
        ),
        name="reads",
    )(meta, projected, halo, conv_weight, tables, keys_t, ef, left)


def factor(tail, head):
    tail = tail.astype(F32)
    return (tail[head : head + 1] + tail[4 + head : 5 + head]) + tail[8 + head : 9 + head]


def compose(left, left_c, right, right_c):
    right_d = right[:, :DK]
    product = dot(right_d.astype(BF16), left.astype(BF16))
    return (
        right_c * left.astype(F32)
        + jnp.concatenate(
            [left_c[:, :DK] * right_d.astype(F32), right[:, DK:].astype(F32)], axis=1
        )
        - product
    )


def apply_map(each, c, state):
    product = dot(each[:, :DK], state)
    return c[:, :DK] * state.astype(F32) + each[:, DK:].astype(F32) - product


def pair_kernel(meta, mine_ref, other_ref, *out_refs):
    def combine(left_ref, right_ref):
        for m, out_ref in enumerate(out_refs):
            g = meta[3] ^ m
            left_tail = left_ref[g, GROUP * DK : ROWS, :]
            right_tail = right_ref[g, GROUP * DK : ROWS, :]
            factors = []
            for h in range(GROUP):
                here = slice(h * DK, (h + 1) * DK)
                left_c, right_c = factor(left_tail, h), factor(right_tail, h)
                both = compose(left_ref[g, here, :], left_c, right_ref[g, here, :], right_c)
                out_ref[here, :] = both.astype(BF16)
                factors.append(left_c * right_c)
            out_ref[GROUP * DK : ROWS, :] = split_rows(factors)

    pl.when(meta[2] == 0)(lambda: combine(mine_ref, other_ref))
    pl.when(meta[2] != 0)(lambda: combine(other_ref, mine_ref))


def pair_maps(meta, mine, other):
    return pl.pallas_call(
        pair_kernel,
        in_specs=[smem_spec(), whole_spec(), whole_spec()],
        out_specs=[whole_spec()] * 4,
        out_shape=[jax.ShapeDtypeStruct((ROWS, 256), BF16)] * 4,
        compiler_params=params(),
        cost_estimate=pl.CostEstimate(
            flops=16 * 2 * 2 * 128**3, bytes_accessed=3 * 2**20, transcendentals=0
        ),
        name="pair",
    )(meta, mine, other)


def plane_kernel(meta, x0, x1, x2, x3, prefix_ref, plane_ref, exit_ref, maps, sems):
    copies = []
    for m, x in enumerate((x0, x1, x2, x3)):
        copy = pltpu.make_async_copy(x, maps.at[meta[3] ^ m], sems.at[m])
        copy.start()
        copies.append(copy)
    prefix_ref[0, 0 : GROUP * DK, :] = jnp.zeros((GROUP * DK, 256), BF16)
    ones = jnp.ones((1, 256), F32)
    prefix_ref[0, GROUP * DK : ROWS, :] = split_rows([ones] * GROUP)
    for copy in copies:
        copy.wait()
    prefix_ref[1] = maps[0]
    run = [maps[0, h * DK : (h + 1) * DK, :].astype(F32) for h in range(GROUP)]
    run_c = [factor(maps[0, GROUP * DK : ROWS, :], h) for h in range(GROUP)]
    for a in range(1, 4):
        tail = maps[a, GROUP * DK : ROWS, :]
        for h in range(GROUP):
            here = slice(h * DK, (h + 1) * DK)
            c = factor(tail, h)
            run[h] = compose(run[h], run_c[h], maps[a, here, :], c)
            run_c[h] = run_c[h] * c
            if a < 3:
                prefix_ref[a + 1, here, :] = run[h].astype(BF16)
            else:
                plane_ref[here, :] = run[h].astype(BF16)
                exit_ref[here, :] = run[h][:, DK:].astype(BF16)
        if a < 3:
            prefix_ref[a + 1, GROUP * DK : ROWS, :] = split_rows(run_c)
    plane_ref[GROUP * DK : ROWS, :] = split_rows(run_c)


def plane_maps(meta, pieces):
    return pl.pallas_call(
        plane_kernel,
        in_specs=[smem_spec()] + [pl.BlockSpec(memory_space=pl.ANY)] * 4,
        out_specs=[whole_spec()] * 3,
        out_shape=[
            jax.ShapeDtypeStruct((4, ROWS, 256), BF16),
            jax.ShapeDtypeStruct((ROWS, 256), BF16),
            jax.ShapeDtypeStruct((GROUP * DK, DV), BF16),
        ],
        scratch_shapes=[pltpu.VMEM((4, ROWS, 256), BF16), pltpu.SemaphoreType.DMA((4,))],
        compiler_params=params(),
        cost_estimate=pl.CostEstimate(
            flops=12 * 2 * 2 * 128**3, bytes_accessed=2 * 2**20, transcendentals=0
        ),
        name="plane",
    )(meta, *pieces)


def hop_kernel(plane_ref, state_ref, out_ref):
    tail = plane_ref[GROUP * DK : ROWS, :]
    for h in range(GROUP):
        here = slice(h * DK, (h + 1) * DK)
        state = apply_map(plane_ref[here, :], factor(tail, h), state_ref[here, :])
        out_ref[here, :] = state.astype(BF16)


def hop(plane_map, state):
    return pl.pallas_call(
        hop_kernel,
        in_specs=[whole_spec()] * 2,
        out_specs=whole_spec(),
        out_shape=jax.ShapeDtypeStruct((GROUP * DK, DV), BF16),
        compiler_params=params(),
        cost_estimate=pl.CostEstimate(
            flops=4 * 2 * 128**3, bytes_accessed=2**19, transcendentals=0
        ),
        name="hop",
    )(plane_map, state)


def spread_kernel(meta, prefix_ref, before_ref, far_ref, *refs):
    out_refs = refs[-4:]
    state_refs = refs[:-4]
    before_tail = before_ref[GROUP * DK : ROWS, :]
    for h in range(GROUP):
        here = slice(h * DK, (h + 1) * DK)
        state = apply_map(before_ref[here, :], factor(before_tail, h), far_ref[here, :])
        state = state.astype(BF16)
        for ref in state_refs:
            state = state + ref[here, :]
        for m, out_ref in enumerate(out_refs):
            a = meta[3] ^ m
            c = factor(prefix_ref[a, GROUP * DK : ROWS, :], h)
            out_ref[here, :] = apply_map(prefix_ref[a, here, :], c, state).astype(BF16)


def spread(meta, prefix, before, far, states):
    return pl.pallas_call(
        spread_kernel,
        in_specs=[smem_spec()] + [whole_spec()] * (3 + len(states)),
        out_specs=[whole_spec()] * 4,
        out_shape=[jax.ShapeDtypeStruct((GROUP * DK, DV), BF16)] * 4,
        compiler_params=params(),
        cost_estimate=pl.CostEstimate(
            flops=20 * 2 * 128**3, bytes_accessed=2**21, transcendentals=0
        ),
        name="spread",
    )(meta, prefix, before, far, *states)


def entering_states(plane_map, leaving, planes):
    def ahead(block, plane, distance=1):
        members = range(8 * plane, 8 * plane + 8)
        return lax.ppermute(block, "seq", [(i, i + 8 * distance) for i in members])

    if planes == 4:
        first = ahead(leaving, 0)
        before = ahead(plane_map, 2)
        second = hop(plane_map, first)
        far = ahead(second, 1, 2)
        near = ahead(second, 1)
        return before, far, [first, near]
    states = []
    for plane in range(planes - 1):
        state = ahead(leaving, plane)
        states.append(state)
        if plane < planes - 2:
            leaving = hop(plane_map, state)
    return jnp.zeros_like(plane_map), jnp.zeros_like(leaving), states


def read_out(meta, r_ref, d_ref, e_refs, rows):
    for m, e_ref in enumerate(e_refs):
        g = meta[3] ^ m
        for h in range(GROUP):
            here = slice(h * TOK, (h + 1) * TOK)
            total = dot(r_ref[g, here, :], e_ref[here, :]) + d_ref[g, here, :]
            rows[g, :, h * DV : (h + 1) * DV] = total.astype(BF16)
        yield m, g


def half_kernel(meta, r_ref, d_ref, e0, e1, e2, e3, rows):
    for _ in read_out(meta, r_ref, d_ref, (e0, e1, e2, e3), rows):
        pass


def read_half(meta, reads, direct, states):
    return pl.pallas_call(
        half_kernel,
        in_specs=[smem_spec()] + [whole_spec()] * 6,
        out_specs=whole_spec(),
        out_shape=jax.ShapeDtypeStruct((4, TOK, GROUP * DV), BF16),
        compiler_params=params(),
        cost_estimate=pl.CostEstimate(
            flops=16 * 2 * 128**3, bytes_accessed=3 * 2**20, transcendentals=0
        ),
        name="half",
    )(meta, reads, direct, *states)


def emit_kernel(meta, kept, r_ref, d_ref, e0, e1, e2, e3, out_ref, rows, sems):
    copies = []

    def put(source, n, slot, g):
        start = pl.multiple_of((meta[slot] + g) * (GROUP * DV), GROUP * DV)
        copy = pltpu.make_async_copy(
            source.at[g], out_ref.at[:, pl.ds(start, GROUP * DV)], sems.at[n]
        )
        copy.start()
        copies.append(copy)

    for g in range(4):
        put(kept, g, 1, g)
    for m, g in read_out(meta, r_ref, d_ref, (e0, e1, e2, e3), rows):
        put(rows, 4 + m, 0, g)
    for copy in copies:
        copy.wait()


def emit(meta, kept, reads, direct, states):
    return pl.pallas_call(
        emit_kernel,
        in_specs=[smem_spec()] + [whole_spec()] * 7,
        out_specs=pl.BlockSpec(memory_space=pl.ANY),
        out_shape=jax.ShapeDtypeStruct((TOK, HV * DV), BF16),
        scratch_shapes=[
            pltpu.VMEM((4, TOK, GROUP * DV), BF16),
            pltpu.SemaphoreType.DMA((8,)),
        ],
        compiler_params=params(),
        cost_estimate=pl.CostEstimate(
            flops=16 * 2 * 128**3, bytes_accessed=3 * 2**20, transcendentals=0
        ),
        name="emit",
    )(meta, kept, reads, direct, *states)


def shards(projected, conv_weight, decay_log, write_strength, starts):
    count = lax.axis_size("seq")
    me = lax.axis_index("seq")
    core, place = me & 1, (me >> 1) & 3
    slots = lax.iota(jnp.int32, 8)
    meta = jnp.zeros((8,), jnp.int32)
    for slot, value in enumerate((4 * (1 - core), 4 * core, core, place, me >> 3)):
        meta = jnp.where(slots == slot, value, meta)

    def exchange(block, bits):
        return lax.ppermute(block, "seq", [(i, i ^ bits) for i in range(count)])

    starts = starts.reshape(1, TOK)
    tail_rows = tail_of(starts, projected)
    halo = lax.ppermute(tail_rows, "seq", [(i, i + 1) for i in range(count - 1)])
    projected, conv_weight, tables, masks, shared = stage(
        decay_log, write_strength, starts, projected, conv_weight
    )
    ins = (projected, halo, conv_weight, tables, masks, shared)

    pay_s, kt_s, ef_s, *ready = send_maps(meta, *ins)
    other = exchange(pay_s, 1)
    mine, kt_k, ef_k = keep_maps(meta, *ins, *ready)
    x0, x1, x2, x3 = pair_maps(meta, mine, other)
    x3, x1, x2 = exchange(x3, 6), exchange(x1, 2), exchange(x2, 4)
    x0, own = lax.optimization_barrier((x0, mine))
    left = exchange(own, 1)
    r_k, d_k = make_reads(meta, 1, projected, halo, conv_weight, tables, kt_k, ef_k, other)
    r_s, d_s = make_reads(meta, 0, projected, halo, conv_weight, tables, kt_s, ef_s, left)
    x0, r_k, d_k, r_s, d_s = lax.optimization_barrier((x0, r_k, d_k, r_s, d_s))
    prefix, plane_map, leaving = plane_maps(meta, (x0, x1, x2, x3))
    before, far, arrived = entering_states(plane_map, leaving, count // 8)
    e0, e1, e2, e3 = spread(meta, prefix, before, far, arrived)
    e3, e1, e2 = exchange(e3, 6), exchange(e1, 2), exchange(e2, 4)
    states = (e0, e1, e2, e3)
    partner = [exchange(e, 1) for e in states]
    kept = read_half(meta, r_k, d_k, states)
    return emit(meta, kept, r_s, d_s, partner)


def solution(mesh):
    in_specs = (
        P(("groups", "seq"), None),
        P(),
        P(None, ("groups", "seq")),
        P(None, ("groups", "seq")),
        P(("groups", "seq")),
    )
    out_specs = P(("groups", "seq"), None)

    return jax.shard_map(shards, mesh=mesh, in_specs=in_specs, out_specs=out_specs, check_vma=False)
```

```python
import functools

import jax
import jax.numpy as jnp
from jax import lax
from jax.experimental import pallas as pl
from jax.experimental.pallas import tpu as pltpu
from jax.sharding import PartitionSpec as P


HK = 16
DK = 128
HV = 32
DV = 128
KW = 4
TOK = 128
NORM_EPS = 1e-06
GROUP = 4
LOG2E = 1.4426950408889634
HIDDEN = -1e30
ROWS = GROUP * DK + 16
F32 = jnp.float32
BF16 = jnp.bfloat16


def dot(a, b):
    return jnp.dot(a, b, preferred_element_type=F32)


def params(**kw):
    return pltpu.CompilerParams(vmem_limit_bytes=20 << 20, **kw)


def whole_spec():
    return pl.BlockSpec(memory_space=pltpu.VMEM)


def smem_spec():
    return pl.BlockSpec(memory_space=pltpu.SMEM)


def in_hbm(x):
    return pltpu.with_memory_space_constraint(x, pltpu.HBM)


def tail_kernel(starts_ref, x_ref, tail_ref):
    rows = x_ref.shape[0]
    flags = starts_ref[...].astype(F32)
    last = 1.0 - flags[:, TOK - 1 : TOK]
    keep = [last * (1.0 - flags[:, TOK - 2 : TOK - 1]), last, jnp.ones((1, 1), F32)]
    for r in range(KW - 1):
        row = x_ref[rows - KW + 1 + r : rows - KW + 2 + r, :].astype(F32)
        tail_ref[r : r + 1, :] = (row * keep[r]).astype(BF16)


def tail_of(starts, projected):
    channels = projected.shape[1]
    last = projected.shape[0] // 16 - 1
    return pl.pallas_call(
        tail_kernel,
        grid=(1,),
        in_specs=[
            pl.BlockSpec((1, TOK), lambda i: (0, 0)),
            pl.BlockSpec((16, channels), lambda i: (last, 0)),
        ],
        out_specs=pl.BlockSpec((KW - 1, channels), lambda i: (0, 0)),
        out_shape=jax.ShapeDtypeStruct((KW - 1, channels), BF16),
        compiler_params=params(),
        cost_estimate=pl.CostEstimate(flops=10**5, bytes_accessed=10**6, transcendentals=0),
        name="tail",
    )(in_hbm(starts), in_hbm(projected))


def write_tables(decay_ref, beta_ref, starts_ref, out_ref):
    src, dst = positions()
    cum = LOG2E * jnp.dot(
        decay_ref[...],
        (src <= dst).astype(F32),
        precision=lax.Precision.HIGHEST,
        preferred_element_type=F32,
    )
    flags = jnp.broadcast_to(starts_ref[...].astype(F32), (8, TOK)).astype(BF16)
    episode = [dot(flags, (src + j <= dst).astype(BF16))[0:1] for j in range(KW)]
    usable = [(episode[0] == episode[j]).astype(F32) for j in range(1, KW)]
    living = (episode[0] == 0.0).astype(F32)
    zero = jnp.zeros((1, TOK), F32)
    shared = jnp.concatenate(usable + [episode[0], living, zero, zero, zero], axis=0)
    for pair in range(HV // GROUP):
        out_ref[pair, 0:4, :] = cum[GROUP * pair : GROUP * (pair + 1)]
        out_ref[pair, 4:8, :] = beta_ref[GROUP * pair : GROUP * (pair + 1), :]
        out_ref[pair, 8:16, :] = shared


def place_window(x, halo, xs, first):
    cols = slice(first, first + x.shape[1])
    xs[8 : 8 + TOK, cols] = x.astype(F32)
    xs[8 - KW + 1 : 8, cols] = halo.astype(F32)


def convolve_piece(xs, first, taps, usable):
    here = slice(first, first + 128)
    total = xs[8 : 8 + TOK, here] * taps[3:4]
    for j in range(1, KW):
        total = total + (xs[8 - j : 8 - j + TOK, here] * usable[j - 1]) * taps[3 - j : 4 - j]
    return (total / (1.0 + jnp.exp2(total * -LOG2E))).astype(BF16)


def column(cols, lane):
    return jnp.broadcast_to(cols[:, lane : lane + 1], (TOK, 128))


def positions():
    i = lax.broadcasted_iota(jnp.int32, (TOK, TOK), 0)
    j = lax.broadcasted_iota(jnp.int32, (TOK, TOK), 1)
    return i, j


def hidden_where(rows, cols):
    i, j = positions()
    seen = (column(cols, 11) == rows[11:12, :]) & (i >= j)
    return jnp.where(seen, 0.0, HIDDEN)


def decay_within(rows, clock, head, hidden):
    return jnp.exp2((clock - rows[head : head + 1, :]) + hidden)


def unit(x, scale=1.0):
    return lax.rsqrt(jnp.sum(x * x, axis=-1, keepdims=True) + NORM_EPS) * scale


def split_rows(x):
    pieces, rest = [], list(x)
    for _ in range(3):
        highs = [c.astype(BF16).astype(F32) for c in rest]
        pieces += highs
        rest = [c - high for c, high in zip(rest, highs)]
    pieces.append(jnp.zeros((4, 256), F32))
    return jnp.concatenate(pieces, axis=0).astype(BF16)


LEVELS = 7
HEADS = 8


def odd_rows(get, size):
    return jnp.concatenate([get(r, r + size) for r in range(size, TOK, 2 * size)], axis=0)


def stage_kernel(
    decay_hbm, beta_hbm, starts_hbm, x_hbm, w_hbm, x_out, w_out, tab_ref, masks, shared,
    decay_ref, beta_ref, starts_ref, sems,
):
    moves = [
        (decay_hbm, decay_ref),
        (beta_hbm, beta_ref),
        (starts_hbm, starts_ref),
        (x_hbm, x_out),
        (w_hbm, w_out),
    ]
    copies = [pltpu.make_async_copy(*move, sems.at[n]) for n, move in enumerate(moves)]
    for copy in copies:
        copy.start()
    for copy in copies[:3]:
        copy.wait()
    write_tables(decay_ref, beta_ref, starts_ref, tab_ref)
    rows = tab_ref[0]
    cols = jnp.transpose(rows)
    for j in range(KW - 1):
        shared[j] = column(cols, 8 + j)
    shared[3] = column(cols, 12)
    shared[4] = hidden_where(rows, cols)
    i, j = positions()
    apart = i ^ j
    for level in range(LEVELS):
        masks[level] = (((apart >> level) == 1) & (i > j)).astype(F32).astype(BF16)
    shared[5] = (i > j).astype(F32)
    masks[LEVELS] = (i == j).astype(F32).astype(BF16)
    for copy in copies[3:]:
        copy.wait()


def stage(decay_log, write_strength, starts, projected, conv_weight):
    return pl.pallas_call(
        stage_kernel,
        in_specs=[pl.BlockSpec(memory_space=pl.ANY)] * 5,
        out_specs=[whole_spec()] * 5,
        out_shape=[
            jax.ShapeDtypeStruct(projected.shape, BF16),
            jax.ShapeDtypeStruct(conv_weight.shape, BF16),
            jax.ShapeDtypeStruct((HV // GROUP, 16, TOK), F32),
            jax.ShapeDtypeStruct((LEVELS + 1, TOK, TOK), BF16),
            jax.ShapeDtypeStruct((6, TOK, 128), F32),
        ],
        scratch_shapes=[
            pltpu.VMEM((HV, TOK), F32),
            pltpu.VMEM((HV, TOK), F32),
            pltpu.VMEM((1, TOK), jnp.int32),
            pltpu.SemaphoreType.DMA((5,)),
        ],
        compiler_params=params(),
        cost_estimate=pl.CostEstimate(flops=10**7, bytes_accessed=4 * 2**20, transcendentals=0),
        name="stage",
    )(
        in_hbm(decay_log),
        in_hbm(write_strength),
        in_hbm(starts),
        in_hbm(projected),
        in_hbm(conv_weight),
    )


def preparing(pair, ins, xs, sys, right, keys):
    x_ref, halo_ref, w_ref, tab_ref, _, shared = ins
    k_at = pl.multiple_of(HK * DK + pair * 256, 512)
    v_at = pl.multiple_of(2 * HK * DK + pair * 512, 1024)
    kt_ref, kt_at = keys

    def usable():
        return [shared[j] for j in range(KW - 1)]

    def place():
        place_window(x_ref[:, pl.ds(k_at, 512)], halo_ref[:, pl.ds(k_at, 512)], xs, 0)
        place_window(x_ref[:, pl.ds(v_at, 1024)], halo_ref[:, pl.ds(v_at, 1024)], xs, 512)

    def key(n):
        p, a = n // 2, n % 2
        rows = tab_ref[pair + p]
        cols = jnp.transpose(rows)
        at = n * DK
        taps = w_ref[:, pl.ds(k_at + at, DK)].astype(F32)
        k = convolve_piece(xs, at, taps, usable()).astype(F32)
        k = k * unit(k)
        kb = k.astype(BF16)
        ktb = jnp.transpose(kb.astype(F32)).astype(BF16)
        kt_ref[kt_at + p, a * DK : (a + 1) * DK, :] = ktb
        inner = dot(kb, ktb) * shared[5]
        for b in range(2):
            lane = 2 * a + b
            h = GROUP * p + lane
            clock = column(cols, lane)
            within = decay_within(rows, clock, lane, shared[4])
            carried = jnp.exp2(clock) * shared[3]
            sys[h] = ((column(cols, 4 + lane) * within) * inner).astype(BF16)
            right[h, :, 0:DK] = (carried * k).astype(BF16)

    def value(h):
        taps = w_ref[:, pl.ds(v_at + h * DV, DV)].astype(F32)
        right[h, :, DK : DK + DV] = convolve_piece(xs, 512 + h * DV, taps, usable())

    steps = [place]
    steps += [functools.partial(key, n) for n in range(4)]
    steps += [functools.partial(value, h) for h in range(HEADS)]
    return steps


def solving(pair, ins, sys, right, keys, inv, pay_ref, ef_ref, at, kt_copy=None):
    tab_ref, masks, shared = ins[3:]
    kt_ref, kt_at = keys
    kept = {}

    def begin():
        for h in range(HEADS):
            inv[h] = masks[LEVELS] - sys[h] * masks[0]

    def first_product(level):
        size = 1 << level
        kept["steps"] = []
        for h in range(HEADS):
            if size < 16:
                left = sys[h]
            else:
                left = odd_rows(lambda r, e: sys[h, r:e, :], size)
            kept["steps"].append(dot(left, inv[h]).astype(BF16))

    def second_product(level):
        size = 1 << level
        steps = kept["steps"]
        if size < 16:
            steps = [dot(inv[h], steps[h]).astype(BF16) for h in range(HEADS)]
            for h in range(HEADS):
                inv[h] = inv[h] - steps[h] * masks[level]
            return
        blank = jnp.zeros((size, 128), BF16)
        found = []
        for h in range(HEADS):
            expanded = []
            for r in range(0, TOK // 2, size):
                expanded += [blank, steps[h][r : r + size]]
            left = odd_rows(lambda r, e: inv[h, r:e, :], size)
            found.append(dot(left, jnp.concatenate(expanded, axis=0)).astype(BF16))
        for h in range(HEADS):
            for n, r in enumerate(range(size, TOK, 2 * size)):
                inv[h, r : r + size, :] = inv[h, r : r + size, :] - (
                    found[h][n * size : (n + 1) * size] * masks[level, r : r + size, :]
                )

    def check():
        kept["gaps"] = []
        for h in range(HEADS):
            rough = inv[h]
            product = dot(sys[h], rough)
            kept["gaps"].append(
                ((masks[LEVELS].astype(F32) - rough.astype(F32)) - product).astype(BF16)
            )

    def row(h, n):
        return tab_ref[pair + h // GROUP, n : n + 1, :]

    def correct():
        for h in range(HEADS):
            fixed = inv[h].astype(F32) + dot(inv[h], kept["gaps"][h])
            inv[h] = (fixed * row(h, 4 + h % GROUP)).astype(BF16)

    def apply():
        kept["ef"] = []
        for h in range(HEADS):
            ef = dot(inv[h], right[h]).astype(BF16)
            here = slice((h % GROUP) * TOK, (h % GROUP + 1) * TOK)
            ef_ref[at + h // GROUP, here, :] = ef
            kept["ef"].append(ef)

    def write():
        last = []
        for h in range(HEADS):
            g, n = h // GROUP, h % GROUP
            ktb = kt_ref[kt_at + g, (n // 2) * DK : (n // 2 + 1) * DK, :]
            if kt_copy is not None and n % 2 == 0:
                kt_copy[at + g, (n // 2) * DK : (n // 2 + 1) * DK, :] = ktb
            clock = row(h, n)
            final = jnp.broadcast_to(clock[:, TOK - 1 : TOK], (1, TOK))
            ending = jnp.exp2((final - clock) + shared[4, TOK - 1 : TOK, :])
            carried = jnp.exp2(final) * shared[3, TOK - 1 : TOK, :]
            last.append(jnp.concatenate([carried, carried], axis=1))
            weighted = (ktb.astype(F32) * ending).astype(BF16)
            pay_ref[at + g, n * DK : (n + 1) * DK, :] = dot(weighted, kept["ef"][h]).astype(BF16)
        for g in range(2):
            pay_ref[at + g, GROUP * DK : ROWS, :] = split_rows(last[GROUP * g : GROUP * (g + 1)])

    steps = [begin]
    for level in range(1, LEVELS):
        steps.append(functools.partial(first_product, level))
        steps.append(functools.partial(second_product, level))
    return steps + [check, correct, apply, write]


def interleave(main, side):
    done = 0
    for n, step in enumerate(main):
        step()
        due = ((n + 1) * len(side) + len(main) - 1) // len(main)
        while done < min(due, len(side)):
            side[done]()
            done += 1


def send_kernel(
    meta, x_ref, halo_ref, w_ref, tab_ref, masks, shared, pay_ref, kt_ref, ef_ref, sys_out,
    right_out, kt_out, xs, sys, right, inv,
):
    ins = (x_ref, halo_ref, w_ref, tab_ref, masks, shared)
    pair, after = meta[0], meta[1]
    sets = [(sys.at[n], right.at[n], (kt_ref, 2 * n)) for n in range(2)]
    third = (sys_out, right_out, (kt_out, 0))
    for step in preparing(pair, ins, xs, *sets[0]):
        step()
    for n in range(2):
        main = solving(pair + 2 * n, ins, *sets[n], inv, pay_ref, ef_ref, 2 * n)
        if n == 0:
            side = preparing(pair + 2, ins, xs, *sets[1])
        else:
            side = preparing(after, ins, xs, *third)
        interleave(main, side)


def keep_kernel(
    meta, x_ref, halo_ref, w_ref, tab_ref, masks, shared, sys_in, right_in, kt_in, pay_ref,
    kt_ref, ef_ref, xs, sys, right, inv,
):
    ins = (x_ref, halo_ref, w_ref, tab_ref, masks, shared)
    pair = meta[1]
    own = (sys, right, (kt_ref, 2))
    interleave(
        solving(pair, ins, sys_in, right_in, (kt_in, 0), inv, pay_ref, ef_ref, 0, kt_ref),
        preparing(pair + 2, ins, xs, *own),
    )
    for step in solving(pair + 2, ins, *own, inv, pay_ref, ef_ref, 2):
        step()


def map_shapes():
    return [
        jax.ShapeDtypeStruct((4, ROWS, 256), BF16),
        jax.ShapeDtypeStruct((4, 2 * DK, TOK), BF16),
        jax.ShapeDtypeStruct((4, GROUP * TOK, 256), BF16),
    ]


def ready_shapes():
    return [
        jax.ShapeDtypeStruct((HEADS, TOK, TOK), BF16),
        jax.ShapeDtypeStruct((HEADS, TOK, 256), BF16),
        jax.ShapeDtypeStruct((2, 2 * DK, TOK), BF16),
    ]


def map_cost():
    return pl.CostEstimate(
        flops=16 * 20 * 2 * 128**3, bytes_accessed=5 * 2**20, transcendentals=10**6
    )


def send_maps(meta, *ins):
    return pl.pallas_call(
        send_kernel,
        in_specs=[smem_spec()] + [whole_spec()] * len(ins),
        out_specs=[whole_spec()] * 6,
        out_shape=map_shapes() + ready_shapes(),
        scratch_shapes=[
            pltpu.VMEM((8 + TOK, 1536), F32),
            pltpu.VMEM((2, HEADS, TOK, TOK), BF16),
            pltpu.VMEM((2, HEADS, TOK, 256), BF16),
            pltpu.VMEM((HEADS, TOK, TOK), BF16),
        ],
        compiler_params=params(),
        cost_estimate=map_cost(),
        name="send_maps",
    )(meta, *ins)


def keep_maps(meta, *ins):
    return pl.pallas_call(
        keep_kernel,
        in_specs=[smem_spec()] + [whole_spec()] * len(ins),
        out_specs=[whole_spec()] * 3,
        out_shape=map_shapes(),
        scratch_shapes=[
            pltpu.VMEM((8 + TOK, 1536), F32),
            pltpu.VMEM((HEADS, TOK, TOK), BF16),
            pltpu.VMEM((HEADS, TOK, 256), BF16),
            pltpu.VMEM((HEADS, TOK, TOK), BF16),
        ],
        compiler_params=params(),
        cost_estimate=map_cost(),
        name="keep_maps",
    )(meta, *ins)


def read_kernel(meta, xq_ref, hq_ref, wq_ref, rows_ref, kt_ref, ef_ref, left_ref, r_ref, d_ref, xs):
    first = meta[2] == 0
    tail = left_ref[0, GROUP * DK : ROWS, :]
    rows = rows_ref[0]
    cols = jnp.transpose(rows)
    usable = [column(cols, 8 + j) for j in range(KW - 1)]
    living = column(cols, 12)
    hidden = hidden_where(rows, cols)
    place_window(xq_ref[...], hq_ref[...], xs, 0)
    taps = wq_ref[...].astype(F32)
    for a in range(2):
        queries = convolve_piece(xs, a * DK, taps[:, a * DK : (a + 1) * DK], usable)
        q = queries.astype(F32)
        scale = unit(q, DK ** (-0.5))
        inner = dot(queries, kt_ref[0, a * DK : (a + 1) * DK, :])
        for b in range(2):
            h = 2 * a + b
            clock = column(cols, h)
            scores = (inner * decay_within(rows, clock, h, hidden)).astype(BF16)
            both = dot(scores, ef_ref[0, h * TOK : (h + 1) * TOK, :])
            carried = jnp.exp2(clock) * living
            mine = slice(h * TOK, (h + 1) * TOK)
            reader = (carried * q - both[:, :DK]) * scale
            direct = both[:, DK:] * scale
            moved = dot(reader.astype(BF16), left_ref[0, h * DK : (h + 1) * DK, :])
            c = factor(tail, h)[:, :DK]
            r_ref[0, mine, :] = jnp.where(first, reader, c * reader - moved[:, :DK]).astype(BF16)
            d_ref[0, mine, :] = jnp.where(first, direct, direct + moved[:, DK:])


def make_reads(meta, slot, projected, halo, conv_weight, tables, keys_t, ef, left):
    def at(i, m):
        return (0, m[slot] + i)

    return pl.pallas_call(
        read_kernel,
        grid_spec=pltpu.PrefetchScalarGridSpec(
            num_scalar_prefetch=1,
            grid=(4,),
            in_specs=[
                pl.BlockSpec((TOK, 256), at),
                pl.BlockSpec((KW - 1, 256), at),
                pl.BlockSpec((KW, 256), at),
                pl.BlockSpec((1, 16, TOK), lambda i, m: (m[slot] + i, 0, 0)),
                pl.BlockSpec((1, 2 * DK, TOK), lambda i, m: (i, 0, 0)),
                pl.BlockSpec((1, GROUP * TOK, 256), lambda i, m: (i, 0, 0)),
                pl.BlockSpec((1, ROWS, 256), lambda i, m: (i, 0, 0)),
            ],
            out_specs=[
                pl.BlockSpec((1, GROUP * TOK, DK), lambda i, m: (i, 0, 0)),
                pl.BlockSpec((1, GROUP * TOK, DV), lambda i, m: (i, 0, 0)),
            ],
            scratch_shapes=[pltpu.VMEM((8 + TOK, 256), F32)],
        ),
        out_shape=[
            jax.ShapeDtypeStruct((4, GROUP * TOK, DK), BF16),
            jax.ShapeDtypeStruct((4, GROUP * TOK, DV), F32),
        ],
        compiler_params=params(),
        cost_estimate=pl.CostEstimate(
            flops=16 * 6 * 2 * 128**3, bytes_accessed=5 * 2**20, transcendentals=10**6
        ),
        name="reads",
    )(meta, projected, halo, conv_weight, tables, keys_t, ef, left)


def factor(tail, head):
    tail = tail.astype(F32)
    return (tail[head : head + 1] + tail[4 + head : 5 + head]) + tail[8 + head : 9 + head]


def compose(left, left_c, right, right_c):
    right_d = right[:, :DK]
    product = dot(right_d.astype(BF16), left.astype(BF16))
    return (
        right_c * left.astype(F32)
        + jnp.concatenate(
            [left_c[:, :DK] * right_d.astype(F32), right[:, DK:].astype(F32)], axis=1
        )
        - product
    )


def apply_map(each, c, state):
    product = dot(each[:, :DK], state)
    return c[:, :DK] * state.astype(F32) + each[:, DK:].astype(F32) - product


def pair_kernel(meta, mine_ref, other_ref, *out_refs):
    def combine(left_ref, right_ref):
        for m, out_ref in enumerate(out_refs):
            g = meta[3] ^ m
            left_tail = left_ref[g, GROUP * DK : ROWS, :]
            right_tail = right_ref[g, GROUP * DK : ROWS, :]
            factors = []
            for h in range(GROUP):
                here = slice(h * DK, (h + 1) * DK)
                left_c, right_c = factor(left_tail, h), factor(right_tail, h)
                both = compose(left_ref[g, here, :], left_c, right_ref[g, here, :], right_c)
                out_ref[here, :] = both.astype(BF16)
                factors.append(left_c * right_c)
            out_ref[GROUP * DK : ROWS, :] = split_rows(factors)

    pl.when(meta[2] == 0)(lambda: combine(mine_ref, other_ref))
    pl.when(meta[2] != 0)(lambda: combine(other_ref, mine_ref))


def pair_maps(meta, mine, other):
    return pl.pallas_call(
        pair_kernel,
        in_specs=[smem_spec(), whole_spec(), whole_spec()],
        out_specs=[whole_spec()] * 4,
        out_shape=[jax.ShapeDtypeStruct((ROWS, 256), BF16)] * 4,
        compiler_params=params(),
        cost_estimate=pl.CostEstimate(
            flops=16 * 2 * 2 * 128**3, bytes_accessed=3 * 2**20, transcendentals=0
        ),
        name="pair",
    )(meta, mine, other)


def by_place(meta, body):
    for place in range(4):
        pl.when(meta[3] == place)(functools.partial(body, place))


def plane_kernel(meta, x0, x1, x2, x3, prefix_ref, plane_ref, exit_ref):
    pieces = (x0, x1, x2, x3)
    prefix_ref[0] = jnp.zeros((ROWS, 256), BF16)

    def chain(place):
        maps = [pieces[place ^ a] for a in range(4)]
        prefix_ref[1] = maps[0][...]
        run = [maps[0][h * DK : (h + 1) * DK, :].astype(F32) for h in range(GROUP)]
        run_c = [factor(maps[0][GROUP * DK : ROWS, :], h) for h in range(GROUP)]
        for a in range(1, 4):
            tail = maps[a][GROUP * DK : ROWS, :]
            for h in range(GROUP):
                here = slice(h * DK, (h + 1) * DK)
                c = factor(tail, h)
                run[h] = compose(run[h], run_c[h], maps[a][here, :], c)
                run_c[h] = run_c[h] * c
                if a < 3:
                    prefix_ref[a + 1, here, :] = run[h].astype(BF16)
                else:
                    plane_ref[here, :] = run[h].astype(BF16)
                    exit_ref[here, :] = run[h][:, DK:].astype(BF16)
            if a < 3:
                prefix_ref[a + 1, GROUP * DK : ROWS, :] = split_rows(run_c)
        plane_ref[GROUP * DK : ROWS, :] = split_rows(run_c)

    by_place(meta, chain)


def plane_maps(meta, pieces):
    return pl.pallas_call(
        plane_kernel,
        in_specs=[smem_spec()] + [whole_spec()] * 4,
        out_specs=[whole_spec()] * 3,
        out_shape=[
            jax.ShapeDtypeStruct((4, ROWS, 256), BF16),
            jax.ShapeDtypeStruct((ROWS, 256), BF16),
            jax.ShapeDtypeStruct((GROUP * DK, DV), BF16),
        ],
        compiler_params=params(),
        cost_estimate=pl.CostEstimate(
            flops=12 * 2 * 2 * 128**3, bytes_accessed=2 * 2**20, transcendentals=0
        ),
        name="plane",
    )(meta, *pieces)


def hop_kernel(plane_ref, state_ref, out_ref):
    tail = plane_ref[GROUP * DK : ROWS, :]
    for h in range(GROUP):
        here = slice(h * DK, (h + 1) * DK)
        state = apply_map(plane_ref[here, :], factor(tail, h), state_ref[here, :])
        out_ref[here, :] = state.astype(BF16)


def hop(plane_map, state):
    return pl.pallas_call(
        hop_kernel,
        in_specs=[whole_spec()] * 2,
        out_specs=whole_spec(),
        out_shape=jax.ShapeDtypeStruct((GROUP * DK, DV), BF16),
        compiler_params=params(),
        cost_estimate=pl.CostEstimate(
            flops=4 * 2 * 128**3, bytes_accessed=2**19, transcendentals=0
        ),
        name="hop",
    )(plane_map, state)


def spread_kernel(meta, prefix_ref, before_ref, far_ref, *refs):
    out_refs = refs[-4:]
    state_refs = refs[:-4]
    before_tail = before_ref[GROUP * DK : ROWS, :]

    def send(place):
        for h in range(GROUP):
            here = slice(h * DK, (h + 1) * DK)
            state = apply_map(before_ref[here, :], factor(before_tail, h), far_ref[here, :])
            state = state.astype(BF16)
            for ref in state_refs:
                state = state + ref[here, :]
            out_refs[place][here, :] = state
            for a in range(1, 4):
                c = factor(prefix_ref[a, GROUP * DK : ROWS, :], h)
                after = apply_map(prefix_ref[a, here, :], c, state)
                out_refs[place ^ a][here, :] = after.astype(BF16)

    by_place(meta, send)


def spread(meta, prefix, before, far, states):
    return pl.pallas_call(
        spread_kernel,
        in_specs=[smem_spec()] + [whole_spec()] * (3 + len(states)),
        out_specs=[whole_spec()] * 4,
        out_shape=[jax.ShapeDtypeStruct((GROUP * DK, DV), BF16)] * 4,
        compiler_params=params(),
        cost_estimate=pl.CostEstimate(
            flops=20 * 2 * 128**3, bytes_accessed=2**21, transcendentals=0
        ),
        name="spread",
    )(meta, prefix, before, far, *states)


def entering_states(plane_map, leaving, planes):
    def ahead(block, plane, distance=1):
        members = range(8 * plane, 8 * plane + 8)
        return lax.ppermute(block, "seq", [(i, i + 8 * distance) for i in members])

    if planes == 4:
        first = ahead(leaving, 0)
        before = ahead(plane_map, 2)
        second = hop(plane_map, first)
        far = ahead(second, 1, 2)
        near = ahead(second, 1)
        return before, far, [first, near]
    states = []
    for plane in range(planes - 1):
        state = ahead(leaving, plane)
        states.append(state)
        if plane < planes - 2:
            leaving = hop(plane_map, state)
    return jnp.zeros_like(plane_map), jnp.zeros_like(leaving), states


def read_group(g, parts, out):
    for n, (r_ref, d_ref, e_ref) in enumerate(parts):
        for h in range(GROUP):
            here = slice(h * TOK, (h + 1) * TOK)
            total = dot(r_ref[g, here, :], e_ref[here, :]) + d_ref[g, here, :]
            out[n, :, h * DV : (h + 1) * DV] = total.astype(BF16)


def group_kernel(m, meta, r_k, d_k, e_k, r_s, d_s, e_s, out):
    read_group(meta[3] ^ m, ((r_k, d_k, e_k), (r_s, d_s, e_s)), out)


def group_cost():
    return pl.CostEstimate(flops=8 * 2 * 128**3, bytes_accessed=2**20, transcendentals=0)


def read_out(m, meta, *parts):
    return pl.pallas_call(
        functools.partial(group_kernel, m),
        in_specs=[smem_spec()] + [whole_spec()] * 6,
        out_specs=whole_spec(),
        out_shape=jax.ShapeDtypeStruct((2, TOK, GROUP * DV), BF16),
        compiler_params=params(),
        cost_estimate=group_cost(),
        name="group",
    )(meta, *parts)


def emit_kernel(meta, g0, g1, g2, r_k, d_k, e_k, r_s, d_s, e_s, out_ref, rows, sems):
    copies = []

    def put(source, m):
        g = meta[3] ^ m
        for n in range(2):
            start = pl.multiple_of((meta[1 - n] + g) * (GROUP * DV), GROUP * DV)
            copy = pltpu.make_async_copy(
                source.at[n], out_ref.at[:, pl.ds(start, GROUP * DV)], sems.at[2 * m + n]
            )
            copy.start()
            copies.append(copy)

    for m, group in enumerate((g0, g1, g2)):
        put(group, m)
    read_group(meta[3] ^ 3, ((r_k, d_k, e_k), (r_s, d_s, e_s)), rows)
    put(rows, 3)
    for copy in copies:
        copy.wait()


def emit(meta, *parts):
    return pl.pallas_call(
        emit_kernel,
        in_specs=[smem_spec()] + [whole_spec()] * 9,
        out_specs=pl.BlockSpec(memory_space=pl.ANY),
        out_shape=jax.ShapeDtypeStruct((TOK, HV * DV), BF16),
        scratch_shapes=[
            pltpu.VMEM((2, TOK, GROUP * DV), BF16),
            pltpu.SemaphoreType.DMA((8,)),
        ],
        compiler_params=params(),
        cost_estimate=group_cost(),
        name="emit",
    )(meta, *parts)


def shards(projected, conv_weight, decay_log, write_strength, starts):
    count = lax.axis_size("seq")
    me = lax.axis_index("seq")
    core, place = me & 1, (me >> 1) & 3
    slots = lax.iota(jnp.int32, 8)
    meta = jnp.zeros((8,), jnp.int32)
    for slot, value in enumerate((4 * (1 - core), 4 * core, core, place, me >> 3)):
        meta = jnp.where(slots == slot, value, meta)

    def exchange(block, bits):
        return lax.ppermute(block, "seq", [(i, i ^ bits) for i in range(count)])

    starts = starts.reshape(1, TOK)
    tail_rows = tail_of(starts, projected)
    halo = lax.ppermute(tail_rows, "seq", [(i, i + 1) for i in range(count - 1)])
    projected, conv_weight, tables, masks, shared = stage(
        decay_log, write_strength, starts, projected, conv_weight
    )
    ins = (projected, halo, conv_weight, tables, masks, shared)

    pay_s, kt_s, ef_s, *ready = send_maps(meta, *ins)
    other = exchange(pay_s, 1)
    mine, kt_k, ef_k = keep_maps(meta, *ins, *ready)
    x0, x1, x2, x3 = pair_maps(meta, mine, other)
    x3, x1, x2 = exchange(x3, 6), exchange(x1, 2), exchange(x2, 4)
    x0, own = lax.optimization_barrier((x0, mine))
    left = exchange(own, 1)
    r_k, d_k = make_reads(meta, 1, projected, halo, conv_weight, tables, kt_k, ef_k, other)
    r_s, d_s = make_reads(meta, 0, projected, halo, conv_weight, tables, kt_s, ef_s, left)
    x0, r_k, d_k, r_s, d_s = lax.optimization_barrier((x0, r_k, d_k, r_s, d_s))
    prefix, plane_map, leaving = plane_maps(meta, (x0, x1, x2, x3))
    before, far, arrived = entering_states(plane_map, leaving, count // 8)
    e0, e1, e2, e3 = spread(meta, prefix, before, far, arrived)
    states = [e0, e1, e2, e3]
    for m in range(1, 4):
        states[m] = exchange(states[m], 2 * m)
    partner = [exchange(e, 1) for e in states]
    groups = []
    for m in range(3):
        groups.append(read_out(m, meta, r_k, d_k, states[m], r_s, d_s, partner[m]))
    return emit(meta, *groups, r_k, d_k, states[3], r_s, d_s, partner[3])


def solution(mesh):
    in_specs = (
        P(("groups", "seq"), None),
        P(),
        P(None, ("groups", "seq")),
        P(None, ("groups", "seq")),
        P(("groups", "seq")),
    )
    out_specs = P(("groups", "seq"), None)

    return jax.shard_map(shards, mesh=mesh, in_specs=in_specs, out_specs=out_specs, check_vma=False)
```

```python
import functools

import jax
import jax.numpy as jnp
from jax import lax
from jax.experimental import pallas as pl
from jax.experimental.pallas import tpu as pltpu
from jax.sharding import PartitionSpec as P


HK = 16
DK = 128
HV = 32
DV = 128
KW = 4
TOK = 128
NORM_EPS = 1e-06
GROUP = 4
LOG2E = 1.4426950408889634
HIDDEN = -1e30
ROWS = GROUP * DK + 16
F32 = jnp.float32
BF16 = jnp.bfloat16


def dot(a, b):
    return jnp.dot(a, b, preferred_element_type=F32)


def params(**kw):
    return pltpu.CompilerParams(vmem_limit_bytes=20 << 20, **kw)


def whole_spec():
    return pl.BlockSpec(memory_space=pltpu.VMEM)


def smem_spec():
    return pl.BlockSpec(memory_space=pltpu.SMEM)


def in_hbm(x):
    return pltpu.with_memory_space_constraint(x, pltpu.HBM)


def tail_kernel(starts_ref, x_ref, tail_ref):
    rows = x_ref.shape[0]
    flags = starts_ref[...].astype(F32)
    last = 1.0 - flags[:, TOK - 1 : TOK]
    keep = [last * (1.0 - flags[:, TOK - 2 : TOK - 1]), last, jnp.ones((1, 1), F32)]
    for r in range(KW - 1):
        row = x_ref[rows - KW + 1 + r : rows - KW + 2 + r, :].astype(F32)
        tail_ref[r : r + 1, :] = (row * keep[r]).astype(BF16)


def tail_of(starts, projected):
    channels = projected.shape[1]
    last = projected.shape[0] // 16 - 1
    return pl.pallas_call(
        tail_kernel,
        grid=(1,),
        in_specs=[
            pl.BlockSpec((1, TOK), lambda i: (0, 0)),
            pl.BlockSpec((16, channels), lambda i: (last, 0)),
        ],
        out_specs=pl.BlockSpec((KW - 1, channels), lambda i: (0, 0)),
        out_shape=jax.ShapeDtypeStruct((KW - 1, channels), BF16),
        compiler_params=params(),
        cost_estimate=pl.CostEstimate(flops=10**5, bytes_accessed=10**6, transcendentals=0),
        name="tail",
    )(in_hbm(starts), in_hbm(projected))


def write_tables(decay_ref, beta_ref, starts_ref, out_ref):
    src, dst = positions()
    cum = LOG2E * jnp.dot(
        decay_ref[...],
        (src <= dst).astype(F32),
        precision=lax.Precision.HIGHEST,
        preferred_element_type=F32,
    )
    flags = jnp.broadcast_to(starts_ref[...].astype(F32), (8, TOK)).astype(BF16)
    episode = [dot(flags, (src + j <= dst).astype(BF16))[0:1] for j in range(KW)]
    usable = [(episode[0] == episode[j]).astype(F32) for j in range(1, KW)]
    living = (episode[0] == 0.0).astype(F32)
    zero = jnp.zeros((1, TOK), F32)
    shared = jnp.concatenate(usable + [episode[0], living, zero, zero, zero], axis=0)
    for pair in range(HV // GROUP):
        out_ref[pair, 0:4, :] = cum[GROUP * pair : GROUP * (pair + 1)]
        out_ref[pair, 4:8, :] = beta_ref[GROUP * pair : GROUP * (pair + 1), :]
        out_ref[pair, 8:16, :] = shared


def place_window(x, halo, xs, first):
    cols = slice(first, first + x.shape[1])
    xs[8 : 8 + TOK, cols] = x.astype(F32)
    xs[8 - KW + 1 : 8, cols] = halo.astype(F32)


def convolve_piece(xs, first, taps, usable):
    here = slice(first, first + 128)
    total = xs[8 : 8 + TOK, here] * taps[3:4]
    for j in range(1, KW):
        total = total + (xs[8 - j : 8 - j + TOK, here] * usable[j - 1]) * taps[3 - j : 4 - j]
    return (total / (1.0 + jnp.exp2(total * -LOG2E))).astype(BF16)


def column(cols, lane):
    return jnp.broadcast_to(cols[:, lane : lane + 1], (TOK, 128))


def positions():
    i = lax.broadcasted_iota(jnp.int32, (TOK, TOK), 0)
    j = lax.broadcasted_iota(jnp.int32, (TOK, TOK), 1)
    return i, j


def hidden_where(rows, cols):
    i, j = positions()
    seen = (column(cols, 11) == rows[11:12, :]) & (i >= j)
    return jnp.where(seen, 0.0, HIDDEN)


def decay_within(rows, clock, head, hidden):
    return jnp.exp2((clock - rows[head : head + 1, :]) + hidden)


def unit(x, scale=1.0):
    return lax.rsqrt(jnp.sum(x * x, axis=-1, keepdims=True) + NORM_EPS) * scale


def split_rows(x):
    pieces, rest = [], list(x)
    for _ in range(3):
        highs = [c.astype(BF16).astype(F32) for c in rest]
        pieces += highs
        rest = [c - high for c, high in zip(rest, highs)]
    pieces.append(jnp.zeros((4, 256), F32))
    return jnp.concatenate(pieces, axis=0).astype(BF16)


LEVELS = 7
HEADS = 8


def odd_rows(get, size):
    return jnp.concatenate([get(r, r + size) for r in range(size, TOK, 2 * size)], axis=0)


def stage_kernel(
    decay_hbm, beta_hbm, starts_hbm, x_hbm, w_hbm, x_out, w_out, tab_ref, masks, shared,
    decay_ref, beta_ref, starts_ref, sems,
):
    moves = [
        (decay_hbm, decay_ref),
        (beta_hbm, beta_ref),
        (starts_hbm, starts_ref),
        (x_hbm, x_out),
        (w_hbm, w_out),
    ]
    copies = [pltpu.make_async_copy(*move, sems.at[n]) for n, move in enumerate(moves)]
    for copy in copies:
        copy.start()
    for copy in copies[:3]:
        copy.wait()
    write_tables(decay_ref, beta_ref, starts_ref, tab_ref)
    rows = tab_ref[0]
    cols = jnp.transpose(rows)
    for j in range(KW - 1):
        shared[j] = column(cols, 8 + j)
    shared[3] = column(cols, 12)
    shared[4] = hidden_where(rows, cols)
    i, j = positions()
    apart = i ^ j
    for level in range(LEVELS):
        masks[level] = (((apart >> level) == 1) & (i > j)).astype(F32).astype(BF16)
    shared[5] = (i > j).astype(F32)
    masks[LEVELS] = (i == j).astype(F32).astype(BF16)
    for copy in copies[3:]:
        copy.wait()


def stage(decay_log, write_strength, starts, projected, conv_weight):
    return pl.pallas_call(
        stage_kernel,
        in_specs=[pl.BlockSpec(memory_space=pl.ANY)] * 5,
        out_specs=[whole_spec()] * 5,
        out_shape=[
            jax.ShapeDtypeStruct(projected.shape, BF16),
            jax.ShapeDtypeStruct(conv_weight.shape, BF16),
            jax.ShapeDtypeStruct((HV // GROUP, 16, TOK), F32),
            jax.ShapeDtypeStruct((LEVELS + 1, TOK, TOK), BF16),
            jax.ShapeDtypeStruct((6, TOK, 128), F32),
        ],
        scratch_shapes=[
            pltpu.VMEM((HV, TOK), F32),
            pltpu.VMEM((HV, TOK), F32),
            pltpu.VMEM((1, TOK), jnp.int32),
            pltpu.SemaphoreType.DMA((5,)),
        ],
        compiler_params=params(),
        cost_estimate=pl.CostEstimate(flops=10**7, bytes_accessed=4 * 2**20, transcendentals=0),
        name="stage",
    )(
        in_hbm(decay_log),
        in_hbm(write_strength),
        in_hbm(starts),
        in_hbm(projected),
        in_hbm(conv_weight),
    )


def preparing(pair, ins, xs, sys, right, keys):
    x_ref, halo_ref, w_ref, tab_ref, _, shared = ins
    k_at = pl.multiple_of(HK * DK + pair * 256, 512)
    v_at = pl.multiple_of(2 * HK * DK + pair * 512, 1024)
    kt_ref, kt_at = keys

    def usable():
        return [shared[j] for j in range(KW - 1)]

    def place():
        place_window(x_ref[:, pl.ds(k_at, 512)], halo_ref[:, pl.ds(k_at, 512)], xs, 0)
        place_window(x_ref[:, pl.ds(v_at, 1024)], halo_ref[:, pl.ds(v_at, 1024)], xs, 512)

    def key(n):
        p, a = n // 2, n % 2
        rows = tab_ref[pair + p]
        cols = jnp.transpose(rows)
        at = n * DK
        taps = w_ref[:, pl.ds(k_at + at, DK)].astype(F32)
        k = convolve_piece(xs, at, taps, usable()).astype(F32)
        k = k * unit(k)
        kb = k.astype(BF16)
        ktb = jnp.transpose(kb.astype(F32)).astype(BF16)
        kt_ref[kt_at + p, a * DK : (a + 1) * DK, :] = ktb
        inner = dot(kb, ktb) * shared[5]
        for b in range(2):
            lane = 2 * a + b
            h = GROUP * p + lane
            clock = column(cols, lane)
            within = decay_within(rows, clock, lane, shared[4])
            carried = jnp.exp2(clock) * shared[3]
            sys[h] = ((column(cols, 4 + lane) * within) * inner).astype(BF16)
            right[h, :, 0:DK] = (carried * k).astype(BF16)

    def value(h):
        taps = w_ref[:, pl.ds(v_at + h * DV, DV)].astype(F32)
        right[h, :, DK : DK + DV] = convolve_piece(xs, 512 + h * DV, taps, usable())

    steps = [place]
    steps += [functools.partial(key, n) for n in range(4)]
    steps += [functools.partial(value, h) for h in range(HEADS)]
    return steps


def solving(pair, ins, sys, right, keys, inv, pay_ref, ef_ref, at, kt_copy=None):
    tab_ref, masks, shared = ins[3:]
    kt_ref, kt_at = keys
    kept = {}

    def begin():
        for h in range(HEADS):
            inv[h] = masks[LEVELS] - sys[h] * masks[0]

    def first_product(level):
        size = 1 << level
        kept["steps"] = []
        for h in range(HEADS):
            if size < 16:
                left = sys[h]
            else:
                left = odd_rows(lambda r, e: sys[h, r:e, :], size)
            kept["steps"].append(dot(left, inv[h]).astype(BF16))

    def second_product(level):
        size = 1 << level
        steps = kept["steps"]
        if size < 16:
            steps = [dot(inv[h], steps[h]).astype(BF16) for h in range(HEADS)]
            for h in range(HEADS):
                inv[h] = inv[h] - steps[h] * masks[level]
            return
        blank = jnp.zeros((size, 128), BF16)
        found = []
        for h in range(HEADS):
            expanded = []
            for r in range(0, TOK // 2, size):
                expanded += [blank, steps[h][r : r + size]]
            left = odd_rows(lambda r, e: inv[h, r:e, :], size)
            found.append(dot(left, jnp.concatenate(expanded, axis=0)).astype(BF16))
        for h in range(HEADS):
            for n, r in enumerate(range(size, TOK, 2 * size)):
                inv[h, r : r + size, :] = inv[h, r : r + size, :] - (
                    found[h][n * size : (n + 1) * size] * masks[level, r : r + size, :]
                )

    def check():
        kept["gaps"] = []
        for h in range(HEADS):
            rough = inv[h]
            product = dot(sys[h], rough)
            kept["gaps"].append(
                ((masks[LEVELS].astype(F32) - rough.astype(F32)) - product).astype(BF16)
            )

    def row(h, n):
        return tab_ref[pair + h // GROUP, n : n + 1, :]

    def correct():
        for h in range(HEADS):
            fixed = inv[h].astype(F32) + dot(inv[h], kept["gaps"][h])
            inv[h] = (fixed * row(h, 4 + h % GROUP)).astype(BF16)

    def apply():
        kept["ef"] = []
        for h in range(HEADS):
            ef = dot(inv[h], right[h]).astype(BF16)
            here = slice((h % GROUP) * TOK, (h % GROUP + 1) * TOK)
            ef_ref[at + h // GROUP, here, :] = ef
            kept["ef"].append(ef)

    def write():
        last = []
        for h in range(HEADS):
            g, n = h // GROUP, h % GROUP
            ktb = kt_ref[kt_at + g, (n // 2) * DK : (n // 2 + 1) * DK, :]
            if kt_copy is not None and n % 2 == 0:
                kt_copy[at + g, (n // 2) * DK : (n // 2 + 1) * DK, :] = ktb
            clock = row(h, n)
            final = jnp.broadcast_to(clock[:, TOK - 1 : TOK], (1, TOK))
            ending = jnp.exp2((final - clock) + shared[4, TOK - 1 : TOK, :])
            carried = jnp.exp2(final) * shared[3, TOK - 1 : TOK, :]
            last.append(jnp.concatenate([carried, carried], axis=1))
            weighted = (ktb.astype(F32) * ending).astype(BF16)
            pay_ref[at + g, n * DK : (n + 1) * DK, :] = dot(weighted, kept["ef"][h]).astype(BF16)
        for g in range(2):
            pay_ref[at + g, GROUP * DK : ROWS, :] = split_rows(last[GROUP * g : GROUP * (g + 1)])

    steps = [begin]
    for level in range(1, LEVELS):
        steps.append(functools.partial(first_product, level))
        steps.append(functools.partial(second_product, level))
    return steps + [check, correct, apply, write]


def interleave(main, side):
    done = 0
    for n, step in enumerate(main):
        step()
        due = ((n + 1) * len(side) + len(main) - 1) // len(main)
        while done < min(due, len(side)):
            side[done]()
            done += 1


def send_kernel(
    meta, x_ref, halo_ref, w_ref, tab_ref, masks, shared, pay_ref, kt_ref, ef_ref, sys_out,
    right_out, kt_out, xs, sys, right, inv,
):
    ins = (x_ref, halo_ref, w_ref, tab_ref, masks, shared)
    pair, after = meta[0], meta[1]
    sets = [(sys.at[n], right.at[n], (kt_ref, 2 * n)) for n in range(2)]
    third = (sys_out, right_out, (kt_out, 0))
    for step in preparing(pair, ins, xs, *sets[0]):
        step()
    for n in range(2):
        main = solving(pair + 2 * n, ins, *sets[n], inv, pay_ref, ef_ref, 2 * n)
        if n == 0:
            side = preparing(pair + 2, ins, xs, *sets[1])
        else:
            side = preparing(after, ins, xs, *third)
        interleave(main, side)


def keep_kernel(
    meta, x_ref, halo_ref, w_ref, tab_ref, masks, shared, sys_in, right_in, kt_in, pay_ref,
    kt_ref, ef_ref, xs, sys, right, inv,
):
    ins = (x_ref, halo_ref, w_ref, tab_ref, masks, shared)
    pair = meta[1]
    own = (sys, right, (kt_ref, 2))
    interleave(
        solving(pair, ins, sys_in, right_in, (kt_in, 0), inv, pay_ref, ef_ref, 0, kt_ref),
        preparing(pair + 2, ins, xs, *own),
    )
    for step in solving(pair + 2, ins, *own, inv, pay_ref, ef_ref, 2):
        step()


def map_shapes():
    return [
        jax.ShapeDtypeStruct((4, ROWS, 256), BF16),
        jax.ShapeDtypeStruct((4, 2 * DK, TOK), BF16),
        jax.ShapeDtypeStruct((4, GROUP * TOK, 256), BF16),
    ]


def ready_shapes():
    return [
        jax.ShapeDtypeStruct((HEADS, TOK, TOK), BF16),
        jax.ShapeDtypeStruct((HEADS, TOK, 256), BF16),
        jax.ShapeDtypeStruct((2, 2 * DK, TOK), BF16),
    ]


def map_cost():
    return pl.CostEstimate(
        flops=16 * 20 * 2 * 128**3, bytes_accessed=5 * 2**20, transcendentals=10**6
    )


def send_maps(meta, *ins):
    return pl.pallas_call(
        send_kernel,
        in_specs=[smem_spec()] + [whole_spec()] * len(ins),
        out_specs=[whole_spec()] * 6,
        out_shape=map_shapes() + ready_shapes(),
        scratch_shapes=[
            pltpu.VMEM((8 + TOK, 1536), F32),
            pltpu.VMEM((2, HEADS, TOK, TOK), BF16),
            pltpu.VMEM((2, HEADS, TOK, 256), BF16),
            pltpu.VMEM((HEADS, TOK, TOK), BF16),
        ],
        compiler_params=params(),
        cost_estimate=map_cost(),
        name="send_maps",
    )(meta, *ins)


def keep_maps(meta, *ins):
    return pl.pallas_call(
        keep_kernel,
        in_specs=[smem_spec()] + [whole_spec()] * len(ins),
        out_specs=[whole_spec()] * 3,
        out_shape=map_shapes(),
        scratch_shapes=[
            pltpu.VMEM((8 + TOK, 1536), F32),
            pltpu.VMEM((HEADS, TOK, TOK), BF16),
            pltpu.VMEM((HEADS, TOK, 256), BF16),
            pltpu.VMEM((HEADS, TOK, TOK), BF16),
        ],
        compiler_params=params(),
        cost_estimate=map_cost(),
        name="keep_maps",
    )(meta, *ins)


def read_kernel(meta, xq_ref, hq_ref, wq_ref, rows_ref, kt_ref, ef_ref, left_ref, r_ref, d_ref, xs):
    first = meta[2] == 0
    tail = left_ref[0, GROUP * DK : ROWS, :]
    rows = rows_ref[0]
    cols = jnp.transpose(rows)
    usable = [column(cols, 8 + j) for j in range(KW - 1)]
    living = column(cols, 12)
    hidden = hidden_where(rows, cols)
    place_window(xq_ref[...], hq_ref[...], xs, 0)
    taps = wq_ref[...].astype(F32)
    for a in range(2):
        queries = convolve_piece(xs, a * DK, taps[:, a * DK : (a + 1) * DK], usable)
        q = queries.astype(F32)
        scale = unit(q, DK ** (-0.5))
        inner = dot(queries, kt_ref[0, a * DK : (a + 1) * DK, :])
        for b in range(2):
            h = 2 * a + b
            clock = column(cols, h)
            scores = (inner * decay_within(rows, clock, h, hidden)).astype(BF16)
            both = dot(scores, ef_ref[0, h * TOK : (h + 1) * TOK, :])
            carried = jnp.exp2(clock) * living
            mine = slice(h * TOK, (h + 1) * TOK)
            reader = (carried * q - both[:, :DK]) * scale
            direct = both[:, DK:] * scale
            moved = dot(reader.astype(BF16), left_ref[0, h * DK : (h + 1) * DK, :])
            c = factor(tail, h)[:, :DK]
            r_ref[0, mine, :] = jnp.where(first, reader, c * reader - moved[:, :DK]).astype(BF16)
            d_ref[0, mine, :] = jnp.where(first, direct, direct + moved[:, DK:])


def make_reads(meta, slot, projected, halo, conv_weight, tables, keys_t, ef, left):
    def at(i, m):
        return (0, m[slot] + i)

    return pl.pallas_call(
        read_kernel,
        grid_spec=pltpu.PrefetchScalarGridSpec(
            num_scalar_prefetch=1,
            grid=(4,),
            in_specs=[
                pl.BlockSpec((TOK, 256), at),
                pl.BlockSpec((KW - 1, 256), at),
                pl.BlockSpec((KW, 256), at),
                pl.BlockSpec((1, 16, TOK), lambda i, m: (m[slot] + i, 0, 0)),
                pl.BlockSpec((1, 2 * DK, TOK), lambda i, m: (i, 0, 0)),
                pl.BlockSpec((1, GROUP * TOK, 256), lambda i, m: (i, 0, 0)),
                pl.BlockSpec((1, ROWS, 256), lambda i, m: (i, 0, 0)),
            ],
            out_specs=[
                pl.BlockSpec((1, GROUP * TOK, DK), lambda i, m: (i, 0, 0)),
                pl.BlockSpec((1, GROUP * TOK, DV), lambda i, m: (i, 0, 0)),
            ],
            scratch_shapes=[pltpu.VMEM((8 + TOK, 256), F32)],
        ),
        out_shape=[
            jax.ShapeDtypeStruct((4, GROUP * TOK, DK), BF16),
            jax.ShapeDtypeStruct((4, GROUP * TOK, DV), F32),
        ],
        compiler_params=params(),
        cost_estimate=pl.CostEstimate(
            flops=16 * 6 * 2 * 128**3, bytes_accessed=5 * 2**20, transcendentals=10**6
        ),
        name="reads",
    )(meta, projected, halo, conv_weight, tables, keys_t, ef, left)


def factor(tail, head):
    tail = tail.astype(F32)
    return (tail[head : head + 1] + tail[4 + head : 5 + head]) + tail[8 + head : 9 + head]


def compose(left, left_c, right, right_c):
    right_d = right[:, :DK]
    product = dot(right_d.astype(BF16), left.astype(BF16))
    return (
        right_c * left.astype(F32)
        + jnp.concatenate(
            [left_c[:, :DK] * right_d.astype(F32), right[:, DK:].astype(F32)], axis=1
        )
        - product
    )


def apply_map(each, c, state):
    product = dot(each[:, :DK], state)
    return c[:, :DK] * state.astype(F32) + each[:, DK:].astype(F32) - product


def pair_kernel(meta, mine_ref, other_ref, *out_refs):
    def combine(left_ref, right_ref):
        for m, out_ref in enumerate(out_refs):
            g = meta[3] ^ m
            left_tail = left_ref[g, GROUP * DK : ROWS, :]
            right_tail = right_ref[g, GROUP * DK : ROWS, :]
            factors = []
            for h in range(GROUP):
                here = slice(h * DK, (h + 1) * DK)
                left_c, right_c = factor(left_tail, h), factor(right_tail, h)
                both = compose(left_ref[g, here, :], left_c, right_ref[g, here, :], right_c)
                out_ref[here, :] = both.astype(BF16)
                factors.append(left_c * right_c)
            out_ref[GROUP * DK : ROWS, :] = split_rows(factors)

    pl.when(meta[2] == 0)(lambda: combine(mine_ref, other_ref))
    pl.when(meta[2] != 0)(lambda: combine(other_ref, mine_ref))


def pair_maps(meta, mine, other):
    return pl.pallas_call(
        pair_kernel,
        in_specs=[smem_spec(), whole_spec(), whole_spec()],
        out_specs=[whole_spec()] * 4,
        out_shape=[jax.ShapeDtypeStruct((ROWS, 256), BF16)] * 4,
        compiler_params=params(),
        cost_estimate=pl.CostEstimate(
            flops=16 * 2 * 2 * 128**3, bytes_accessed=3 * 2**20, transcendentals=0
        ),
        name="pair",
    )(meta, mine, other)


def by_place(meta, body):
    for place in range(4):
        pl.when(meta[3] == place)(functools.partial(body, place))


def plane_kernel(meta, x0, x1, x2, x3, prefix_ref, plane_ref, exit_ref):
    pieces = (x0, x1, x2, x3)
    prefix_ref[0] = jnp.zeros((ROWS, 256), BF16)

    def chain(place):
        maps = [pieces[place ^ a] for a in range(4)]
        prefix_ref[1] = maps[0][...]
        run = [maps[0][h * DK : (h + 1) * DK, :].astype(F32) for h in range(GROUP)]
        run_c = [factor(maps[0][GROUP * DK : ROWS, :], h) for h in range(GROUP)]
        for a in range(1, 4):
            tail = maps[a][GROUP * DK : ROWS, :]
            for h in range(GROUP):
                here = slice(h * DK, (h + 1) * DK)
                c = factor(tail, h)
                run[h] = compose(run[h], run_c[h], maps[a][here, :], c)
                run_c[h] = run_c[h] * c
                if a < 3:
                    prefix_ref[a + 1, here, :] = run[h].astype(BF16)
                else:
                    plane_ref[here, :] = run[h].astype(BF16)
                    exit_ref[here, :] = run[h][:, DK:].astype(BF16)
            if a < 3:
                prefix_ref[a + 1, GROUP * DK : ROWS, :] = split_rows(run_c)
        plane_ref[GROUP * DK : ROWS, :] = split_rows(run_c)

    by_place(meta, chain)


def plane_maps(meta, pieces):
    return pl.pallas_call(
        plane_kernel,
        in_specs=[smem_spec()] + [whole_spec()] * 4,
        out_specs=[whole_spec()] * 3,
        out_shape=[
            jax.ShapeDtypeStruct((4, ROWS, 256), BF16),
            jax.ShapeDtypeStruct((ROWS, 256), BF16),
            jax.ShapeDtypeStruct((GROUP * DK, DV), BF16),
        ],
        compiler_params=params(),
        cost_estimate=pl.CostEstimate(
            flops=12 * 2 * 2 * 128**3, bytes_accessed=2 * 2**20, transcendentals=0
        ),
        name="plane",
    )(meta, *pieces)


def hop_kernel(plane_ref, state_ref, out_ref):
    tail = plane_ref[GROUP * DK : ROWS, :]
    for h in range(GROUP):
        here = slice(h * DK, (h + 1) * DK)
        state = apply_map(plane_ref[here, :], factor(tail, h), state_ref[here, :])
        out_ref[here, :] = state.astype(BF16)


def hop(plane_map, state):
    return pl.pallas_call(
        hop_kernel,
        in_specs=[whole_spec()] * 2,
        out_specs=whole_spec(),
        out_shape=jax.ShapeDtypeStruct((GROUP * DK, DV), BF16),
        compiler_params=params(),
        cost_estimate=pl.CostEstimate(
            flops=4 * 2 * 128**3, bytes_accessed=2**19, transcendentals=0
        ),
        name="hop",
    )(plane_map, state)


def spread_kernel(meta, prefix_ref, before_ref, far_ref, *refs):
    out_refs = refs[-4:]
    state_refs = refs[:-4]
    before_tail = before_ref[GROUP * DK : ROWS, :]

    def send(place):
        for h in range(GROUP):
            here = slice(h * DK, (h + 1) * DK)
            state = apply_map(before_ref[here, :], factor(before_tail, h), far_ref[here, :])
            state = state.astype(BF16)
            for ref in state_refs:
                state = state + ref[here, :]
            out_refs[place][here, :] = state
            for a in range(1, 4):
                c = factor(prefix_ref[a, GROUP * DK : ROWS, :], h)
                after = apply_map(prefix_ref[a, here, :], c, state)
                out_refs[place ^ a][here, :] = after.astype(BF16)

    by_place(meta, send)


def spread(meta, prefix, before, far, states):
    return pl.pallas_call(
        spread_kernel,
        in_specs=[smem_spec()] + [whole_spec()] * (3 + len(states)),
        out_specs=[whole_spec()] * 4,
        out_shape=[jax.ShapeDtypeStruct((GROUP * DK, DV), BF16)] * 4,
        compiler_params=params(),
        cost_estimate=pl.CostEstimate(
            flops=20 * 2 * 128**3, bytes_accessed=2**21, transcendentals=0
        ),
        name="spread",
    )(meta, prefix, before, far, *states)


def entering_states(plane_map, leaving, planes):
    def ahead(block, plane, distance=1):
        members = range(8 * plane, 8 * plane + 8)
        return lax.ppermute(block, "seq", [(i, i + 8 * distance) for i in members])

    if planes == 4:
        first = ahead(leaving, 0)
        before = ahead(plane_map, 2)
        second = hop(plane_map, first)
        far = ahead(second, 1, 2)
        near = ahead(second, 1)
        return before, far, [first, near]
    states = []
    for plane in range(planes - 1):
        state = ahead(leaving, plane)
        states.append(state)
        if plane < planes - 2:
            leaving = hop(plane_map, state)
    return jnp.zeros_like(plane_map), jnp.zeros_like(leaving), states


def read_out(meta, r_ref, d_ref, e_refs, rows):
    for m, e_ref in enumerate(e_refs):
        g = meta[3] ^ m
        for h in range(GROUP):
            here = slice(h * TOK, (h + 1) * TOK)
            total = dot(r_ref[g, here, :], e_ref[here, :]) + d_ref[g, here, :]
            rows[g, :, h * DV : (h + 1) * DV] = total.astype(BF16)
        yield m, g


def half_kernel(meta, r_ref, d_ref, e0, e1, e2, e3, rows):
    for _ in read_out(meta, r_ref, d_ref, (e0, e1, e2, e3), rows):
        pass


def read_half(meta, reads, direct, states):
    return pl.pallas_call(
        half_kernel,
        in_specs=[smem_spec()] + [whole_spec()] * 6,
        out_specs=whole_spec(),
        out_shape=jax.ShapeDtypeStruct((4, TOK, GROUP * DV), BF16),
        compiler_params=params(),
        cost_estimate=pl.CostEstimate(
            flops=16 * 2 * 128**3, bytes_accessed=3 * 2**20, transcendentals=0
        ),
        name="half",
    )(meta, reads, direct, *states)


def emit_kernel(meta, kept, r_ref, d_ref, e0, e1, e2, e3, out_ref, rows, sems):
    copies = []

    def put(source, n, slot, g):
        start = pl.multiple_of((meta[slot] + g) * (GROUP * DV), GROUP * DV)
        copy = pltpu.make_async_copy(
            source.at[g], out_ref.at[:, pl.ds(start, GROUP * DV)], sems.at[n]
        )
        copy.start()
        copies.append(copy)

    for g in range(4):
        put(kept, g, 1, g)
    for m, g in read_out(meta, r_ref, d_ref, (e0, e1, e2, e3), rows):
        put(rows, 4 + m, 0, g)
    for copy in copies:
        copy.wait()


def emit(meta, kept, reads, direct, states):
    return pl.pallas_call(
        emit_kernel,
        in_specs=[smem_spec()] + [whole_spec()] * 7,
        out_specs=pl.BlockSpec(memory_space=pl.ANY),
        out_shape=jax.ShapeDtypeStruct((TOK, HV * DV), BF16),
        scratch_shapes=[
            pltpu.VMEM((4, TOK, GROUP * DV), BF16),
            pltpu.SemaphoreType.DMA((8,)),
        ],
        compiler_params=params(),
        cost_estimate=pl.CostEstimate(
            flops=16 * 2 * 128**3, bytes_accessed=3 * 2**20, transcendentals=0
        ),
        name="emit",
    )(meta, kept, reads, direct, *states)


def shards(projected, conv_weight, decay_log, write_strength, starts):
    count = lax.axis_size("seq")
    me = lax.axis_index("seq")
    core, place = me & 1, (me >> 1) & 3
    slots = lax.iota(jnp.int32, 8)
    meta = jnp.zeros((8,), jnp.int32)
    for slot, value in enumerate((4 * (1 - core), 4 * core, core, place, me >> 3)):
        meta = jnp.where(slots == slot, value, meta)

    def exchange(block, bits):
        return lax.ppermute(block, "seq", [(i, i ^ bits) for i in range(count)])

    starts = starts.reshape(1, TOK)
    tail_rows = tail_of(starts, projected)
    halo = lax.ppermute(tail_rows, "seq", [(i, i + 1) for i in range(count - 1)])
    projected, conv_weight, tables, masks, shared = stage(
        decay_log, write_strength, starts, projected, conv_weight
    )
    ins = (projected, halo, conv_weight, tables, masks, shared)

    pay_s, kt_s, ef_s, *ready = send_maps(meta, *ins)
    other = exchange(pay_s, 1)
    mine, kt_k, ef_k = keep_maps(meta, *ins, *ready)
    x0, x1, x2, x3 = pair_maps(meta, mine, other)
    x3, x1, x2 = exchange(x3, 6), exchange(x1, 2), exchange(x2, 4)
    x0, own = lax.optimization_barrier((x0, mine))
    left = exchange(own, 1)
    r_k, d_k = make_reads(meta, 1, projected, halo, conv_weight, tables, kt_k, ef_k, other)
    r_s, d_s = make_reads(meta, 0, projected, halo, conv_weight, tables, kt_s, ef_s, left)
    x0, r_k, d_k, r_s, d_s = lax.optimization_barrier((x0, r_k, d_k, r_s, d_s))
    prefix, plane_map, leaving = plane_maps(meta, (x0, x1, x2, x3))
    before, far, arrived = entering_states(plane_map, leaving, count // 8)
    e0, e1, e2, e3 = spread(meta, prefix, before, far, arrived)
    e3, e1, e2 = exchange(e3, 6), exchange(e1, 2), exchange(e2, 4)
    states = (e0, e1, e2, e3)
    partner = [exchange(e, 1) for e in states]
    kept = read_half(meta, r_k, d_k, states)
    return emit(meta, kept, r_s, d_s, partner)


def solution(mesh):
    in_specs = (
        P(("groups", "seq"), None),
        P(),
        P(None, ("groups", "seq")),
        P(None, ("groups", "seq")),
        P(("groups", "seq")),
    )
    out_specs = P(("groups", "seq"), None)

    return jax.shard_map(shards, mesh=mesh, in_specs=in_specs, out_specs=out_specs, check_vma=False)
```

```python
import functools

import jax
import jax.numpy as jnp
from jax import lax
from jax.experimental import pallas as pl
from jax.experimental.pallas import tpu as pltpu
from jax.sharding import PartitionSpec as P


HK = 16
DK = 128
HV = 32
DV = 128
KW = 4
TOK = 128
NORM_EPS = 1e-06
GROUP = 4
LOG2E = 1.4426950408889634
HIDDEN = -1e30
ROWS = GROUP * DK + 16
F32 = jnp.float32
BF16 = jnp.bfloat16


def dot(a, b):
    return jnp.dot(a, b, preferred_element_type=F32)


def params(**kw):
    return pltpu.CompilerParams(vmem_limit_bytes=20 << 20, **kw)


def whole_spec():
    return pl.BlockSpec(memory_space=pltpu.VMEM)


def smem_spec():
    return pl.BlockSpec(memory_space=pltpu.SMEM)


def in_hbm(x):
    return pltpu.with_memory_space_constraint(x, pltpu.HBM)


def tail_kernel(starts_ref, x_ref, tail_ref):
    rows = x_ref.shape[0]
    flags = starts_ref[...].astype(F32)
    last = 1.0 - flags[:, TOK - 1 : TOK]
    keep = [last * (1.0 - flags[:, TOK - 2 : TOK - 1]), last, jnp.ones((1, 1), F32)]
    for r in range(KW - 1):
        row = x_ref[rows - KW + 1 + r : rows - KW + 2 + r, :].astype(F32)
        tail_ref[r : r + 1, :] = (row * keep[r]).astype(BF16)


def tail_of(starts, projected):
    channels = projected.shape[1]
    last = projected.shape[0] // 16 - 1
    return pl.pallas_call(
        tail_kernel,
        grid=(1,),
        in_specs=[
            pl.BlockSpec((1, TOK), lambda i: (0, 0)),
            pl.BlockSpec((16, channels), lambda i: (last, 0)),
        ],
        out_specs=pl.BlockSpec((KW - 1, channels), lambda i: (0, 0)),
        out_shape=jax.ShapeDtypeStruct((KW - 1, channels), BF16),
        compiler_params=params(),
        cost_estimate=pl.CostEstimate(flops=10**5, bytes_accessed=10**6, transcendentals=0),
        name="tail",
    )(in_hbm(starts), in_hbm(projected))


def write_tables(decay_ref, beta_ref, starts_ref, out_ref):
    src, dst = positions()
    cum = LOG2E * jnp.dot(
        decay_ref[...],
        (src <= dst).astype(F32),
        precision=lax.Precision.HIGHEST,
        preferred_element_type=F32,
    )
    flags = jnp.broadcast_to(starts_ref[...].astype(F32), (8, TOK)).astype(BF16)
    episode = [dot(flags, (src + j <= dst).astype(BF16))[0:1] for j in range(KW)]
    usable = [(episode[0] == episode[j]).astype(F32) for j in range(1, KW)]
    living = (episode[0] == 0.0).astype(F32)
    zero = jnp.zeros((1, TOK), F32)
    shared = jnp.concatenate(usable + [episode[0], living, zero, zero, zero], axis=0)
    for pair in range(HV // GROUP):
        out_ref[pair, 0:4, :] = cum[GROUP * pair : GROUP * (pair + 1)]
        out_ref[pair, 4:8, :] = beta_ref[GROUP * pair : GROUP * (pair + 1), :]
        out_ref[pair, 8:16, :] = shared


def place_window(x, halo, xs, first):
    cols = slice(first, first + x.shape[1])
    xs[8 : 8 + TOK, cols] = x.astype(F32)
    xs[8 - KW + 1 : 8, cols] = halo.astype(F32)


def convolve_piece(xs, first, taps, usable):
    here = slice(first, first + 128)
    total = xs[8 : 8 + TOK, here] * taps[3:4]
    for j in range(1, KW):
        total = total + (xs[8 - j : 8 - j + TOK, here] * usable[j - 1]) * taps[3 - j : 4 - j]
    return (total / (1.0 + jnp.exp2(total * -LOG2E))).astype(BF16)


def column(cols, lane):
    return jnp.broadcast_to(cols[:, lane : lane + 1], (TOK, 128))


def positions():
    i = lax.broadcasted_iota(jnp.int32, (TOK, TOK), 0)
    j = lax.broadcasted_iota(jnp.int32, (TOK, TOK), 1)
    return i, j


def hidden_where(rows, cols):
    i, j = positions()
    seen = (column(cols, 11) == rows[11:12, :]) & (i >= j)
    return jnp.where(seen, 0.0, HIDDEN)


def decay_within(rows, clock, head, hidden):
    return jnp.exp2((clock - rows[head : head + 1, :]) + hidden)


def unit(x, scale=1.0):
    return lax.rsqrt(jnp.sum(x * x, axis=-1, keepdims=True) + NORM_EPS) * scale


def split_rows(x):
    pieces, rest = [], list(x)
    for _ in range(3):
        highs = [c.astype(BF16).astype(F32) for c in rest]
        pieces += highs
        rest = [c - high for c, high in zip(rest, highs)]
    pieces.append(jnp.zeros((4, 256), F32))
    return jnp.concatenate(pieces, axis=0).astype(BF16)


LEVELS = 7
HEADS = 8


def odd_rows(get, size):
    return jnp.concatenate([get(r, r + size) for r in range(size, TOK, 2 * size)], axis=0)


def stage_kernel(
    decay_hbm, beta_hbm, starts_hbm, x_hbm, w_hbm, x_out, w_out, tab_ref, masks, shared,
    decay_ref, beta_ref, starts_ref, sems,
):
    moves = [
        (decay_hbm, decay_ref),
        (beta_hbm, beta_ref),
        (starts_hbm, starts_ref),
        (x_hbm, x_out),
        (w_hbm, w_out),
    ]
    copies = [pltpu.make_async_copy(*move, sems.at[n]) for n, move in enumerate(moves)]
    for copy in copies:
        copy.start()
    for copy in copies[:3]:
        copy.wait()
    write_tables(decay_ref, beta_ref, starts_ref, tab_ref)
    rows = tab_ref[0]
    cols = jnp.transpose(rows)
    for j in range(KW - 1):
        shared[j] = column(cols, 8 + j)
    shared[3] = column(cols, 12)
    shared[4] = hidden_where(rows, cols)
    i, j = positions()
    apart = i ^ j
    for level in range(LEVELS):
        masks[level] = (((apart >> level) == 1) & (i > j)).astype(F32).astype(BF16)
    shared[5] = (i > j).astype(F32)
    masks[LEVELS] = (i == j).astype(F32).astype(BF16)
    for copy in copies[3:]:
        copy.wait()


def stage(decay_log, write_strength, starts, projected, conv_weight):
    return pl.pallas_call(
        stage_kernel,
        in_specs=[pl.BlockSpec(memory_space=pl.ANY)] * 5,
        out_specs=[whole_spec()] * 5,
        out_shape=[
            jax.ShapeDtypeStruct(projected.shape, BF16),
            jax.ShapeDtypeStruct(conv_weight.shape, BF16),
            jax.ShapeDtypeStruct((HV // GROUP, 16, TOK), F32),
            jax.ShapeDtypeStruct((LEVELS + 1, TOK, TOK), BF16),
            jax.ShapeDtypeStruct((6, TOK, 128), F32),
        ],
        scratch_shapes=[
            pltpu.VMEM((HV, TOK), F32),
            pltpu.VMEM((HV, TOK), F32),
            pltpu.VMEM((1, TOK), jnp.int32),
            pltpu.SemaphoreType.DMA((5,)),
        ],
        compiler_params=params(),
        cost_estimate=pl.CostEstimate(flops=10**7, bytes_accessed=4 * 2**20, transcendentals=0),
        name="stage",
    )(
        in_hbm(decay_log),
        in_hbm(write_strength),
        in_hbm(starts),
        in_hbm(projected),
        in_hbm(conv_weight),
    )


def preparing(pair, ins, xs, sys, right, keys):
    x_ref, halo_ref, w_ref, tab_ref, _, shared = ins
    k_at = pl.multiple_of(HK * DK + pair * 256, 512)
    v_at = pl.multiple_of(2 * HK * DK + pair * 512, 1024)
    kt_ref, kt_at = keys

    def usable():
        return [shared[j] for j in range(KW - 1)]

    def place():
        place_window(x_ref[:, pl.ds(k_at, 512)], halo_ref[:, pl.ds(k_at, 512)], xs, 0)
        place_window(x_ref[:, pl.ds(v_at, 1024)], halo_ref[:, pl.ds(v_at, 1024)], xs, 512)

    def key(n):
        p, a = n // 2, n % 2
        rows = tab_ref[pair + p]
        cols = jnp.transpose(rows)
        at = n * DK
        taps = w_ref[:, pl.ds(k_at + at, DK)].astype(F32)
        k = convolve_piece(xs, at, taps, usable()).astype(F32)
        k = k * unit(k)
        kb = k.astype(BF16)
        ktb = jnp.transpose(kb.astype(F32)).astype(BF16)
        kt_ref[kt_at + p, a * DK : (a + 1) * DK, :] = ktb
        inner = dot(kb, ktb) * shared[5]
        for b in range(2):
            lane = 2 * a + b
            h = GROUP * p + lane
            clock = column(cols, lane)
            within = decay_within(rows, clock, lane, shared[4])
            carried = jnp.exp2(clock) * shared[3]
            sys[h] = ((column(cols, 4 + lane) * within) * inner).astype(BF16)
            right[h, :, 0:DK] = (carried * k).astype(BF16)

    def value(h):
        taps = w_ref[:, pl.ds(v_at + h * DV, DV)].astype(F32)
        right[h, :, DK : DK + DV] = convolve_piece(xs, 512 + h * DV, taps, usable())

    steps = [place]
    steps += [functools.partial(key, n) for n in range(4)]
    steps += [functools.partial(value, h) for h in range(HEADS)]
    return steps


def solving(pair, ins, sys, right, keys, inv, pay_ref, ef_ref, at, kt_copy=None):
    tab_ref, masks, shared = ins[3:]
    kt_ref, kt_at = keys
    kept = {}

    def begin():
        for h in range(HEADS):
            inv[h] = masks[LEVELS] - sys[h] * masks[0]

    def first_product(level):
        size = 1 << level
        kept["steps"] = []
        for h in range(HEADS):
            if size < 16:
                left = sys[h]
            else:
                left = odd_rows(lambda r, e: sys[h, r:e, :], size)
            kept["steps"].append(dot(left, inv[h]).astype(BF16))

    def second_product(level):
        size = 1 << level
        steps = kept["steps"]
        if size < 16:
            steps = [dot(inv[h], steps[h]).astype(BF16) for h in range(HEADS)]
            for h in range(HEADS):
                inv[h] = inv[h] - steps[h] * masks[level]
            return
        blank = jnp.zeros((size, 128), BF16)
        found = []
        for h in range(HEADS):
            expanded = []
            for r in range(0, TOK // 2, size):
                expanded += [blank, steps[h][r : r + size]]
            left = odd_rows(lambda r, e: inv[h, r:e, :], size)
            found.append(dot(left, jnp.concatenate(expanded, axis=0)).astype(BF16))
        for h in range(HEADS):
            for n, r in enumerate(range(size, TOK, 2 * size)):
                inv[h, r : r + size, :] = inv[h, r : r + size, :] - (
                    found[h][n * size : (n + 1) * size] * masks[level, r : r + size, :]
                )

    def check():
        kept["gaps"] = []
        for h in range(HEADS):
            rough = inv[h]
            product = dot(sys[h], rough)
            kept["gaps"].append(
                ((masks[LEVELS].astype(F32) - rough.astype(F32)) - product).astype(BF16)
            )

    def row(h, n):
        return tab_ref[pair + h // GROUP, n : n + 1, :]

    def correct():
        for h in range(HEADS):
            fixed = inv[h].astype(F32) + dot(inv[h], kept["gaps"][h])
            inv[h] = (fixed * row(h, 4 + h % GROUP)).astype(BF16)

    def apply():
        kept["ef"] = []
        for h in range(HEADS):
            ef = dot(inv[h], right[h]).astype(BF16)
            here = slice((h % GROUP) * TOK, (h % GROUP + 1) * TOK)
            ef_ref[at + h // GROUP, here, :] = ef
            kept["ef"].append(ef)

    def write():
        last = []
        for h in range(HEADS):
            g, n = h // GROUP, h % GROUP
            ktb = kt_ref[kt_at + g, (n // 2) * DK : (n // 2 + 1) * DK, :]
            if kt_copy is not None and n % 2 == 0:
                kt_copy[at + g, (n // 2) * DK : (n // 2 + 1) * DK, :] = ktb
            clock = row(h, n)
            final = jnp.broadcast_to(clock[:, TOK - 1 : TOK], (1, TOK))
            ending = jnp.exp2((final - clock) + shared[4, TOK - 1 : TOK, :])
            carried = jnp.exp2(final) * shared[3, TOK - 1 : TOK, :]
            last.append(jnp.concatenate([carried, carried], axis=1))
            weighted = (ktb.astype(F32) * ending).astype(BF16)
            pay_ref[at + g, n * DK : (n + 1) * DK, :] = dot(weighted, kept["ef"][h]).astype(BF16)
        for g in range(2):
            pay_ref[at + g, GROUP * DK : ROWS, :] = split_rows(last[GROUP * g : GROUP * (g + 1)])

    steps = [begin]
    for level in range(1, LEVELS):
        steps.append(functools.partial(first_product, level))
        steps.append(functools.partial(second_product, level))
    return steps + [check, correct, apply, write]


def interleave(main, side):
    done = 0
    for n, step in enumerate(main):
        step()
        due = ((n + 1) * len(side) + len(main) - 1) // len(main)
        while done < min(due, len(side)):
            side[done]()
            done += 1


def send_kernel(
    meta, x_ref, halo_ref, w_ref, tab_ref, masks, shared, pay_ref, kt_ref, ef_ref, sys_out,
    right_out, kt_out, xs, sys, right, inv,
):
    ins = (x_ref, halo_ref, w_ref, tab_ref, masks, shared)
    pair, after = meta[0], meta[1]
    sets = [(sys.at[n], right.at[n], (kt_ref, 2 * n)) for n in range(2)]
    third = (sys_out, right_out, (kt_out, 0))
    for step in preparing(pair, ins, xs, *sets[0]):
        step()
    for n in range(2):
        main = solving(pair + 2 * n, ins, *sets[n], inv, pay_ref, ef_ref, 2 * n)
        if n == 0:
            side = preparing(pair + 2, ins, xs, *sets[1])
        else:
            side = preparing(after, ins, xs, *third)
        interleave(main, side)


def keep_kernel(
    meta, x_ref, halo_ref, w_ref, tab_ref, masks, shared, sys_in, right_in, kt_in, pay_ref,
    kt_ref, ef_ref, xs, sys, right, inv,
):
    ins = (x_ref, halo_ref, w_ref, tab_ref, masks, shared)
    pair = meta[1]
    own = (sys, right, (kt_ref, 2))
    interleave(
        solving(pair, ins, sys_in, right_in, (kt_in, 0), inv, pay_ref, ef_ref, 0, kt_ref),
        preparing(pair + 2, ins, xs, *own),
    )
    for step in solving(pair + 2, ins, *own, inv, pay_ref, ef_ref, 2):
        step()


def map_shapes():
    return [
        jax.ShapeDtypeStruct((4, ROWS, 256), BF16),
        jax.ShapeDtypeStruct((4, 2 * DK, TOK), BF16),
        jax.ShapeDtypeStruct((4, GROUP * TOK, 256), BF16),
    ]


def ready_shapes():
    return [
        jax.ShapeDtypeStruct((HEADS, TOK, TOK), BF16),
        jax.ShapeDtypeStruct((HEADS, TOK, 256), BF16),
        jax.ShapeDtypeStruct((2, 2 * DK, TOK), BF16),
    ]


def map_cost():
    return pl.CostEstimate(
        flops=16 * 20 * 2 * 128**3, bytes_accessed=5 * 2**20, transcendentals=10**6
    )


def send_maps(meta, *ins):
    return pl.pallas_call(
        send_kernel,
        in_specs=[smem_spec()] + [whole_spec()] * len(ins),
        out_specs=[whole_spec()] * 6,
        out_shape=map_shapes() + ready_shapes(),
        scratch_shapes=[
            pltpu.VMEM((8 + TOK, 1536), F32),
            pltpu.VMEM((2, HEADS, TOK, TOK), BF16),
            pltpu.VMEM((2, HEADS, TOK, 256), BF16),
            pltpu.VMEM((HEADS, TOK, TOK), BF16),
        ],
        compiler_params=params(),
        cost_estimate=map_cost(),
        name="send_maps",
    )(meta, *ins)


def keep_maps(meta, *ins):
    return pl.pallas_call(
        keep_kernel,
        in_specs=[smem_spec()] + [whole_spec()] * len(ins),
        out_specs=[whole_spec()] * 3,
        out_shape=map_shapes(),
        scratch_shapes=[
            pltpu.VMEM((8 + TOK, 1536), F32),
            pltpu.VMEM((HEADS, TOK, TOK), BF16),
            pltpu.VMEM((HEADS, TOK, 256), BF16),
            pltpu.VMEM((HEADS, TOK, TOK), BF16),
        ],
        compiler_params=params(),
        cost_estimate=map_cost(),
        name="keep_maps",
    )(meta, *ins)


def read_kernel(meta, xq_ref, hq_ref, wq_ref, rows_ref, kt_ref, ef_ref, left_ref, r_ref, d_ref, xs):
    first = meta[2] == 0
    tail = left_ref[0, GROUP * DK : ROWS, :]
    rows = rows_ref[0]
    cols = jnp.transpose(rows)
    usable = [column(cols, 8 + j) for j in range(KW - 1)]
    living = column(cols, 12)
    hidden = hidden_where(rows, cols)
    place_window(xq_ref[...], hq_ref[...], xs, 0)
    taps = wq_ref[...].astype(F32)
    for a in range(2):
        queries = convolve_piece(xs, a * DK, taps[:, a * DK : (a + 1) * DK], usable)
        q = queries.astype(F32)
        scale = unit(q, DK ** (-0.5))
        inner = dot(queries, kt_ref[0, a * DK : (a + 1) * DK, :])
        for b in range(2):
            h = 2 * a + b
            clock = column(cols, h)
            scores = (inner * decay_within(rows, clock, h, hidden)).astype(BF16)
            both = dot(scores, ef_ref[0, h * TOK : (h + 1) * TOK, :])
            carried = jnp.exp2(clock) * living
            mine = slice(h * TOK, (h + 1) * TOK)
            reader = (carried * q - both[:, :DK]) * scale
            direct = both[:, DK:] * scale
            moved = dot(reader.astype(BF16), left_ref[0, h * DK : (h + 1) * DK, :])
            c = factor(tail, h)[:, :DK]
            r_ref[0, mine, :] = jnp.where(first, reader, c * reader - moved[:, :DK]).astype(BF16)
            d_ref[0, mine, :] = jnp.where(first, direct, direct + moved[:, DK:])


def make_reads(meta, slot, projected, halo, conv_weight, tables, keys_t, ef, left):
    def at(i, m):
        return (0, m[slot] + i)

    return pl.pallas_call(
        read_kernel,
        grid_spec=pltpu.PrefetchScalarGridSpec(
            num_scalar_prefetch=1,
            grid=(4,),
            in_specs=[
                pl.BlockSpec((TOK, 256), at),
                pl.BlockSpec((KW - 1, 256), at),
                pl.BlockSpec((KW, 256), at),
                pl.BlockSpec((1, 16, TOK), lambda i, m: (m[slot] + i, 0, 0)),
                pl.BlockSpec((1, 2 * DK, TOK), lambda i, m: (i, 0, 0)),
                pl.BlockSpec((1, GROUP * TOK, 256), lambda i, m: (i, 0, 0)),
                pl.BlockSpec((1, ROWS, 256), lambda i, m: (i, 0, 0)),
            ],
            out_specs=[
                pl.BlockSpec((1, GROUP * TOK, DK), lambda i, m: (i, 0, 0)),
                pl.BlockSpec((1, GROUP * TOK, DV), lambda i, m: (i, 0, 0)),
            ],
            scratch_shapes=[pltpu.VMEM((8 + TOK, 256), F32)],
        ),
        out_shape=[
            jax.ShapeDtypeStruct((4, GROUP * TOK, DK), BF16),
            jax.ShapeDtypeStruct((4, GROUP * TOK, DV), F32),
        ],
        compiler_params=params(),
        cost_estimate=pl.CostEstimate(
            flops=16 * 6 * 2 * 128**3, bytes_accessed=5 * 2**20, transcendentals=10**6
        ),
        name="reads",
    )(meta, projected, halo, conv_weight, tables, keys_t, ef, left)


def factor(tail, head):
    tail = tail.astype(F32)
    return (tail[head : head + 1] + tail[4 + head : 5 + head]) + tail[8 + head : 9 + head]


def compose(left, left_c, right, right_c):
    right_d = right[:, :DK]
    product = dot(right_d.astype(BF16), left.astype(BF16))
    return (
        right_c * left.astype(F32)
        + jnp.concatenate(
            [left_c[:, :DK] * right_d.astype(F32), right[:, DK:].astype(F32)], axis=1
        )
        - product
    )


def apply_map(each, c, state):
    product = dot(each[:, :DK], state)
    return c[:, :DK] * state.astype(F32) + each[:, DK:].astype(F32) - product


def pair_kernel(places, meta, mine_ref, other_ref, *out_refs):
    def combine(left_ref, right_ref):
        for m, out_ref in zip(places, out_refs):
            g = meta[3] ^ m
            left_tail = left_ref[g, GROUP * DK : ROWS, :]
            right_tail = right_ref[g, GROUP * DK : ROWS, :]
            factors = []
            for h in range(GROUP):
                here = slice(h * DK, (h + 1) * DK)
                left_c, right_c = factor(left_tail, h), factor(right_tail, h)
                both = compose(left_ref[g, here, :], left_c, right_ref[g, here, :], right_c)
                out_ref[here, :] = both.astype(BF16)
                factors.append(left_c * right_c)
            out_ref[GROUP * DK : ROWS, :] = split_rows(factors)

    pl.when(meta[2] == 0)(lambda: combine(mine_ref, other_ref))
    pl.when(meta[2] != 0)(lambda: combine(other_ref, mine_ref))


def pair_maps(meta, places, mine, other):
    return pl.pallas_call(
        functools.partial(pair_kernel, places),
        in_specs=[smem_spec(), whole_spec(), whole_spec()],
        out_specs=[whole_spec()] * len(places),
        out_shape=[jax.ShapeDtypeStruct((ROWS, 256), BF16)] * len(places),
        compiler_params=params(),
        cost_estimate=pl.CostEstimate(
            flops=len(places) * 4 * 2 * 2 * 128**3, bytes_accessed=2**21, transcendentals=0
        ),
        name="pair",
    )(meta, mine, other)


def by_place(meta, body):
    for place in range(4):
        pl.when(meta[3] == place)(functools.partial(body, place))


def plane_kernel(meta, x0, x1, x2, x3, prefix_ref, plane_ref, exit_ref):
    pieces = (x0, x1, x2, x3)
    prefix_ref[0] = jnp.zeros((ROWS, 256), BF16)

    def chain(place):
        maps = [pieces[place ^ a] for a in range(4)]
        prefix_ref[1] = maps[0][...]
        run = [maps[0][h * DK : (h + 1) * DK, :].astype(F32) for h in range(GROUP)]
        run_c = [factor(maps[0][GROUP * DK : ROWS, :], h) for h in range(GROUP)]
        for a in range(1, 4):
            tail = maps[a][GROUP * DK : ROWS, :]
            for h in range(GROUP):
                here = slice(h * DK, (h + 1) * DK)
                c = factor(tail, h)
                run[h] = compose(run[h], run_c[h], maps[a][here, :], c)
                run_c[h] = run_c[h] * c
                if a < 3:
                    prefix_ref[a + 1, here, :] = run[h].astype(BF16)
                else:
                    plane_ref[here, :] = run[h].astype(BF16)
                    exit_ref[here, :] = run[h][:, DK:].astype(BF16)
            if a < 3:
                prefix_ref[a + 1, GROUP * DK : ROWS, :] = split_rows(run_c)
        plane_ref[GROUP * DK : ROWS, :] = split_rows(run_c)

    by_place(meta, chain)


def plane_maps(meta, pieces):
    return pl.pallas_call(
        plane_kernel,
        in_specs=[smem_spec()] + [whole_spec()] * 4,
        out_specs=[whole_spec()] * 3,
        out_shape=[
            jax.ShapeDtypeStruct((4, ROWS, 256), BF16),
            jax.ShapeDtypeStruct((ROWS, 256), BF16),
            jax.ShapeDtypeStruct((GROUP * DK, DV), BF16),
        ],
        compiler_params=params(),
        cost_estimate=pl.CostEstimate(
            flops=12 * 2 * 2 * 128**3, bytes_accessed=2 * 2**20, transcendentals=0
        ),
        name="plane",
    )(meta, *pieces)


def hop_kernel(plane_ref, state_ref, out_ref):
    tail = plane_ref[GROUP * DK : ROWS, :]
    for h in range(GROUP):
        here = slice(h * DK, (h + 1) * DK)
        state = apply_map(plane_ref[here, :], factor(tail, h), state_ref[here, :])
        out_ref[here, :] = state.astype(BF16)


def hop(plane_map, state):
    return pl.pallas_call(
        hop_kernel,
        in_specs=[whole_spec()] * 2,
        out_specs=whole_spec(),
        out_shape=jax.ShapeDtypeStruct((GROUP * DK, DV), BF16),
        compiler_params=params(),
        cost_estimate=pl.CostEstimate(
            flops=4 * 2 * 128**3, bytes_accessed=2**19, transcendentals=0
        ),
        name="hop",
    )(plane_map, state)


def spread_kernel(meta, prefix_ref, before_ref, far_ref, *refs):
    out_refs = refs[-4:]
    state_refs = refs[:-4]
    before_tail = before_ref[GROUP * DK : ROWS, :]

    def send(place):
        for h in range(GROUP):
            here = slice(h * DK, (h + 1) * DK)
            state = apply_map(before_ref[here, :], factor(before_tail, h), far_ref[here, :])
            state = state.astype(BF16)
            for ref in state_refs:
                state = state + ref[here, :]
            out_refs[place][here, :] = state
            for a in range(1, 4):
                c = factor(prefix_ref[a, GROUP * DK : ROWS, :], h)
                after = apply_map(prefix_ref[a, here, :], c, state)
                out_refs[place ^ a][here, :] = after.astype(BF16)

    by_place(meta, send)


def spread(meta, prefix, before, far, states):
    return pl.pallas_call(
        spread_kernel,
        in_specs=[smem_spec()] + [whole_spec()] * (3 + len(states)),
        out_specs=[whole_spec()] * 4,
        out_shape=[jax.ShapeDtypeStruct((GROUP * DK, DV), BF16)] * 4,
        compiler_params=params(),
        cost_estimate=pl.CostEstimate(
            flops=20 * 2 * 128**3, bytes_accessed=2**21, transcendentals=0
        ),
        name="spread",
    )(meta, prefix, before, far, *states)


def entering_states(plane_map, leaving, planes):
    def ahead(block, plane, distance=1):
        members = range(8 * plane, 8 * plane + 8)
        return lax.ppermute(block, "seq", [(i, i + 8 * distance) for i in members])

    if planes == 4:
        first = ahead(leaving, 0)
        before = ahead(plane_map, 2)
        second = hop(plane_map, first)
        far = ahead(second, 1, 2)
        near = ahead(second, 1)
        return before, far, [first, near]
    states = []
    for plane in range(planes - 1):
        state = ahead(leaving, plane)
        states.append(state)
        if plane < planes - 2:
            leaving = hop(plane_map, state)
    return jnp.zeros_like(plane_map), jnp.zeros_like(leaving), states


def read_out(meta, r_ref, d_ref, e_refs, rows):
    for m, e_ref in enumerate(e_refs):
        g = meta[3] ^ m
        for h in range(GROUP):
            here = slice(h * TOK, (h + 1) * TOK)
            total = dot(r_ref[g, here, :], e_ref[here, :]) + d_ref[g, here, :]
            rows[g, :, h * DV : (h + 1) * DV] = total.astype(BF16)
        yield m, g


def half_kernel(meta, r_ref, d_ref, e0, e1, e2, e3, rows):
    for _ in read_out(meta, r_ref, d_ref, (e0, e1, e2, e3), rows):
        pass


def read_half(meta, reads, direct, states):
    return pl.pallas_call(
        half_kernel,
        in_specs=[smem_spec()] + [whole_spec()] * 6,
        out_specs=whole_spec(),
        out_shape=jax.ShapeDtypeStruct((4, TOK, GROUP * DV), BF16),
        compiler_params=params(),
        cost_estimate=pl.CostEstimate(
            flops=16 * 2 * 128**3, bytes_accessed=3 * 2**20, transcendentals=0
        ),
        name="half",
    )(meta, reads, direct, *states)


def emit_kernel(meta, kept, r_ref, d_ref, e0, e1, e2, e3, out_ref, rows, sems):
    copies = []

    def put(source, n, slot, g):
        start = pl.multiple_of((meta[slot] + g) * (GROUP * DV), GROUP * DV)
        copy = pltpu.make_async_copy(
            source.at[g], out_ref.at[:, pl.ds(start, GROUP * DV)], sems.at[n]
        )
        copy.start()
        copies.append(copy)

    for g in range(4):
        put(kept, g, 1, g)
    for m, g in read_out(meta, r_ref, d_ref, (e0, e1, e2, e3), rows):
        put(rows, 4 + m, 0, g)
    for copy in copies:
        copy.wait()


def emit(meta, kept, reads, direct, states):
    return pl.pallas_call(
        emit_kernel,
        in_specs=[smem_spec()] + [whole_spec()] * 7,
        out_specs=pl.BlockSpec(memory_space=pl.ANY),
        out_shape=jax.ShapeDtypeStruct((TOK, HV * DV), BF16),
        scratch_shapes=[
            pltpu.VMEM((4, TOK, GROUP * DV), BF16),
            pltpu.SemaphoreType.DMA((8,)),
        ],
        compiler_params=params(),
        cost_estimate=pl.CostEstimate(
            flops=16 * 2 * 128**3, bytes_accessed=3 * 2**20, transcendentals=0
        ),
        name="emit",
    )(meta, kept, reads, direct, *states)


def shards(projected, conv_weight, decay_log, write_strength, starts):
    count = lax.axis_size("seq")
    me = lax.axis_index("seq")
    core, place = me & 1, (me >> 1) & 3
    slots = lax.iota(jnp.int32, 8)
    meta = jnp.zeros((8,), jnp.int32)
    for slot, value in enumerate((4 * (1 - core), 4 * core, core, place, me >> 3)):
        meta = jnp.where(slots == slot, value, meta)

    def exchange(block, bits):
        return lax.ppermute(block, "seq", [(i, i ^ bits) for i in range(count)])

    starts = starts.reshape(1, TOK)
    tail_rows = tail_of(starts, projected)
    halo = lax.ppermute(tail_rows, "seq", [(i, i + 1) for i in range(count - 1)])
    projected, conv_weight, tables, masks, shared = stage(
        decay_log, write_strength, starts, projected, conv_weight
    )
    ins = (projected, halo, conv_weight, tables, masks, shared)

    pay_s, kt_s, ef_s, *ready = send_maps(meta, *ins)
    other = exchange(pay_s, 1)
    mine, kt_k, ef_k = keep_maps(meta, *ins, *ready)
    x1, x2 = pair_maps(meta, (1, 2), mine, other)
    x1 = exchange(x1, 2)
    x2 = exchange(x2, 4)
    x0, x3 = pair_maps(meta, (0, 3), mine, other)
    x3 = exchange(x3, 6)
    x0, own = lax.optimization_barrier((x0, mine))
    left = exchange(own, 1)
    r_k, d_k = make_reads(meta, 1, projected, halo, conv_weight, tables, kt_k, ef_k, other)
    r_s, d_s = make_reads(meta, 0, projected, halo, conv_weight, tables, kt_s, ef_s, left)
    x0, r_k, d_k, r_s, d_s = lax.optimization_barrier((x0, r_k, d_k, r_s, d_s))
    prefix, plane_map, leaving = plane_maps(meta, (x0, x1, x2, x3))
    before, far, arrived = entering_states(plane_map, leaving, count // 8)
    e0, e1, e2, e3 = spread(meta, prefix, before, far, arrived)
    e3, e1, e2 = exchange(e3, 6), exchange(e1, 2), exchange(e2, 4)
    states = (e0, e1, e2, e3)
    partner = [exchange(e, 1) for e in states]
    kept = read_half(meta, r_k, d_k, states)
    return emit(meta, kept, r_s, d_s, partner)


def solution(mesh):
    in_specs = (
        P(("groups", "seq"), None),
        P(),
        P(None, ("groups", "seq")),
        P(None, ("groups", "seq")),
        P(("groups", "seq")),
    )
    out_specs = P(("groups", "seq"), None)

    return jax.shard_map(shards, mesh=mesh, in_specs=in_specs, out_specs=out_specs, check_vma=False)
```
